128 devices in a mesh: gx: 4 (over x_hi, core), gy: 4 (over y), gz: 8 (over x_lo, z).
Axes of the slice: x: 4 (x_hi: 2, x_lo: 2; x = x_hi * 2 + x_lo), y: 4, z: 4, core: 2. Of those that a mesh axis runs over, the one named last changes fastest.
Arguments:
- state: float32 [7, 16, 16, 128, 128], P(None, 'gx', 'gy', 'gz'), may hold values from -6 to 6, as said below
- arms: float32 [3, 16, 16, 128, 128], P(None, 'gx', 'gy', 'gz'), may hold values from -6 to 6
- sphere_frag: int32 [16, 16, 128, 128], P('gx', 'gy', 'gz'), may hold values from 0 to 63
- frag_owner: int32 [8192, 1], P(('gx', 'gy', 'gz')), may hold values from 0 to 127; in each aligned block of 64 rows (0 to 63, 64 to 127, ...) at most 2 rows name the same one
- frag_clump: int32 [8192], P(('gx', 'gy', 'gz')), may hold values from 0 to 47
- tiles: int32 [128, 2048], P(('gx', 'gy', 'gz')), may hold values from 0 to 6911, as said below
- clump_motion: float32 [6, 6144], P(None, ('gx', 'gy', 'gz')), may hold values from -6 to 6
- inv_mass: float32 [6144], P(('gx', 'gy', 'gz')), may hold values from 0.3 to 3
- inv_moment: float32 [6144], P(('gx', 'gy', 'gz')), may hold values from 0.1 to 1
Outputs:
- sphere_next: float32 [6, 16, 16, 128, 128], P(None, 'gx', 'gy', 'gz')
- clump_next: float32 [6, 6144], P(None, ('gx', 'gy', 'gz'))
The draws below stay inside these ranges and needn't reach their ends.
Inputs may be any that keep to these rules, and one draw needn't show every extreme that they name: `state`: rows 0 to 2 lie in [0, 1), rows 3 to 5 in [-6, 6], row 6 in [0.08, 0.14]. `tiles`: the 2048 codes of one brick are distinct. `frag_owner`: among the 64 fragments of one brick at most 2 name the same owner.
All inputs are finite; a program needn't handle non-finite values.
Results may differ from the reference program's by a relative error of at most 0.0003.
Values sent between devices are 32-bit elements; how exact they have to be, the bound alone decides.
A program may use at most 64 MiB of HBM per device.

```python
import math
import jax
import jax.numpy as jnp
import numpy as np
from jax import lax

SLOT = 128
CX = 4
CY = 4
CZ = 16
HELD = 64
OWN = 48
CAP = 2
BRICKS = 128
TILES_DEV = 2048
CLUMPS = 6144
NX = 16
NY = 16
NZ = 128
N_GX = 4
N_GY = 4
N_GZ = 8


def sphere_world(key):
    base = jax.random.fold_in(key, 23)
    keys = jax.random.split(base, 5)
    grid = (NX, NY, NZ, SLOT)
    position = jax.random.uniform(keys[0], (3,) + grid, jnp.float32, 0.0, 0.999)
    velocity = jnp.clip(jax.random.normal(keys[1], (3,) + grid, jnp.float32), -6.0, 6.0)
    radius = jax.random.uniform(keys[2], (1,) + grid, jnp.float32, 0.08, 0.14)
    state = jnp.concatenate([position, velocity, radius], axis=0)
    index_x = lax.broadcasted_iota(jnp.int32, grid, 0)
    index_y = lax.broadcasted_iota(jnp.int32, grid, 1)
    index_z = lax.broadcasted_iota(jnp.int32, grid, 2)
    slot_index = lax.broadcasted_iota(jnp.int32, grid, 3)
    local_x = index_x % CX
    local_y = index_y % CY
    local_z = index_z % CZ
    spheres = CX * CY * CZ * SLOT
    linear = ((local_x * CY + local_y) * CZ + local_z) * SLOT + slot_index
    home = linear * HELD // spheres
    side = jax.random.randint(keys[3], grid, 0, 2) * 2 - 1
    stray = jax.random.randint(keys[4], grid, 0, 4) == 0
    target_z = local_z + side
    inside = (target_z >= 0) & (target_z < CZ)
    other = (linear + side * SLOT) * HELD // spheres
    edge = (slot_index == 0) | (slot_index == SLOT - 1)
    frag = jnp.where(stray & inside & jnp.logical_not(edge), other, home).astype(jnp.int32)
    brick = (index_x // CX * N_GY + index_y // CY) * N_GZ + index_z // CZ
    global_frag = (brick * HELD + frag).reshape(-1)
    place = jnp.stack([index_x.astype(jnp.float32) + position[0], index_y.astype(jnp.float32) + position[1], index_z.astype(jnp.float32) + position[2]])
    flat = place.reshape(3, -1).T
    segments = N_GX * N_GY * N_GZ * HELD
    total = jax.ops.segment_sum(flat, global_frag, num_segments=segments)
    count = jax.ops.segment_sum(jnp.ones((flat.shape[0],), jnp.float32), global_frag, num_segments=segments)
    centre = total / jnp.maximum(count, 1.0)[:, None]
    arms = place - jnp.take(centre, global_frag, axis=0).T.reshape((3,) + grid)
    return (state, frag, arms)


def draw_state(key, part):
    return sphere_world(key)[0]


def draw_sphere_frag(key, part):
    return sphere_world(key)[1]


def draw_arms(key, part):
    return sphere_world(key)[2]


def draw_tiles(key, part):
    base = jax.random.fold_in(key, 7)
    brick_keys = jax.random.split(base, N_GX * N_GY * N_GZ)

    def one_brick(brick_key):
        return jax.random.permutation(brick_key, 27 * CX * CY * CZ)[:TILES_DEV]
    return jax.vmap(one_brick)(brick_keys).astype(jnp.int32)


def with_ends(values, stream_key, least, top_value):
    shape = values.shape
    spot = [jax.random.randint(jax.random.fold_in(stream_key, axis), (), 0, shape[axis]) for axis in range(len(shape))]
    values = values.at[tuple(spot)].set(least)
    longest = shape.index(max(shape))
    spot[longest] = (spot[longest] + 1) % shape[longest]
    return values.at[tuple(spot)].set(top_value)


def level_of(own_key, shape, cuts, smallest, high):
    def one(axis_at, shards_of):
        draws = jax.random.uniform(jax.random.fold_in(jax.random.fold_in(own_key, 6), axis_at), (shards_of,), jnp.float32, smallest / len(cuts), high / len(cuts))
        return jnp.repeat(jnp.exp(draws), shape[axis_at] // shards_of).reshape((-1,) + (1,) * (len(shape) - axis_at - 1))

    level = one(*cuts[0])
    for cut in cuts[1:]:
        level = level * one(*cut)
    return level


def routed_block(own_key, own, number, rows, number_of, top, reach, lean):
    ranking = jax.random.permutation(own_key, number_of)
    crowded, ordinary = portions_of(number_of, rows * top, reach, lean, True), portions_of(number_of, rows * top, reach, lean, False)
    places = jnp.arange(number_of)

    def named(tallies, offset_by):
        used = int((tallies > 0).sum())
        fixed = max(1, used // 4)
        moved = fixed + (places - fixed + offset_by * (used - fixed)) % max(1, number_of - fixed)
        return jnp.zeros((number_of,), jnp.int32).at[ranking[jnp.where(places < fixed, places, moved)]].set(jnp.asarray(tallies, jnp.int32))

    tallies = jnp.where(number % 4 == 0, named(crowded, number // 4), named(ordinary, number - number // 4 - 1))
    mixed = jax.random.permutation(jax.random.fold_in(own, 3), number_of)
    donor, sink = mixed[0:number_of // 2 * 2:2], mixed[1:number_of // 2 * 2:2]
    room = jnp.minimum(tallies[donor] - 1, reach - tallies[sink]) // 2
    room = jnp.where((donor == ranking[0]) | (sink == ranking[0]) | (tallies[sink] == 0), 0, jnp.maximum(room, 0))
    moved = jax.random.randint(jax.random.fold_in(own, 4), (number_of // 2,), 0, 1 << 20) % (room + 1)
    tallies = tallies.at[donor].add(-moved).at[sink].add(moved)
    members = jnp.searchsorted(jnp.cumsum(tallies), jnp.arange(rows * top), side="right").astype(jnp.int32)
    table = members.reshape(top, rows).T
    table = table[jax.random.permutation(jax.random.fold_in(own, 1), rows)]
    offset_by = jax.random.randint(jax.random.fold_in(own, 2), (rows, 1), 0, top)
    return jnp.take_along_axis(table, (jnp.arange(top)[None, :] + offset_by) % top, axis=1)


def portions_of(number_of, total, most, slope, full):
    weights = [(1 << 20) // math.isqrt(rank ** slope) + 1 for rank in range(1, number_of + 1)]
    largest = most if full else min(most, max(-(-total // number_of), total * weights[0] // sum(weights)))
    least = 1 if total - largest >= number_of - 1 else 0
    counts, spare = [largest] + [least] * (number_of - 1), total - largest - least * (number_of - 1)
    while spare > 0:
        candidates = [i for i in range(1, number_of) if counts[i] < largest] or [i for i in range(1, number_of) if counts[i] < most]
        pool, budget = sum([weights[i] for i in candidates]), spare
        for i in candidates:
            addition = min(most - counts[i], max(1, budget * weights[i] // pool), spare)
            counts[i] = counts[i] + addition
            spare = spare - addition
    return np.array(counts)


def gaussian(key, extent, spread, bound, cuts=(), kind=jnp.bfloat16):
    result = jax.random.normal(key, extent, jnp.float32) * spread
    if len(cuts) > 0:
        result = level_of(key, extent, cuts, -0.22, 0.18) * result
    return jnp.clip(result, min=-bound, max=bound).astype(kind)


def setup_inputs(seed: int = 0) -> dict:
    splits = jax.random.split(jax.random.key(seed), 10)
    state = draw_state(jax.random.fold_in(splits[9], 71), 0)
    arms = draw_arms(jax.random.fold_in(splits[9], 71), 0)
    sphere_frag = draw_sphere_frag(jax.random.fold_in(splits[9], 71), 0)
    frag_owner_keys = jax.random.split(jax.random.fold_in(splits[3], 1), (BRICKS * HELD) // HELD)
    frag_owner_turns = jax.random.permutation(jax.random.fold_in(splits[3], 3), (BRICKS * HELD) // HELD)
    frag_owner = jax.vmap(lambda own, number: routed_block(jax.random.fold_in(splits[3], 2), own, number, HELD, BRICKS, 1, CAP, 2))(frag_owner_keys, frag_owner_turns).reshape((BRICKS * HELD, 1))
    frag_clump = with_ends(jax.random.randint(splits[4], (BRICKS * HELD,), 0, OWN), jax.random.fold_in(splits[4], 1), 0, OWN - 1).astype(jnp.int32)
    tiles = draw_tiles(jax.random.fold_in(splits[9], 71), 0)
    clump_motion = gaussian(splits[6], (6, CLUMPS), 1.0, 6.0, ((1, 128),), jnp.float32)
    inv_mass = jnp.clip(jnp.exp(math.log(3.0) - 2.3025851 * jax.random.uniform(splits[7], (CLUMPS,), jnp.float32) ** level_of(splits[7], (CLUMPS,), ((0, 128),), -0.2, 0.2)), 0.3, 3.0)
    inv_moment = jnp.clip(jnp.exp(math.log(1.0) - 2.3025851 * jax.random.uniform(splits[8], (CLUMPS,), jnp.float32) ** level_of(splits[8], (CLUMPS,), ((0, 128),), -0.2, 0.2)), 0.1, 1.0)
    return {"state": state, "arms": arms, "sphere_frag": sphere_frag, "frag_owner": frag_owner, "frag_clump": frag_clump, "tiles": tiles, "clump_motion": clump_motion, "inv_mass": inv_mass, "inv_moment": inv_moment}


stiffness = 100.0
damping = 2.0
time_step = 0.01
gravity = 9.81
epsilon_sq = 1e-08

def cross_rows(first, second):
    return jnp.stack([first[1] * second[2] - first[2] * second[1], first[2] * second[0] - first[0] * second[2], first[0] * second[1] - first[1] * second[0]])

def pair_forces(own_block, neighbor_block, cell_shift):
    separation = [neighbor_block[axis_k][:, None, :] + cell_shift[axis_k][:, None, None] - own_block[axis_k][:, :, None] for axis_k in range(3)]
    distance = jnp.sqrt(separation[0] * separation[0] + separation[1] * separation[1] + separation[2] * separation[2] + epsilon_sq)
    radius_own = own_block[6][:, :, None]
    radius_other = neighbor_block[6][:, None, :]
    distinct = (own_block[7][:, :, None] != neighbor_block[7][:, None, :]).astype(jnp.float32)
    intersection = jnp.maximum(radius_own + radius_other - distance, 0.0) * distinct
    reduced = radius_own * radius_other / (radius_own + radius_other)
    closing = sum(((neighbor_block[3 + axis_k][:, None, :] - own_block[3 + axis_k][:, :, None]) * separation[axis_k] for axis_k in range(3))) / distance
    magnitude = stiffness * jnp.sqrt(reduced) * intersection * jnp.sqrt(intersection) - damping * jnp.sqrt(reduced * intersection) * closing
    factor = magnitude / distance
    return jnp.stack([-lax.optimization_barrier(jnp.sum(factor * separation[axis_k], axis=2)) for axis_k in range(3)])

def decode_tiles(codes, cells_y, cells_z):
    own_cell = codes // 27
    offset = codes % 27
    step_x = offset // 9 - 1
    step_y = offset // 3 % 3 - 1
    step_z = offset % 3 - 1
    cell_x = own_cell // (cells_y * cells_z)
    cell_y = own_cell // cells_z % cells_y
    cell_z = own_cell % cells_z
    return (own_cell, cell_x, cell_y, cell_z, step_x, step_y, step_z)

def advance(motion, sums, inv_mass, inv_moment):
    pull = jnp.array([0.0, 0.0, gravity], jnp.float32)[:, None]
    velocity = motion[0:3] + time_step * (sums[0:3] * inv_mass[None, :] - pull)
    spin = motion[3:6] + time_step * sums[3:6] * inv_moment[None, :]
    return jnp.concatenate([velocity, spin], axis=0)

def move_spheres(state, arms, motion):
    velocity = motion[0:3]
    spin = motion[3:6]
    half = 0.5 * time_step * spin
    turned = cross_rows(half, arms)
    twice = cross_rows(half, turned)
    scale = 2.0 / (1.0 + half[0] * half[0] + half[1] * half[1] + half[2] * half[2])
    new_arm = arms + scale * (turned + twice)
    position = state[0:3] + time_step * velocity + (new_arm - arms)
    moving = velocity + cross_rows(spin, new_arm)
    return jnp.concatenate([position, moving], axis=0)

def to_bricks(values):
    comps = values.shape[0]
    shaped = values.reshape(comps, N_GX, CX, N_GY, CY, N_GZ, CZ, SLOT)
    shaped = shaped.transpose(1, 3, 5, 0, 2, 4, 6, 7)
    return shaped.reshape(N_GX * N_GY * N_GZ, comps, CX * CY * CZ, SLOT)

def reference(state, arms, sphere_frag, frag_owner, frag_clump, tiles, clump_motion, inv_mass, inv_moment):
    bricks = N_GX * N_GY * N_GZ
    owner = frag_owner[:, 0]
    grid = (NX, NY, NZ, SLOT)
    index_x = lax.broadcasted_iota(jnp.int32, grid, 0)
    index_y = lax.broadcasted_iota(jnp.int32, grid, 1)
    index_z = lax.broadcasted_iota(jnp.int32, grid, 2)
    brick = (index_x // CX * N_GY + index_y // CY) * N_GZ + index_z // CZ
    frag_global = brick * HELD + sphere_frag
    sphere_clump = owner[frag_global] * OWN + frag_clump[frag_global]
    full = jnp.concatenate([state, sphere_clump.astype(jnp.float32)[None]], axis=0).reshape(8, NX * NY * NZ, SLOT)

    def brick_forces(index):
        codes = tiles[index]
        brick_x = index // (N_GY * N_GZ)
        brick_y = index // N_GZ % N_GY
        brick_z = index % N_GZ
        own_cell, cell_x, cell_y, cell_z, step_x, step_y, step_z = decode_tiles(codes, CY, CZ)
        global_x = brick_x * CX + cell_x
        global_y = brick_y * CY + cell_y
        global_z = brick_z * CZ + cell_z
        own_glob = ((global_x * NY + global_y) * NZ + global_z).astype(jnp.int32)
        other_x = (global_x + step_x) % NX
        other_y = (global_y + step_y) % NY
        other_z = (global_z + step_z) % NZ
        other_glob = ((other_x * NY + other_y) * NZ + other_z).astype(jnp.int32)
        cell_shift = jnp.stack([step_x, step_y, step_z]).astype(jnp.float32)
        forces = pair_forces(jnp.take(full, own_glob, axis=1), jnp.take(full, other_glob, axis=1), cell_shift)
        return jnp.zeros((3, CX * CY * CZ, SLOT), jnp.float32).at[:, own_cell].add(forces)
    per_brick = lax.map(brick_forces, jnp.arange(bricks, dtype=jnp.int32))
    force = per_brick.transpose(1, 0, 2, 3)
    lever = to_bricks(arms).transpose(1, 0, 2, 3)
    torque = cross_rows(lever, force)
    loads = jnp.concatenate([force, torque], axis=0).reshape(6, -1)
    frag_blocks = to_bricks(sphere_frag[None])[:, 0]
    frag_index = (frag_blocks + (jnp.arange(bricks, dtype=jnp.int32) * HELD)[:, None, None]).reshape(-1)
    frag_sums = jax.ops.segment_sum(loads.T, frag_index, num_segments=bricks * HELD)
    clump_index = owner * OWN + frag_clump
    clump_sums = jax.ops.segment_sum(frag_sums, clump_index, num_segments=OWN * bricks).T
    clump_next = advance(clump_motion, clump_sums, inv_mass, inv_moment)
    sphere_motion = jnp.take(clump_next, sphere_clump, axis=1)
    return (move_spheres(state, arms, sphere_motion), clump_next)
```

```python
import functools

import jax
import jax.numpy as jnp
from jax import lax
from jax.experimental import pallas as pl
from jax.experimental.pallas import tpu as pltpu
from jax.sharding import PartitionSpec as P

CAP = 2
REACH = 0.14001
time_step = 0.01
gravity = 9.81
epsilon_sq = 1e-08
UNROLL = 8
VMEM = pl.BlockSpec(memory_space=pltpu.VMEM)
SMEM = pl.BlockSpec(memory_space=pltpu.SMEM)


def lane_take(rows, index):
    return jnp.take_along_axis(rows, index, axis=1, mode="promise_in_bounds")


def cross_rows(first, second):
    return [
        first[1] * second[2] - first[2] * second[1],
        first[2] * second[0] - first[0] * second[2],
        first[0] * second[1] - first[1] * second[0],
    ]


def pack_kernel(state, frag, table, out):
    keys = jnp.broadcast_to(table[...], (8, 128))
    for g in range(frag.shape[0] // 8):
        rows = pl.ds(8 * g, 8)
        for k in range(7):
            out[pl.ds(64 * g + k, 8, stride=8), :] = state[k, rows, :]
        out[pl.ds(64 * g + 7, 8, stride=8), :] = lane_take(keys, frag[rows, :])


def tile_parts(code, ny, nz):
    own = (code * 38837) >> 20
    offset = code - 27 * own
    step_x = ((offset * 57) >> 9) - 1
    left = offset - 9 * (step_x + 1)
    step_y = ((left * 11) >> 5) - 1
    step_z = left - 3 * (step_y + 1) - 1
    cell = ((own >> 6) + 1 + step_x) * (ny * nz) + (((own >> 4) & 3) + 1 + step_y) * nz + (own & 15) + 1 + step_z
    return own, offset, cell


def tiles_kernel(
    codes, cells, arms, frag, out, cand, mask, perm, counts, counts_s, lens, lists, shifts, cols, loads, sem
):
    tiles = codes.shape[0]
    pad = cells.shape[0] // 8
    ny, nz = 6, 18
    chunks = lists.shape[1]
    sub = lax.broadcasted_iota(jnp.int32, (8, 128), 0)
    lane = lax.broadcasted_iota(jnp.int32, (8, 128), 1)

    @pl.loop(0, pad // 8)
    def _(g):
        base = pl.multiple_of(g * 64, 64)
        pos = [cells[pl.ds(base + k, 8, stride=8), :] for k in range(3)]
        reach = cells[pl.ds(base + 6, 8, stride=8), :] + REACH
        reach = reach * reach
        near = [p * p for p in pos]
        far = [(1.0 - p) * (1.0 - p) for p in pos]
        bits = jnp.full((8, 128), 1 << 13, jnp.int32)
        for o in range(27):
            steps = (o // 9 - 1, o // 3 % 3 - 1, o % 3 - 1)
            terms = [near[k] if s > 0 else far[k] for k, s in enumerate(steps) if s]
            if not terms:
                continue
            bits = bits | jnp.where(sum(terms[1:], terms[0]) <= reach, 1 << o, 0)
        cand[pl.ds(pl.multiple_of(g * 8, 8), 8), :] = bits

    @pl.loop(0, 27)
    def _(o):
        step_x = ((o * 57) >> 9) - 1
        left = o - 9 * (step_x + 1)
        step_y = ((left * 11) >> 5) - 1
        step_z = left - 3 * (step_y + 1) - 1
        value = jnp.where(sub == 0, step_x, jnp.where(sub == 1, step_y, jnp.where(sub == 2, step_z, 0)))
        shifts[o] = value.astype(jnp.float32)

    @pl.loop(0, 256)
    def _(c):
        lens[c] = 0

    @pl.loop(0, tiles // 16)
    def _(b):
        for u in range(16):
            t = b * 16 + u
            own, offset, cell = tile_parts(codes[t], ny, nz)
            mask[pl.ds(t, 1), :] = (cand[pl.ds(cell, 1), :] >> offset) & 1

    row = lax.broadcasted_iota(jnp.int32, (128, 128), 0)
    col = lax.broadcasted_iota(jnp.int32, (128, 128), 1)
    before = (row < col).astype(jnp.bfloat16)
    ones = jnp.ones((8, 128), jnp.bfloat16)

    @pl.loop(0, tiles // 128)
    def _(b):
        rows = pl.ds(pl.multiple_of(b * 128, 128), 128)
        active = mask[rows, :]
        flags = active.astype(jnp.float32).astype(jnp.bfloat16)
        rank = jnp.dot(flags, before, preferred_element_type=jnp.float32).astype(jnp.int32)
        number = lax.dot_general(ones, flags, (((1,), (1,)), ((), ())), preferred_element_type=jnp.float32)
        counts[pl.ds(b, 1), :] = number[0:1].astype(jnp.int32)
        value = jnp.where(active > 0, ((col - rank) << 7) | col, 0)
        for bit in range(7):
            moved = pltpu.roll(value, 128 - (1 << bit), axis=1)
            flag = 1 << (7 + bit)
            value = jnp.where((moved & flag) != 0, moved, jnp.where((value & flag) != 0, 0, value))
        perm[rows, :] = value & 127

    copy = pltpu.make_async_copy(counts, counts_s, sem)
    copy.start()
    copy.wait()

    def append(own, sorted_rows, number):
        at = lens[own]
        lens[own] = at + number
        chunk = at >> 7
        turn = at & 127
        turned = pltpu.roll(sorted_rows, turn, axis=1)
        lists[own, chunk] = jnp.where(lane >= turn, turned, lists[own, chunk])
        lists[own, chunk + 1] = turned

    @pl.loop(0, tiles // 8)
    def _(b):
        for u in range(8):
            t = b * 8 + u
            own, offset, cell = tile_parts(codes[t], ny, nz)
            values = cells[pl.ds(pl.multiple_of(cell * 8, 8), 8), :]
            index = jnp.broadcast_to(perm[pl.ds(t, 1), :], (8, 128))
            append(own, lane_take(values, index) + shifts[offset], counts_s[t >> 7, t & 127])

    dummy = jnp.where(sub < 3, 1000.0, 0.1)

    @pl.loop(0, 32)
    def _(b):
        for u in range(8):
            append(b * 8 + u, dummy, 0)

    @pl.loop(0, 16)
    def _(g):
        most = lax.fori_loop(0, 16, lambda k, m: jnp.maximum(m, lens[g * 16 + k]), 0)

        @pl.loop(0, (most + 127) // 128)
        def _(m):
            block = lists[pl.ds(g * 16, 16), m].reshape(128, 128)
            cols[pl.ds(pl.multiple_of(m * 128, 128), 128), :] = block.T

        first = ((g >> 2) + 1) * (ny * nz) + ((g & 3) + 1) * nz + 1

        @pl.loop(0, 16)
        def _(cc):
            cell = g * 16 + cc
            mine = cells[pl.ds(pl.multiple_of((first + cc) * 8, 8), 8), :]
            own = [jnp.broadcast_to(mine[k : k + 1], (8, 128)) for k in range(8)]
            turn = (128 - 8 * cc) & 127

            def step(it, total):
                for u in range(UNROLL):
                    at = pl.multiple_of(it * (8 * UNROLL) + 8 * u, 8)
                    data = pltpu.roll(cols[pl.ds(at, 8), :], turn, axis=1)
                    other = [jnp.broadcast_to(data[:, k : k + 1], (8, 128)) for k in range(8)]
                    apart = [other[k] - own[k] for k in range(3)]
                    square = apart[0] * apart[0] + apart[1] * apart[1] + apart[2] * apart[2] + epsilon_sq
                    inverse = lax.rsqrt(square)
                    reach = own[6] + other[6]
                    depth = jnp.where(own[7] != other[7], jnp.maximum(reach - square * inverse, 0.0), 0.0)
                    closing = (
                        (other[3] - own[3]) * apart[0]
                        + (other[4] - own[4]) * apart[1]
                        + (other[5] - own[5]) * apart[2]
                    )
                    along = closing * inverse - 50.0 * depth
                    area = own[6] * other[6] * depth
                    factor = area * lax.rsqrt(jnp.maximum(area * reach, 1e-20)) * along * inverse
                    total = tuple(total[k] + factor * apart[k] for k in range(3))
                return total

            zero = jnp.zeros((8, 128), jnp.float32)
            count = (lens[cell] + (8 * UNROLL - 1)) // (8 * UNROLL)
            total = lax.fori_loop(0, count, step, (zero, zero, zero))
            force = [2.0 * jnp.sum(t, axis=0, keepdims=True) for t in total]
            lever = [arms[k, pl.ds(cell, 1), :] for k in range(3)]
            turn_rows = cross_rows(lever, force)
            at = pl.multiple_of(cell * 128, 128)
            for k in range(3):
                loads[pl.ds(k, 1), pl.ds(at, 128)] = force[k]
                loads[pl.ds(3 + k, 1), pl.ds(at, 128)] = turn_rows[k]
            loads[pl.ds(6, 1), pl.ds(at, 128)] = frag[pl.ds(cell, 1), :].astype(jnp.float32)
            loads[pl.ds(7, 1), pl.ds(at, 128)] = jnp.zeros((1, 128), jnp.float32)

    span = 1024
    ids = lax.broadcasted_iota(jnp.int32, (128, span), 0).astype(jnp.float32)

    def gather(b, total):
        at = pl.ds(pl.multiple_of(b * span, span), span)
        which = (ids == loads[6:7, at]).astype(jnp.float32)
        return total + lax.dot_general(
            loads[:, at], which, (((1,), (1,)), ((), ())), precision=lax.Precision.HIGHEST,
            preferred_element_type=jnp.float32,
        )

    out[...] = lax.fori_loop(0, loads.shape[1] // span, gather, jnp.zeros((8, 128), jnp.float32))


def move_kernel(state, arms, frag, table, out):
    rows_of = [jnp.broadcast_to(table[k : k + 1, :], (8, 128)) for k in range(6)]
    for g in range(frag.shape[0] // 8):
        rows = pl.ds(8 * g, 8)
        index = frag[rows, :]
        motion = [lane_take(r, index) for r in rows_of]
        velocity, spin = motion[0:3], motion[3:6]
        lever = [arms[k, rows, :] for k in range(3)]
        half = [0.5 * time_step * w for w in spin]
        turned = cross_rows(half, lever)
        twice = cross_rows(half, turned)
        scale = 2.0 / (1.0 + half[0] * half[0] + half[1] * half[1] + half[2] * half[2])
        moved = [lever[k] + scale * (turned[k] + twice[k]) for k in range(3)]
        swing = cross_rows(spin, moved)
        for k in range(3):
            out[k, rows, :] = state[k, rows, :] + time_step * velocity[k] + (moved[k] - lever[k])
            out[3 + k, rows, :] = velocity[k] + swing[k]


def pack(state, frag, table):
    n = frag.shape[0]
    part = n // 4
    return pl.pallas_call(
        pack_kernel,
        grid=(4,),
        in_specs=[
            pl.BlockSpec((7, part, 128), lambda i: (0, i, 0)),
            pl.BlockSpec((part, 128), lambda i: (i, 0)),
            pl.BlockSpec((1, 128), lambda i: (0, 0)),
        ],
        out_specs=pl.BlockSpec((8 * part, 128), lambda i: (i, 0)),
        out_shape=jax.ShapeDtypeStruct((8 * n, 128), jnp.float32),
        name="pack",
    )(state, frag, table)


def forces(codes, cells, arms, frag):
    tiles = codes.shape[0]
    return pl.pallas_call(
        tiles_kernel,
        in_specs=[SMEM, VMEM, VMEM, VMEM],
        out_specs=VMEM,
        out_shape=jax.ShapeDtypeStruct((8, 128), jnp.float32),
        scratch_shapes=[
            pltpu.VMEM((cells.shape[0] // 8, 128), jnp.int32),
            pltpu.VMEM((tiles, 128), jnp.int32),
            pltpu.VMEM((tiles, 128), jnp.int32),
            pltpu.VMEM((tiles // 128, 128), jnp.int32),
            pltpu.SMEM((tiles // 128, 128), jnp.int32),
            pltpu.SMEM((256,), jnp.int32),
            pltpu.VMEM((256, 29, 8, 128), jnp.float32),
            pltpu.VMEM((27, 8, 128), jnp.float32),
            pltpu.VMEM((29 * 128, 128), jnp.float32),
            pltpu.VMEM((8, 256 * 128), jnp.float32),
            pltpu.SemaphoreType.DMA,
        ],
        compiler_params=pltpu.CompilerParams(vmem_limit_bytes=60 * 1024 * 1024),
        name="forces",
    )(codes, cells, arms, frag)


def move(state, arms, frag, table):
    n = frag.shape[0]
    part = n // 4
    return pl.pallas_call(
        move_kernel,
        grid=(4,),
        in_specs=[
            pl.BlockSpec((3, part, 128), lambda i: (0, i, 0)),
            pl.BlockSpec((3, part, 128), lambda i: (0, i, 0)),
            pl.BlockSpec((part, 128), lambda i: (i, 0)),
            pl.BlockSpec((8, 128), lambda i: (0, 0)),
        ],
        out_specs=pl.BlockSpec((6, part, 128), lambda i: (0, i, 0)),
        out_shape=jax.ShapeDtypeStruct((6, n, 128), jnp.float32),
        name="move",
    )(state, arms, frag, table)


def with_halo(x, sides):
    for axis, dim in sides:
        devices, length = (lax.axis_size(axis), x.shape[dim])
        up = [(i, (i + 1) % devices) for i in range(devices)]
        down = [(j, i) for i, j in up]
        last = lax.slice_in_dim(x, length - 1, length, axis=dim)
        initial = lax.slice_in_dim(x, 0, 1, axis=dim)
        before = lax.ppermute(last, axis, up)
        after = lax.ppermute(initial, axis, down)
        x = jnp.concatenate([before, x, after], axis=dim)
    return x


def advance(motion, sums, inv_mass, inv_moment):
    pull = jnp.array([0.0, 0.0, gravity], jnp.float32)[:, None]
    velocity = motion[0:3] + time_step * (sums[0:3] * inv_mass[None, :] - pull)
    spin = motion[3:6] + time_step * sums[3:6] * inv_moment[None, :]
    return jnp.concatenate([velocity, spin], axis=0)


def local(state, arms, sphere_frag, frag_owner, frag_clump, tiles, clump_motion, inv_mass, inv_moment):
    cx, cy, cz, slots = state.shape[1:]
    count = cx * cy * cz
    owned = inv_mass.shape[0]
    held = frag_clump.shape[0]
    bricks = lax.axis_size("gx") * lax.axis_size("gy") * lax.axis_size("gz")
    owner = frag_owner[:, 0]
    frag = sphere_frag.reshape(count, slots)
    key = (owner * owned + frag_clump).astype(jnp.float32)
    own_cells = pack(state.reshape(7, count, slots), frag, jnp.pad(key, (0, 128 - held))[None])
    padded = with_halo(own_cells.reshape(cx, cy, cz, 8, slots), (("gx", 0), ("gy", 1), ("gz", 2)))
    frag_sums = forces(tiles[0], padded.reshape(-1, slots), arms.reshape(3, count, slots), frag)[0:6, 0:held]

    hits = (owner[:, None] == jnp.arange(bricks, dtype=jnp.int32)[None, :]).astype(jnp.int32)
    rank = jnp.sum((jnp.cumsum(hits, axis=0) - hits) * hits, axis=1)
    slot_index = owner * CAP + rank
    payload = jnp.concatenate([frag_sums, (frag_clump + 1).astype(jnp.float32)[None]], axis=0)
    outbox = jnp.zeros((7, bricks * CAP), jnp.float32).at[:, slot_index].set(payload)
    inbox = lax.all_to_all(outbox, ("gx", "gy", "gz"), split_axis=1, concat_axis=1, tiled=True)
    labels = (jnp.arange(owned, dtype=jnp.int32) + 1).astype(jnp.float32)
    which = (inbox[6][:, None] == labels[None, :]).astype(jnp.float32)
    clump_sums = jnp.dot(
        inbox[0:6], which, precision=lax.Precision.HIGHEST, preferred_element_type=jnp.float32
    )
    clump_next = advance(clump_motion, clump_sums, inv_mass, inv_moment)
    column = jnp.clip(inbox[6].astype(jnp.int32) - 1, 0, owned - 1)
    reply = jnp.take(clump_next, column, axis=1)
    answer = lax.all_to_all(reply, ("gx", "gy", "gz"), split_axis=1, concat_axis=1, tiled=True)
    frag_motion = jnp.take(answer, slot_index, axis=1)
    table = jnp.pad(frag_motion, ((0, 2), (0, 128 - held)))
    sphere_next = move(state.reshape(7, count, slots), arms.reshape(3, count, slots), frag, table)
    return sphere_next.reshape(6, cx, cy, cz, slots), clump_next


def solution(mesh):
    return jax.shard_map(
        local,
        mesh=mesh,
        in_specs=(
            P(None, "gx", "gy", "gz", None),
            P(None, "gx", "gy", "gz", None),
            P("gx", "gy", "gz", None),
            P(("gx", "gy", "gz"), None),
            P(("gx", "gy", "gz")),
            P(("gx", "gy", "gz"), None),
            P(None, ("gx", "gy", "gz")),
            P(("gx", "gy", "gz")),
            P(("gx", "gy", "gz")),
        ),
        out_specs=(P(None, "gx", "gy", "gz", None), P(None, ("gx", "gy", "gz"))),
        check_vma=False,
    )
```

```python
import functools

import jax
import jax.numpy as jnp
from jax import lax
from jax.experimental import pallas as pl
from jax.experimental.pallas import tpu as pltpu
from jax.sharding import PartitionSpec as P

CAP = 2
QUICK = 6
GROUP = 8
REACH = 0.14001
time_step = 0.01
gravity = 9.81
epsilon_sq = 1e-08
VMEM = pl.BlockSpec(memory_space=pltpu.VMEM)


def lane_take(rows, index):
    return jnp.take_along_axis(rows, index, axis=1, mode="promise_in_bounds")


def cross_rows(first, second):
    return [
        first[1] * second[2] - first[2] * second[1],
        first[2] * second[0] - first[0] * second[2],
        first[0] * second[1] - first[1] * second[0],
    ]


def pack_kernel(state, frag, table, out):
    keys = jnp.broadcast_to(table[...], (8, 128))
    for g in range(frag.shape[0] // 8):
        rows = pl.ds(8 * g, 8)
        for k in range(7):
            out[pl.ds(64 * g + k, 8, stride=8), :] = state[k, rows, :]
        out[pl.ds(64 * g + 7, 8, stride=8), :] = lane_take(keys, frag[rows, :])


def tiles_kernel(
    codes, cells, arms, frag, out, cand, mask, counts, where_v, where_s, place_v, place_s, lens_v, lens_s, items,
    carry, lists, shifts, wide_a, wide_b, push_x, push_y, push_z, loads, sems,
):
    pushes = (push_x, push_y, push_z)
    lines = codes.shape[0]
    tiles = lines * 128
    pad = cells.shape[0] // 8
    ny, nz = 6, 18
    owned = 256
    depth = lists.shape[0] // (8 * owned)
    sub = lax.broadcasted_iota(jnp.int32, (8, 128), 0)
    lane = lax.broadcasted_iota(jnp.int32, (8, 128), 1)

    code = codes[...]
    own_of = (code * 38837) >> 20
    way = code - 27 * own_of
    step_x = ((way * 57) >> 9) - 1
    left = way - 9 * (step_x + 1)
    step_y = ((left * 11) >> 5) - 1
    step_z = left - 3 * (step_y + 1) - 1
    cell_of = ((own_of >> 6) + 1 + step_x) * (ny * nz) + (((own_of >> 4) & 3) + 1 + step_y) * nz
    cell_of = cell_of + (own_of & 15) + 1 + step_z
    where_v[...] = cell_of * 8 + (way << 16)
    place_v[...] = own_of
    first_copy = pltpu.make_async_copy(where_v, where_s, sems.at[0])
    first_copy.start()

    @pl.loop(0, pad // 8)
    def _(g):
        base = pl.multiple_of(g * 64, 64)
        pos = [cells[pl.ds(base + k, 8, stride=8), :] for k in range(3)]
        reach = cells[pl.ds(base + 6, 8, stride=8), :] + REACH
        reach = reach * reach
        near = [p * p for p in pos]
        far = [(1.0 - p) * (1.0 - p) for p in pos]
        bits = jnp.full((8, 128), 1 << 13, jnp.int32)
        for o in range(27):
            steps = (o // 9 - 1, o // 3 % 3 - 1, o % 3 - 1)
            terms = [near[k] if s > 0 else far[k] for k, s in enumerate(steps) if s]
            if not terms:
                continue
            bits = bits | jnp.where(sum(terms[1:], terms[0]) <= reach, 1 << o, 0)
        cand[pl.ds(pl.multiple_of(g * 8, 8), 8), :] = bits

    @pl.loop(0, 27)
    def _(o):
        step_x = ((o * 57) >> 9) - 1
        left = o - 9 * (step_x + 1)
        step_y = ((left * 11) >> 5) - 1
        step_z = left - 3 * (step_y + 1) - 1
        value = jnp.where(sub == 0, step_x, jnp.where(sub == 1, step_y, jnp.where(sub == 2, step_z, 0)))
        shifts[pl.ds(pl.multiple_of(o * 8, 8), 8), :] = value.astype(jnp.float32)

    @pl.loop(0, owned // 16)
    def _(b):
        rows = pl.ds(pl.multiple_of(b * 128, 128), 128)
        for push in pushes:
            push[rows, :] = jnp.zeros((128, 128), jnp.float32)

    first_copy.wait()

    @pl.loop(0, tiles // 16)
    def _(b):
        line, at = b >> 3, (b & 7) * 16
        for u in range(16):
            word = where_s[line, at + u]
            mask[pl.ds(b * 16 + u, 1), :] = (cand[pl.ds((word & 0xFFFF) >> 3, 1), :] >> (word >> 16)) & 1

    row = lax.broadcasted_iota(jnp.int32, (128, 128), 0)
    col = lax.broadcasted_iota(jnp.int32, (128, 128), 1)
    before = (row < col).astype(jnp.bfloat16)
    ones = jnp.ones((8, 128), jnp.bfloat16)

    @pl.loop(0, lines)
    def _(b):
        rows = pl.ds(pl.multiple_of(b * 128, 128), 128)
        active = mask[rows, :]
        flags = active.astype(jnp.float32).astype(jnp.bfloat16)
        rank = jnp.dot(flags, before, preferred_element_type=jnp.float32).astype(jnp.int32)
        number = lax.dot_general(ones, flags, (((1,), (1,)), ((), ())), preferred_element_type=jnp.float32)
        counts[pl.ds(b, 1), :] = number[0:1]
        value = jnp.where(active > 0, ((col - rank) << 7) | col, 0)
        for bit in range(7):
            moved = pltpu.roll(value, 128 - (1 << bit), axis=1)
            flag = 1 << (7 + bit)
            value = jnp.where((moved & flag) != 0, moved, jnp.where((value & flag) != 0, 0, value))
        mask[rows, :] = value & 127

    both = jnp.concatenate([before, jnp.ones((128, 128), jnp.bfloat16)], axis=1)
    cell_id = lax.broadcasted_iota(jnp.int32, (owned, 128), 0)
    carry[...] = jnp.zeros((owned, 128), jnp.float32)

    @pl.loop(0, lines)
    def _(b):
        mine = place_v[pl.ds(b, 1), :]
        hot = cell_id == mine
        amount = jnp.where(hot, counts[pl.ds(b, 1), :], 0.0)
        summed = jnp.dot(amount.astype(jnp.bfloat16), both, preferred_element_type=jnp.float32)
        so_far = carry[...]
        at = jnp.sum(jnp.where(hot, summed[:, 0:128] + so_far, 0.0), axis=0, keepdims=True)
        carry[...] = so_far + summed[:, 128:256]
        place_v[pl.ds(b, 1), :] = mine * (depth * 128) + at.astype(jnp.int32)

    length = carry[...].T[0:8, :]
    most = jnp.max(length, axis=1, keepdims=True)
    lens_v[...] = jnp.where(lax.broadcasted_iota(jnp.int32, (8, owned), 0) == 0, length, most).astype(jnp.int32)
    copies = [
        pltpu.make_async_copy(place_v, place_s, sems.at[1]),
        pltpu.make_async_copy(lens_v, lens_s, sems.at[2]),
    ]
    for copy in copies:
        copy.start()
    for copy in copies:
        copy.wait()

    def append(sorted_rows, spot):
        turn = spot & 127
        to = pl.multiple_of((spot >> 7) * 8, 8)
        turned = pltpu.roll(sorted_rows, turn, axis=1)
        pltpu.store(lists.at[pl.ds(to, 8), :], turned, mask=lane >= turn)
        lists[pl.ds(to + 8, 8), :] = turned

    @pl.loop(0, tiles // 16)
    def _(b):
        line, at = b >> 3, (b & 7) * 16
        for u in range(16):
            word = where_s[line, at + u]
            values = cells[pl.ds(pl.multiple_of(word & 0xFFFF, 8), 8), :]
            index = jnp.broadcast_to(mask[pl.ds(b * 16 + u, 1), :], (8, 128))
            shift = shifts[pl.ds(pl.multiple_of((word >> 16) * 8, 8), 8), :]
            append(lane_take(values, index) + shift, place_s[line, at + u])

    dummy = jnp.where(sub < 3, 1000.0, 0.1)

    def item(c, k):
        return (c << 16) | (c * (2 * depth) + k)

    def close(b, total):
        for u in range(8):
            c = b * 8 + u
            length = lens_s[0, c]
            append(dummy, c * (depth * 128) + length)
            for k in range(QUICK):
                items[total + k] = item(c, k)
            total = total + jnp.minimum((length + 63) >> 6, QUICK)
        return total

    number = lax.fori_loop(0, owned // 8, close, 0)

    def longer(c, total):
        def add(k, total):
            items[total] = item(c, k)
            return total + 1

        return lax.fori_loop(QUICK, (lens_s[0, c] + 63) >> 6, add, total)

    longest = lens_s[1, 0]
    number = lax.fori_loop(0, jnp.where(longest > 64 * QUICK, owned, 0), longer, number)
    for k in range(3 * GROUP):
        items[number + k] = owned << 16

    which_row = lax.broadcasted_iota(jnp.int32, (24, 1024), 0)
    which_col = lax.broadcasted_iota(jnp.int32, (24, 1024), 1)
    pick = ((which_row & 7) == (which_col >> 7)).astype(jnp.float32).astype(jnp.bfloat16)

    def spread(words, wide):
        splits = []
        for word in words:
            spot = word & 0xFFFF
            values = lists[pl.ds(pl.multiple_of((spot >> 1) * 8, 8), 8), :]
            values = pltpu.roll(values, (spot & 1) * 64, axis=1)
            high = values.astype(jnp.bfloat16).astype(jnp.float32)
            rest = values - high
            mid = rest.astype(jnp.bfloat16).astype(jnp.float32)
            split = jnp.concatenate([high, mid, rest - mid], axis=0)
            splits.append(split.T[0:64])
        split = jnp.concatenate(splits, axis=0).astype(jnp.bfloat16)
        spreads = jnp.dot(split, pick, preferred_element_type=jnp.float32)
        for u in range(8 * len(words)):
            for k in range(8):
                wide[8 * u + k] = spreads[8 * u : 8 * u + 8, 128 * k : 128 * k + 128]

    def press(word, wide, first):
        c = word >> 16
        base = ((c >> 6) + 1) * (ny * nz) + (((c >> 4) & 3) + 1) * nz + (c & 15) + 1
        own = [jnp.broadcast_to(cells[pl.ds(base * 8 + k, 1), :], (8, 128)) for k in range(8)]
        total = [None] * 3
        for u in range(8):
            other = [wide[8 * (first + u) + k] for k in range(8)]
            apart = [other[k] - own[k] for k in range(3)]
            square = apart[0] * apart[0] + apart[1] * apart[1] + apart[2] * apart[2] + epsilon_sq
            inverse = lax.rsqrt(square)
            reach = own[6] + other[6]
            depth_in = jnp.where(own[7] != other[7], jnp.maximum(reach - square * inverse, 0.0), 0.0)
            closing = (
                (other[3] - own[3]) * apart[0] + (other[4] - own[4]) * apart[1] + (other[5] - own[5]) * apart[2]
            )
            along = closing * inverse - 50.0 * depth_in
            area = own[6] * other[6] * depth_in
            factor = area * lax.rsqrt(jnp.maximum(area * reach, 1e-20)) * along * inverse
            for k in range(3):
                term = factor * apart[k]
                total[k] = term if u == 0 else total[k] + term
        rows = pl.ds(pl.multiple_of(c * 8, 8), 8)
        for k in range(3):
            pushes[k][rows, :] += total[k]

    def group(n):
        return [items[n * GROUP + k] for k in range(GROUP)]

    spread(group(0), wide_a)

    @pl.loop(0, (number + (2 * GROUP - 1)) // (2 * GROUP))
    def _(p):
        def half(n, now, later):
            spread(group(n + 1), later)
            for k, word in enumerate(group(n)):
                press(word, now, 8 * k)

        half(2 * p, wide_a, wide_b)
        half(2 * p + 1, wide_b, wide_a)

    ids = lax.broadcasted_iota(jnp.int32, (64, 128), 0)

    def gather(g, total):
        rows = pl.ds(pl.multiple_of(g * 8, 8), 8)
        force = []
        for push in pushes:
            parts = [push[pl.ds(g * 64 + s, 8, stride=8), :] for s in range(8)]
            while len(parts) > 1:
                parts = [parts[i] + parts[i + 1] for i in range(0, len(parts), 2)]
            force.append(2.0 * parts[0])
        turn = cross_rows([arms[k, rows, :] for k in range(3)], force)
        zero = jnp.zeros((8, 128), jnp.float32)
        for k, value in enumerate(force + turn + [zero, zero]):
            loads[pl.ds(k, 8, stride=8), :] = value
        wide = jnp.concatenate([loads[pl.ds(8 * c, 8), :] for c in range(8)], axis=1)
        high = wide.astype(jnp.bfloat16).astype(jnp.float32)
        rest = wide - high
        mid = rest.astype(jnp.bfloat16).astype(jnp.float32)
        split = jnp.concatenate([high, mid, rest - mid], axis=0).astype(jnp.bfloat16)
        which = jnp.concatenate(
            [(ids == frag[pl.ds(g * 8 + c, 1), :]).astype(jnp.float32) for c in range(8)], axis=1
        ).astype(jnp.bfloat16)
        return total + lax.dot_general(split, which, (((1,), (1,)), ((), ())), preferred_element_type=jnp.float32)

    total = lax.fori_loop(0, owned // 8, gather, jnp.zeros((24, 64), jnp.float32))
    out[...] = total[0:8] + total[8:16] + total[16:24]


def move_kernel(state, arms, frag, table, out):
    rows_of = [jnp.broadcast_to(table[k : k + 1, :], (8, 128)) for k in range(6)]
    for g in range(frag.shape[0] // 8):
        rows = pl.ds(8 * g, 8)
        index = frag[rows, :]
        motion = [lane_take(r, index) for r in rows_of]
        velocity, spin = motion[0:3], motion[3:6]
        lever = [arms[k, rows, :] for k in range(3)]
        half = [0.5 * time_step * w for w in spin]
        turned = cross_rows(half, lever)
        twice = cross_rows(half, turned)
        scale = 2.0 / (1.0 + half[0] * half[0] + half[1] * half[1] + half[2] * half[2])
        moved = [lever[k] + scale * (turned[k] + twice[k]) for k in range(3)]
        swing = cross_rows(spin, moved)
        for k in range(3):
            out[k, rows, :] = state[k, rows, :] + time_step * velocity[k] + (moved[k] - lever[k])
            out[3 + k, rows, :] = velocity[k] + swing[k]


def pack(state, frag, table):
    n = frag.shape[0]
    part = n // 4
    return pl.pallas_call(
        pack_kernel,
        grid=(4,),
        in_specs=[
            pl.BlockSpec((7, part, 128), lambda i: (0, i, 0)),
            pl.BlockSpec((part, 128), lambda i: (i, 0)),
            pl.BlockSpec((1, 128), lambda i: (0, 0)),
        ],
        out_specs=pl.BlockSpec((8 * part, 128), lambda i: (i, 0)),
        out_shape=jax.ShapeDtypeStruct((8 * n, 128), jnp.float32),
        name="pack",
    )(state, frag, table)


def forces(codes, cells, arms, frag):
    lines = codes.shape[0] // 128
    owned, depth = frag.shape[0], 29
    return pl.pallas_call(
        tiles_kernel,
        in_specs=[VMEM, VMEM, VMEM, VMEM],
        out_specs=VMEM,
        out_shape=jax.ShapeDtypeStruct((8, 64), jnp.float32),
        scratch_shapes=[
            pltpu.VMEM((cells.shape[0] // 8, 128), jnp.int32),
            pltpu.VMEM((lines * 128, 128), jnp.int32),
            pltpu.VMEM((lines, 128), jnp.float32),
            pltpu.VMEM((lines, 128), jnp.int32),
            pltpu.SMEM((lines, 128), jnp.int32),
            pltpu.VMEM((lines, 128), jnp.int32),
            pltpu.SMEM((lines, 128), jnp.int32),
            pltpu.VMEM((8, owned), jnp.int32),
            pltpu.SMEM((8, owned), jnp.int32),
            pltpu.SMEM((owned * 54 + 32,), jnp.int32),
            pltpu.VMEM((owned, 128), jnp.float32),
            pltpu.VMEM((owned * depth * 8, 128), jnp.float32),
            pltpu.VMEM((27 * 8, 128), jnp.float32),
            pltpu.VMEM((64 * GROUP, 8, 128), jnp.float32),
            pltpu.VMEM((64 * GROUP, 8, 128), jnp.float32),
            pltpu.VMEM((owned * 8 + 8, 128), jnp.float32),
            pltpu.VMEM((owned * 8 + 8, 128), jnp.float32),
            pltpu.VMEM((owned * 8 + 8, 128), jnp.float32),
            pltpu.VMEM((64, 128), jnp.float32),
            pltpu.SemaphoreType.DMA((3,)),
        ],
        compiler_params=pltpu.CompilerParams(vmem_limit_bytes=60 * 1024 * 1024),
        name="forces",
    )(codes.reshape(lines, 128), cells, arms, frag)


def move(state, arms, frag, table):
    n = frag.shape[0]
    part = n // 4
    return pl.pallas_call(
        move_kernel,
        grid=(4,),
        in_specs=[
            pl.BlockSpec((3, part, 128), lambda i: (0, i, 0)),
            pl.BlockSpec((3, part, 128), lambda i: (0, i, 0)),
            pl.BlockSpec((part, 128), lambda i: (i, 0)),
            pl.BlockSpec((8, 128), lambda i: (0, 0)),
        ],
        out_specs=pl.BlockSpec((6, part, 128), lambda i: (0, i, 0)),
        out_shape=jax.ShapeDtypeStruct((6, n, 128), jnp.float32),
        name="move",
    )(state, arms, frag, table)


def with_halo(x, sides):
    for axis, dim in sides:
        devices, length = (lax.axis_size(axis), x.shape[dim])
        up = [(i, (i + 1) % devices) for i in range(devices)]
        down = [(j, i) for i, j in up]
        last = lax.slice_in_dim(x, length - 1, length, axis=dim)
        initial = lax.slice_in_dim(x, 0, 1, axis=dim)
        before = lax.ppermute(last, axis, up)
        after = lax.ppermute(initial, axis, down)
        x = jnp.concatenate([before, x, after], axis=dim)
    return x


def advance(motion, sums, inv_mass, inv_moment):
    pull = jnp.array([0.0, 0.0, gravity], jnp.float32)[:, None]
    velocity = motion[0:3] + time_step * (sums[0:3] * inv_mass[None, :] - pull)
    spin = motion[3:6] + time_step * sums[3:6] * inv_moment[None, :]
    return jnp.concatenate([velocity, spin], axis=0)


def local(state, arms, sphere_frag, frag_owner, frag_clump, tiles, clump_motion, inv_mass, inv_moment):
    cx, cy, cz, slots = state.shape[1:]
    count = cx * cy * cz
    owned = inv_mass.shape[0]
    held = frag_clump.shape[0]
    bricks = lax.axis_size("gx") * lax.axis_size("gy") * lax.axis_size("gz")
    owner = frag_owner[:, 0]
    frag = sphere_frag.reshape(count, slots)
    key = (owner * owned + frag_clump).astype(jnp.float32)
    own_cells = pack(state.reshape(7, count, slots), frag, jnp.pad(key, (0, 128 - held))[None])
    padded = with_halo(own_cells.reshape(cx, cy, cz, 8, slots), (("gx", 0), ("gy", 1), ("gz", 2)))
    frag_sums = forces(tiles[0], padded.reshape(-1, slots), arms.reshape(3, count, slots), frag)[0:6]

    hits = (owner[:, None] == jnp.arange(bricks, dtype=jnp.int32)[None, :]).astype(jnp.int32)
    rank = jnp.sum((jnp.cumsum(hits, axis=0) - hits) * hits, axis=1)
    slot_index = owner * CAP + rank
    payload = jnp.concatenate([frag_sums, (frag_clump + 1).astype(jnp.float32)[None]], axis=0)
    outbox = jnp.zeros((7, bricks * CAP), jnp.float32).at[:, slot_index].set(payload)
    inbox = lax.all_to_all(outbox, ("gx", "gy", "gz"), split_axis=1, concat_axis=1, tiled=True)
    labels = (jnp.arange(owned, dtype=jnp.int32) + 1).astype(jnp.float32)
    which = (inbox[6][:, None] == labels[None, :]).astype(jnp.float32)
    clump_sums = jnp.dot(
        inbox[0:6], which, precision=lax.Precision.HIGHEST, preferred_element_type=jnp.float32
    )
    clump_next = advance(clump_motion, clump_sums, inv_mass, inv_moment)
    column = jnp.clip(inbox[6].astype(jnp.int32) - 1, 0, owned - 1)
    reply = jnp.take(clump_next, column, axis=1)
    answer = lax.all_to_all(reply, ("gx", "gy", "gz"), split_axis=1, concat_axis=1, tiled=True)
    frag_motion = jnp.take(answer, slot_index, axis=1)
    table = jnp.pad(frag_motion, ((0, 2), (0, 128 - held)))
    sphere_next = move(state.reshape(7, count, slots), arms.reshape(3, count, slots), frag, table)
    return sphere_next.reshape(6, cx, cy, cz, slots), clump_next


def solution(mesh):
    return jax.shard_map(
        local,
        mesh=mesh,
        in_specs=(
            P(None, "gx", "gy", "gz", None),
            P(None, "gx", "gy", "gz", None),
            P("gx", "gy", "gz", None),
            P(("gx", "gy", "gz"), None),
            P(("gx", "gy", "gz")),
            P(("gx", "gy", "gz"), None),
            P(None, ("gx", "gy", "gz")),
            P(("gx", "gy", "gz")),
            P(("gx", "gy", "gz")),
        ),
        out_specs=(P(None, "gx", "gy", "gz", None), P(None, ("gx", "gy", "gz"))),
        check_vma=False,
    )
```

```python
import functools

import jax
import jax.numpy as jnp
from jax import lax
from jax.experimental import pallas as pl
from jax.experimental.pallas import tpu as pltpu
from jax.sharding import PartitionSpec as P

CAP = 2
OWN = 48
QUICK = 6
GROUP = 8
REACH = 0.14001
time_step = 0.01
gravity = 9.81
epsilon_sq = 1e-08
VMEM = pl.BlockSpec(memory_space=pltpu.VMEM)


def lane_take(rows, index):
    return jnp.take_along_axis(rows, index, axis=1, mode="promise_in_bounds")


def cross_rows(first, second):
    return [
        first[1] * second[2] - first[2] * second[1],
        first[2] * second[0] - first[0] * second[2],
        first[0] * second[1] - first[1] * second[0],
    ]


MESH = pl.DeviceIdType.MESH
HBM = pl.BlockSpec(memory_space=pl.ANY)


def place_of(shift):
    return tuple(
        lax.rem(lax.axis_index(axis) + step + lax.axis_size(axis), lax.axis_size(axis))
        for axis, step in zip(("gx", "gy", "gz"), shift)
    )


def meet(others):
    barrier = pltpu.get_barrier_semaphore()
    for other in others:
        pl.semaphore_signal(barrier, inc=1, device_id=other, device_id_type=MESH)
    return lambda: pl.semaphore_wait(barrier, len(others))


def halo_kernel(state, frag, info, out, own, send, recv, near):
    sizes = out.shape[0] - 2, out.shape[1] - 2, out.shape[2] - 2
    shifts = [(o // 9 - 1, o // 3 % 3 - 1, o % 3 - 1) for o in range(27) if o != 13]
    shifts.sort(key=lambda s: sum(map(abs, s)))
    arrive = meet([place_of(s) for s in shifts])
    keys = info[0:1, :] * OWN + info[1:2, :]
    keys = jnp.broadcast_to(keys.astype(jnp.float32), (8, 128))
    for g in range(frag.shape[0] // 8):
        rows = pl.ds(8 * g, 8)
        for k in range(7):
            own[pl.ds(64 * g + k, 8, stride=8), :] = state[k, rows, :]
        own[pl.ds(64 * g + 7, 8, stride=8), :] = lane_take(keys, frag[rows, :])
    arrive()
    cells = own.reshape(sizes + (8, 128))
    copies = []
    for n, shift in enumerate(shifts):
        source = [pl.ds(0, size) if s == 0 else pl.ds(size - 1 if s > 0 else 0, 1) for s, size in zip(shift, sizes)]
        target = [pl.ds(1, size) if s == 0 else pl.ds(0 if s > 0 else size + 1, 1) for s, size in zip(shift, sizes)]
        copies.append(
            pltpu.make_async_remote_copy(
                src_ref=cells.at[tuple(source)],
                dst_ref=out.at[tuple(target)],
                send_sem=send.at[n],
                recv_sem=recv.at[n],
                device_id=place_of(shift),
                device_id_type=MESH,
            )
        )
        copies[-1].start()
    inner = pltpu.make_async_copy(cells, out.at[tuple(pl.ds(1, size) for size in sizes)], near)
    inner.start()
    for copy in copies:
        copy.wait()
    inner.wait()


def exchange_kernel(
    info, sums, motion, mass, moment, table, clump_next,
    outbox, got_z, got_y, inbox, reply, back_x, back_y, answer, send, recv, near,
):
    axes = ("gz", "gy", "gx")
    me = {axis: lax.axis_index(axis) for axis in axes}
    size = {axis: lax.axis_size(axis) for axis in axes}
    peers = {
        axis: [lax.rem(me[axis] + d, size[axis]) for d in range(1, size[axis])] for axis in axes
    }

    def device(axis, index):
        return tuple(index if a == axis else me[a] for a in ("gx", "gy", "gz"))

    arrive = meet([device(axis, p) for axis in axes for p in peers[axis]])

    def stage(number, axis, source, target):
        copies = [pltpu.make_async_copy(source(me[axis]), target(me[axis]), near.at[number])]
        copies[0].start()
        for n, peer in enumerate(peers[axis]):
            copies.append(
                pltpu.make_async_remote_copy(
                    src_ref=source(peer),
                    dst_ref=target(me[axis]),
                    send_sem=send.at[number, n],
                    recv_sem=recv.at[number, n],
                    device_id=device(axis, peer),
                    device_id_type=MESH,
                )
            )
            copies[-1].start()
        for copy in copies:
            copy.wait()

    exact = dict(precision=lax.Precision.HIGHEST, preferred_element_type=jnp.float32)
    owner = info[0:1, :]
    place = (owner & 7) * 16 + ((owner >> 3) & 3) * 4 + (owner >> 5)
    place = jnp.where(owner >= 0, place, -1)
    row = lax.broadcasted_iota(jnp.int32, (128, 128), 0)
    col = lax.broadcasted_iota(jnp.int32, (128, 128), 1)
    hit = (row == place).astype(jnp.float32)
    earlier = jnp.dot(
        hit.astype(jnp.bfloat16), (row < col).astype(jnp.float32).astype(jnp.bfloat16),
        preferred_element_type=jnp.float32,
    )
    slots = [jnp.where(earlier == float(e), hit, 0.0) for e in range(CAP)]
    across = (((1,), (1,)), ((), ()))
    filler = jnp.zeros((112, 128), jnp.float32)
    empty = jnp.zeros((8, 128), jnp.float32)
    sub = lax.broadcasted_iota(jnp.int32, (8, 128), 0)
    label = (info[1:2, :] + 1).astype(jnp.float32)
    payload = jnp.where(sub == 6, label, jnp.where(sub == 7, 0.0, sums[...]))
    outbox[...] = (
        lax.dot_general(slots[0], jnp.concatenate([payload, empty, filler], axis=0), across, **exact)
        + lax.dot_general(slots[1], jnp.concatenate([empty, payload, filler], axis=0), across, **exact)
    ).reshape(outbox.shape)
    arrive()
    stage(0, "gz", lambda p: outbox.at[p], lambda p: got_z.at[:, p])
    by_y = got_z.reshape(4, 4, 8, 128)
    stage(1, "gy", lambda p: by_y.at[p], lambda p: got_y.at[:, p])
    stage(2, "gx", lambda p: got_y.at[p], lambda p: inbox.at[p])

    flat = inbox[...].reshape(128, 128)
    turned = flat.T
    names = lax.broadcasted_iota(jnp.int32, (128, motion.shape[1]), 1).astype(jnp.float32) + 1.0
    which = [(jnp.broadcast_to(flat[:, 8 * e + 6 : 8 * e + 7], names.shape) == names).astype(jnp.float32) for e in range(CAP)]
    total = jnp.dot(turned[0:8], which[0], **exact) + jnp.dot(turned[8:16], which[1], **exact)
    lower = lax.broadcasted_iota(jnp.int32, (3, motion.shape[1]), 0)
    pull = jnp.where(lower == 2, gravity, 0.0)
    velocity = motion[0:3, :] + time_step * (total[0:3] * mass[...] - pull)
    spin = motion[3:6, :] + time_step * total[3:6] * moment[...]
    clump_next[0:3, :] = velocity
    clump_next[3:6, :] = spin
    moved = jnp.concatenate([velocity, spin, jnp.zeros((2, motion.shape[1]), jnp.float32)], axis=0)
    blank = jnp.zeros((8, motion.shape[1]), jnp.float32)
    rest = jnp.zeros((112, motion.shape[1]), jnp.float32)
    reply[...] = (
        lax.dot_general(which[0], jnp.concatenate([moved, blank, rest], axis=0), across, **exact)
        + lax.dot_general(which[1], jnp.concatenate([blank, moved, rest], axis=0), across, **exact)
    ).reshape(reply.shape)
    stage(3, "gx", lambda p: reply.at[p], lambda p: back_x.at[p])
    stage(4, "gy", lambda p: back_x.at[:, p], lambda p: back_y.at[p])
    by_z = back_y.reshape(16, 8, 128)
    stage(5, "gz", lambda p: by_z.at[:, p], lambda p: answer.at[p])
    turned = answer[...].reshape(128, 128).T
    table[...] = jnp.dot(turned[0:8], slots[0], **exact) + jnp.dot(turned[8:16], slots[1], **exact)


def tiles_kernel(
    codes, cells, arms, frag, out, cand, mask, counts, where_v, where_s, place_v, place_s, lens_v, lens_s, items,
    carry, lists, shifts, wide_a, wide_b, push_x, push_y, push_z, loads, sems,
):
    pushes = (push_x, push_y, push_z)
    lines = codes.shape[0]
    tiles = lines * 128
    pad = cells.shape[0] // 8
    ny, nz = 6, 18
    owned = 256
    depth = lists.shape[0] // (8 * owned)
    sub = lax.broadcasted_iota(jnp.int32, (8, 128), 0)
    lane = lax.broadcasted_iota(jnp.int32, (8, 128), 1)

    code = codes[...]
    own_of = (code * 38837) >> 20
    way = code - 27 * own_of
    step_x = ((way * 57) >> 9) - 1
    left = way - 9 * (step_x + 1)
    step_y = ((left * 11) >> 5) - 1
    step_z = left - 3 * (step_y + 1) - 1
    cell_of = ((own_of >> 6) + 1 + step_x) * (ny * nz) + (((own_of >> 4) & 3) + 1 + step_y) * nz
    cell_of = cell_of + (own_of & 15) + 1 + step_z
    where_v[...] = cell_of * 8 + (way << 16)
    place_v[...] = own_of
    first_copy = pltpu.make_async_copy(where_v, where_s, sems.at[0])
    first_copy.start()

    @pl.loop(0, pad // 8)
    def _(g):
        base = pl.multiple_of(g * 64, 64)
        pos = [cells[pl.ds(base + k, 8, stride=8), :] for k in range(3)]
        reach = cells[pl.ds(base + 6, 8, stride=8), :] + REACH
        reach = reach * reach
        near = [p * p for p in pos]
        far = [(1.0 - p) * (1.0 - p) for p in pos]
        bits = jnp.full((8, 128), 1 << 13, jnp.int32)
        for o in range(27):
            steps = (o // 9 - 1, o // 3 % 3 - 1, o % 3 - 1)
            terms = [near[k] if s > 0 else far[k] for k, s in enumerate(steps) if s]
            if not terms:
                continue
            bits = bits | jnp.where(sum(terms[1:], terms[0]) <= reach, 1 << o, 0)
        cand[pl.ds(pl.multiple_of(g * 8, 8), 8), :] = bits

    @pl.loop(0, 27)
    def _(o):
        step_x = ((o * 57) >> 9) - 1
        left = o - 9 * (step_x + 1)
        step_y = ((left * 11) >> 5) - 1
        step_z = left - 3 * (step_y + 1) - 1
        value = jnp.where(sub == 0, step_x, jnp.where(sub == 1, step_y, jnp.where(sub == 2, step_z, 0)))
        shifts[pl.ds(pl.multiple_of(o * 8, 8), 8), :] = value.astype(jnp.float32)

    @pl.loop(0, owned // 16)
    def _(b):
        rows = pl.ds(pl.multiple_of(b * 128, 128), 128)
        for push in pushes:
            push[rows, :] = jnp.zeros((128, 128), jnp.float32)

    first_copy.wait()

    @pl.loop(0, tiles // 16)
    def _(b):
        line, at = b >> 3, (b & 7) * 16
        for u in range(16):
            word = where_s[line, at + u]
            mask[pl.ds(b * 16 + u, 1), :] = (cand[pl.ds((word & 0xFFFF) >> 3, 1), :] >> (word >> 16)) & 1

    row = lax.broadcasted_iota(jnp.int32, (128, 128), 0)
    col = lax.broadcasted_iota(jnp.int32, (128, 128), 1)
    before = (row < col).astype(jnp.bfloat16)
    ones = jnp.ones((8, 128), jnp.bfloat16)

    @pl.loop(0, lines)
    def _(b):
        rows = pl.ds(pl.multiple_of(b * 128, 128), 128)
        active = mask[rows, :]
        flags = active.astype(jnp.float32).astype(jnp.bfloat16)
        rank = jnp.dot(flags, before, preferred_element_type=jnp.float32).astype(jnp.int32)
        number = lax.dot_general(ones, flags, (((1,), (1,)), ((), ())), preferred_element_type=jnp.float32)
        counts[pl.ds(b, 1), :] = number[0:1]
        value = jnp.where(active > 0, ((col - rank) << 7) | col, 0)
        for bit in range(7):
            moved = pltpu.roll(value, 128 - (1 << bit), axis=1)
            flag = 1 << (7 + bit)
            value = jnp.where((moved & flag) != 0, moved, jnp.where((value & flag) != 0, 0, value))
        mask[rows, :] = value & 127

    both = jnp.concatenate([before, jnp.ones((128, 128), jnp.bfloat16)], axis=1)
    cell_id = lax.broadcasted_iota(jnp.int32, (owned, 128), 0)
    carry[...] = jnp.zeros((owned, 128), jnp.float32)

    @pl.loop(0, lines)
    def _(b):
        mine = place_v[pl.ds(b, 1), :]
        hot = cell_id == mine
        amount = jnp.where(hot, counts[pl.ds(b, 1), :], 0.0)
        summed = jnp.dot(amount.astype(jnp.bfloat16), both, preferred_element_type=jnp.float32)
        so_far = carry[...]
        at = jnp.sum(jnp.where(hot, summed[:, 0:128] + so_far, 0.0), axis=0, keepdims=True)
        carry[...] = so_far + summed[:, 128:256]
        place_v[pl.ds(b, 1), :] = mine * (depth * 128) + at.astype(jnp.int32)

    length = carry[...].T[0:8, :]
    most = jnp.max(length, axis=1, keepdims=True)
    lens_v[...] = jnp.where(lax.broadcasted_iota(jnp.int32, (8, owned), 0) == 0, length, most).astype(jnp.int32)
    copies = [
        pltpu.make_async_copy(place_v, place_s, sems.at[1]),
        pltpu.make_async_copy(lens_v, lens_s, sems.at[2]),
    ]
    for copy in copies:
        copy.start()
    for copy in copies:
        copy.wait()

    def append(sorted_rows, spot):
        turn = spot & 127
        to = pl.multiple_of((spot >> 7) * 8, 8)
        turned = pltpu.roll(sorted_rows, turn, axis=1)
        pltpu.store(lists.at[pl.ds(to, 8), :], turned, mask=lane >= turn)
        lists[pl.ds(to + 8, 8), :] = turned

    @pl.loop(0, tiles // 16)
    def _(b):
        line, at = b >> 3, (b & 7) * 16
        for u in range(16):
            word = where_s[line, at + u]
            values = cells[pl.ds(pl.multiple_of(word & 0xFFFF, 8), 8), :]
            index = jnp.broadcast_to(mask[pl.ds(b * 16 + u, 1), :], (8, 128))
            shift = shifts[pl.ds(pl.multiple_of((word >> 16) * 8, 8), 8), :]
            append(lane_take(values, index) + shift, place_s[line, at + u])

    dummy = jnp.where(sub < 3, 1000.0, 0.1)

    def item(c, k):
        return (c << 16) | (c * (2 * depth) + k)

    def close(b, total):
        for u in range(8):
            c = b * 8 + u
            length = lens_s[0, c]
            append(dummy, c * (depth * 128) + length)
            for k in range(QUICK):
                items[total + k] = item(c, k)
            total = total + jnp.minimum((length + 63) >> 6, QUICK)
        return total

    number = lax.fori_loop(0, owned // 8, close, 0)

    def longer(c, total):
        def add(k, total):
            items[total] = item(c, k)
            return total + 1

        return lax.fori_loop(QUICK, (lens_s[0, c] + 63) >> 6, add, total)

    longest = lens_s[1, 0]
    number = lax.fori_loop(0, jnp.where(longest > 64 * QUICK, owned, 0), longer, number)
    for k in range(3 * GROUP):
        items[number + k] = owned << 16

    which_row = lax.broadcasted_iota(jnp.int32, (24, 1024), 0)
    which_col = lax.broadcasted_iota(jnp.int32, (24, 1024), 1)
    pick = ((which_row & 7) == (which_col >> 7)).astype(jnp.float32).astype(jnp.bfloat16)

    def spread(words, wide):
        splits = []
        for word in words:
            spot = word & 0xFFFF
            values = lists[pl.ds(pl.multiple_of((spot >> 1) * 8, 8), 8), :]
            values = pltpu.roll(values, (spot & 1) * 64, axis=1)
            high = values.astype(jnp.bfloat16).astype(jnp.float32)
            rest = values - high
            mid = rest.astype(jnp.bfloat16).astype(jnp.float32)
            split = jnp.concatenate([high, mid, rest - mid], axis=0)
            splits.append(split.T[0:64])
        split = jnp.concatenate(splits, axis=0).astype(jnp.bfloat16)
        spreads = jnp.dot(split, pick, preferred_element_type=jnp.float32)
        for u in range(8 * len(words)):
            for k in range(8):
                wide[8 * u + k] = spreads[8 * u : 8 * u + 8, 128 * k : 128 * k + 128]

    def press(word, wide, first):
        c = word >> 16
        base = ((c >> 6) + 1) * (ny * nz) + (((c >> 4) & 3) + 1) * nz + (c & 15) + 1
        own = [jnp.broadcast_to(cells[pl.ds(base * 8 + k, 1), :], (8, 128)) for k in range(8)]
        total = [None] * 3
        for u in range(8):
            other = [wide[8 * (first + u) + k] for k in range(8)]
            apart = [other[k] - own[k] for k in range(3)]
            square = apart[0] * apart[0] + apart[1] * apart[1] + apart[2] * apart[2] + epsilon_sq
            inverse = lax.rsqrt(square)
            reach = own[6] + other[6]
            depth_in = jnp.where(own[7] != other[7], jnp.maximum(reach - square * inverse, 0.0), 0.0)
            closing = (
                (other[3] - own[3]) * apart[0] + (other[4] - own[4]) * apart[1] + (other[5] - own[5]) * apart[2]
            )
            along = closing * inverse - 50.0 * depth_in
            area = own[6] * other[6] * depth_in
            factor = area * lax.rsqrt(jnp.maximum(area * reach, 1e-20)) * along * inverse
            for k in range(3):
                term = factor * apart[k]
                total[k] = term if u == 0 else total[k] + term
        rows = pl.ds(pl.multiple_of(c * 8, 8), 8)
        for k in range(3):
            pushes[k][rows, :] += total[k]

    def group(n):
        return [items[n * GROUP + k] for k in range(GROUP)]

    spread(group(0), wide_a)

    @pl.loop(0, (number + (2 * GROUP - 1)) // (2 * GROUP))
    def _(p):
        def half(n, now, later):
            spread(group(n + 1), later)
            for k, word in enumerate(group(n)):
                press(word, now, 8 * k)

        half(2 * p, wide_a, wide_b)
        half(2 * p + 1, wide_b, wide_a)

    ids = lax.broadcasted_iota(jnp.int32, (128, 128), 0)

    def gather(g, total):
        rows = pl.ds(pl.multiple_of(g * 8, 8), 8)
        force = []
        for push in pushes:
            parts = [push[pl.ds(g * 64 + s, 8, stride=8), :] for s in range(8)]
            while len(parts) > 1:
                parts = [parts[i] + parts[i + 1] for i in range(0, len(parts), 2)]
            force.append(2.0 * parts[0])
        turn = cross_rows([arms[k, rows, :] for k in range(3)], force)
        zero = jnp.zeros((8, 128), jnp.float32)
        for k, value in enumerate(force + turn + [zero, zero]):
            loads[pl.ds(k, 8, stride=8), :] = value
        wide = jnp.concatenate([loads[pl.ds(8 * c, 8), :] for c in range(8)], axis=1)
        high = wide.astype(jnp.bfloat16).astype(jnp.float32)
        rest = wide - high
        mid = rest.astype(jnp.bfloat16).astype(jnp.float32)
        split = jnp.concatenate([high, mid, rest - mid], axis=0).astype(jnp.bfloat16)
        which = jnp.concatenate(
            [(ids == frag[pl.ds(g * 8 + c, 1), :]).astype(jnp.float32) for c in range(8)], axis=1
        ).astype(jnp.bfloat16)
        return total + lax.dot_general(split, which, (((1,), (1,)), ((), ())), preferred_element_type=jnp.float32)

    total = lax.fori_loop(0, owned // 8, gather, jnp.zeros((24, 128), jnp.float32))
    out[...] = total[0:8] + total[8:16] + total[16:24]


def move_kernel(state, arms, frag, table, out):
    rows_of = [jnp.broadcast_to(table[k : k + 1, :], (8, 128)) for k in range(6)]
    for g in range(frag.shape[0] // 8):
        rows = pl.ds(8 * g, 8)
        index = frag[rows, :]
        motion = [lane_take(r, index) for r in rows_of]
        velocity, spin = motion[0:3], motion[3:6]
        lever = [arms[k, rows, :] for k in range(3)]
        half = [0.5 * time_step * w for w in spin]
        turned = cross_rows(half, lever)
        twice = cross_rows(half, turned)
        scale = 2.0 / (1.0 + half[0] * half[0] + half[1] * half[1] + half[2] * half[2])
        moved = [lever[k] + scale * (turned[k] + twice[k]) for k in range(3)]
        swing = cross_rows(spin, moved)
        for k in range(3):
            out[k, rows, :] = state[k, rows, :] + time_step * velocity[k] + (moved[k] - lever[k])
            out[3 + k, rows, :] = velocity[k] + swing[k]


def halo(state, frag, info, cells):
    return pl.pallas_call(
        halo_kernel,
        in_specs=[VMEM, VMEM, VMEM],
        out_specs=HBM,
        out_shape=jax.ShapeDtypeStruct(tuple(c + 2 for c in cells) + (8, 128), jnp.float32),
        scratch_shapes=[
            pltpu.VMEM((8 * frag.shape[0], 128), jnp.float32),
            pltpu.SemaphoreType.DMA((26,)),
            pltpu.SemaphoreType.DMA((26,)),
            pltpu.SemaphoreType.DMA,
        ],
        compiler_params=pltpu.CompilerParams(collective_id=0, has_side_effects=True),
        name="halo",
    )(state, frag, info)


def exchange(info, sums, motion, mass, moment):
    block = lambda *shape: pltpu.VMEM(shape + (128,), jnp.float32)
    return pl.pallas_call(
        exchange_kernel,
        in_specs=[VMEM] * 5,
        out_specs=(VMEM, VMEM),
        out_shape=(
            jax.ShapeDtypeStruct((8, 128), jnp.float32),
            jax.ShapeDtypeStruct(motion.shape, jnp.float32),
        ),
        scratch_shapes=[
            block(8, 16),
            block(16, 8),
            block(4, 4, 8),
            block(4, 4, 8),
            block(4, 4, 8),
            block(4, 4, 8),
            block(4, 4, 8),
            block(8, 16),
            pltpu.SemaphoreType.DMA((6, 7)),
            pltpu.SemaphoreType.DMA((6, 7)),
            pltpu.SemaphoreType.DMA((6,)),
        ],
        compiler_params=pltpu.CompilerParams(collective_id=1, has_side_effects=True),
        name="exchange",
    )(info, sums, motion, mass, moment)


def forces(codes, cells, arms, frag):
    lines = codes.shape[0] // 128
    owned, depth = frag.shape[0], 29
    return pl.pallas_call(
        tiles_kernel,
        in_specs=[VMEM, VMEM, VMEM, VMEM],
        out_specs=VMEM,
        out_shape=jax.ShapeDtypeStruct((8, 128), jnp.float32),
        scratch_shapes=[
            pltpu.VMEM((cells.shape[0] // 8, 128), jnp.int32),
            pltpu.VMEM((lines * 128, 128), jnp.int32),
            pltpu.VMEM((lines, 128), jnp.float32),
            pltpu.VMEM((lines, 128), jnp.int32),
            pltpu.SMEM((lines, 128), jnp.int32),
            pltpu.VMEM((lines, 128), jnp.int32),
            pltpu.SMEM((lines, 128), jnp.int32),
            pltpu.VMEM((8, owned), jnp.int32),
            pltpu.SMEM((8, owned), jnp.int32),
            pltpu.SMEM((owned * 54 + 32,), jnp.int32),
            pltpu.VMEM((owned, 128), jnp.float32),
            pltpu.VMEM((owned * depth * 8, 128), jnp.float32),
            pltpu.VMEM((27 * 8, 128), jnp.float32),
            pltpu.VMEM((64 * GROUP, 8, 128), jnp.float32),
            pltpu.VMEM((64 * GROUP, 8, 128), jnp.float32),
            pltpu.VMEM((owned * 8 + 8, 128), jnp.float32),
            pltpu.VMEM((owned * 8 + 8, 128), jnp.float32),
            pltpu.VMEM((owned * 8 + 8, 128), jnp.float32),
            pltpu.VMEM((64, 128), jnp.float32),
            pltpu.SemaphoreType.DMA((3,)),
        ],
        compiler_params=pltpu.CompilerParams(vmem_limit_bytes=60 * 1024 * 1024),
        name="forces",
    )(codes.reshape(lines, 128), cells, arms, frag)


def move(state, arms, frag, table):
    n = frag.shape[0]
    part = n // 4
    return pl.pallas_call(
        move_kernel,
        grid=(4,),
        in_specs=[
            pl.BlockSpec((3, part, 128), lambda i: (0, i, 0)),
            pl.BlockSpec((3, part, 128), lambda i: (0, i, 0)),
            pl.BlockSpec((part, 128), lambda i: (i, 0)),
            pl.BlockSpec((8, 128), lambda i: (0, 0)),
        ],
        out_specs=pl.BlockSpec((6, part, 128), lambda i: (0, i, 0)),
        out_shape=jax.ShapeDtypeStruct((6, n, 128), jnp.float32),
        name="move",
    )(state, arms, frag, table)


def local(state, arms, sphere_frag, frag_owner, frag_clump, tiles, clump_motion, inv_mass, inv_moment):
    cells = state.shape[1:4]
    slots = state.shape[4]
    count = cells[0] * cells[1] * cells[2]
    held = frag_clump.shape[0]
    frag = sphere_frag.reshape(count, slots)
    info = jnp.pad(jnp.stack([frag_owner[:, 0], frag_clump]), ((0, 0), (0, slots - held)), constant_values=-1)
    padded = halo(state.reshape(7, count, slots), frag, info, cells)
    sums = forces(tiles[0], padded.reshape(-1, slots), arms.reshape(3, count, slots), frag)
    table, clump_next = exchange(info, sums, clump_motion, inv_mass[None], inv_moment[None])
    sphere_next = move(state.reshape(7, count, slots), arms.reshape(3, count, slots), frag, table)
    return sphere_next.reshape((6,) + cells + (slots,)), clump_next


def solution(mesh):
    return jax.shard_map(
        local,
        mesh=mesh,
        in_specs=(
            P(None, "gx", "gy", "gz", None),
            P(None, "gx", "gy", "gz", None),
            P("gx", "gy", "gz", None),
            P(("gx", "gy", "gz"), None),
            P(("gx", "gy", "gz")),
            P(("gx", "gy", "gz"), None),
            P(None, ("gx", "gy", "gz")),
            P(("gx", "gy", "gz")),
            P(("gx", "gy", "gz")),
        ),
        out_specs=(P(None, "gx", "gy", "gz", None), P(None, ("gx", "gy", "gz"))),
        check_vma=False,
    )
```

```python
import functools

import jax
import jax.numpy as jnp
from jax import lax
from jax.experimental import pallas as pl
from jax.experimental.pallas import tpu as pltpu
from jax.sharding import PartitionSpec as P

CAP = 2
OWN = 48
QUICK = 8
GROUP = 8
REACH = 0.14001
time_step = 0.01
gravity = 9.81
epsilon_sq = 1e-08
VMEM = pl.BlockSpec(memory_space=pltpu.VMEM)


def lane_take(rows, index):
    return jnp.take_along_axis(rows, index, axis=1, mode="promise_in_bounds")


def cross_rows(first, second):
    return [
        first[1] * second[2] - first[2] * second[1],
        first[2] * second[0] - first[0] * second[2],
        first[0] * second[1] - first[1] * second[0],
    ]


MESH = pl.DeviceIdType.MESH
HBM = pl.BlockSpec(memory_space=pl.ANY)


def place_of(shift):
    return tuple(
        lax.rem(lax.axis_index(axis) + step + lax.axis_size(axis), lax.axis_size(axis))
        for axis, step in zip(("gx", "gy", "gz"), shift)
    )


def meet(others):
    barrier = pltpu.get_barrier_semaphore()
    for other in others:
        pl.semaphore_signal(barrier, inc=1, device_id=other, device_id_type=MESH)
    return lambda: pl.semaphore_wait(barrier, len(others))


def halo_kernel(state, frag, owner, clump, out, info, own, send, recv, near):
    sizes = out.shape[0] - 2, out.shape[1] - 2, out.shape[2] - 2
    shifts = [(o // 9 - 1, o // 3 % 3 - 1, o % 3 - 1) for o in range(27) if o != 13]
    shifts.sort(key=lambda s: sum(map(abs, s)))
    arrive = meet([place_of(s) for s in shifts])
    held = owner.shape[1]
    info[...] = jnp.full(info.shape, -1, jnp.int32)
    info[0:1, 0:held] = owner[...]
    info[1:2, 0:held] = clump[...]
    keys = info[0:1, :] * OWN + info[1:2, :]
    keys = jnp.broadcast_to(keys.astype(jnp.float32), (8, 128))
    for g in range(frag.shape[0] // 8):
        rows = pl.ds(8 * g, 8)
        for k in range(7):
            own[pl.ds(64 * g + k, 8, stride=8), :] = state[k, rows, :]
        own[pl.ds(64 * g + 7, 8, stride=8), :] = lane_take(keys, frag[rows, :])
    arrive()
    cells = own.reshape(sizes + (8, 128))
    copies = []
    for n, shift in enumerate(shifts):
        source = [pl.ds(0, size) if s == 0 else pl.ds(size - 1 if s > 0 else 0, 1) for s, size in zip(shift, sizes)]
        target = [pl.ds(1, size) if s == 0 else pl.ds(0 if s > 0 else size + 1, 1) for s, size in zip(shift, sizes)]
        copies.append(
            pltpu.make_async_remote_copy(
                src_ref=cells.at[tuple(source)],
                dst_ref=out.at[tuple(target)],
                send_sem=send.at[n],
                recv_sem=recv.at[n],
                device_id=place_of(shift),
                device_id_type=MESH,
            )
        )
        copies[-1].start()
    inner = pltpu.make_async_copy(cells, out.at[tuple(pl.ds(1, size) for size in sizes)], near)
    inner.start()
    for copy in copies:
        copy.wait()
    inner.wait()


def exchange_kernel(
    info, sums, motion, mass, moment, table, clump_next,
    outbox, got_z, got_y, inbox, reply, back_x, back_y, answer, send, recv, near,
):
    axes = ("gz", "gy", "gx")
    me = {axis: lax.axis_index(axis) for axis in axes}
    size = {axis: lax.axis_size(axis) for axis in axes}
    peers = {
        axis: [lax.rem(me[axis] + d, size[axis]) for d in range(1, size[axis])] for axis in axes
    }

    def device(axis, index):
        return tuple(index if a == axis else me[a] for a in ("gx", "gy", "gz"))

    arrive = meet([device(axis, p) for axis in axes for p in peers[axis]])

    def stage(number, axis, source, target):
        copies = [pltpu.make_async_copy(source(me[axis]), target(me[axis]), near.at[number])]
        copies[0].start()
        for n, peer in enumerate(peers[axis]):
            copies.append(
                pltpu.make_async_remote_copy(
                    src_ref=source(peer),
                    dst_ref=target(me[axis]),
                    send_sem=send.at[number, n],
                    recv_sem=recv.at[number, n],
                    device_id=device(axis, peer),
                    device_id_type=MESH,
                )
            )
            copies[-1].start()
        for copy in copies:
            copy.wait()

    exact = dict(precision=lax.Precision.HIGHEST, preferred_element_type=jnp.float32)
    owner = info[0:1, :]
    place = (owner & 7) * 16 + ((owner >> 3) & 3) * 4 + (owner >> 5)
    place = jnp.where(owner >= 0, place, -1)
    row = lax.broadcasted_iota(jnp.int32, (128, 128), 0)
    col = lax.broadcasted_iota(jnp.int32, (128, 128), 1)
    hit = (row == place).astype(jnp.float32)
    earlier = jnp.dot(
        hit.astype(jnp.bfloat16), (row < col).astype(jnp.float32).astype(jnp.bfloat16),
        preferred_element_type=jnp.float32,
    )
    slots = [jnp.where(earlier == float(e), hit, 0.0) for e in range(CAP)]
    across = (((1,), (1,)), ((), ()))
    filler = jnp.zeros((112, 128), jnp.float32)
    empty = jnp.zeros((8, 128), jnp.float32)
    sub = lax.broadcasted_iota(jnp.int32, (8, 128), 0)
    label = (info[1:2, :] + 1).astype(jnp.float32)
    payload = jnp.where(sub == 6, label, jnp.where(sub == 7, 0.0, sums[...]))
    outbox[...] = (
        lax.dot_general(slots[0], jnp.concatenate([payload, empty, filler], axis=0), across, **exact)
        + lax.dot_general(slots[1], jnp.concatenate([empty, payload, filler], axis=0), across, **exact)
    ).reshape(outbox.shape)
    arrive()
    stage(0, "gz", lambda p: outbox.at[p], lambda p: got_z.at[:, p])
    by_y = got_z.reshape(4, 4, 8, 128)
    stage(1, "gy", lambda p: by_y.at[p], lambda p: got_y.at[:, p])
    stage(2, "gx", lambda p: got_y.at[p], lambda p: inbox.at[p])

    flat = inbox[...].reshape(128, 128)
    turned = flat.T
    names = lax.broadcasted_iota(jnp.int32, (128, motion.shape[1]), 1).astype(jnp.float32) + 1.0
    which = [(jnp.broadcast_to(flat[:, 8 * e + 6 : 8 * e + 7], names.shape) == names).astype(jnp.float32) for e in range(CAP)]
    total = jnp.dot(turned[0:8], which[0], **exact) + jnp.dot(turned[8:16], which[1], **exact)
    lower = lax.broadcasted_iota(jnp.int32, (3, motion.shape[1]), 0)
    pull = jnp.where(lower == 2, gravity, 0.0)
    velocity = motion[0:3, :] + time_step * (total[0:3] * mass[...] - pull)
    spin = motion[3:6, :] + time_step * total[3:6] * moment[...]
    clump_next[0:3, :] = velocity
    clump_next[3:6, :] = spin
    moved = jnp.concatenate([velocity, spin, jnp.zeros((2, motion.shape[1]), jnp.float32)], axis=0)
    blank = jnp.zeros((8, motion.shape[1]), jnp.float32)
    rest = jnp.zeros((112, motion.shape[1]), jnp.float32)
    reply[...] = (
        lax.dot_general(which[0], jnp.concatenate([moved, blank, rest], axis=0), across, **exact)
        + lax.dot_general(which[1], jnp.concatenate([blank, moved, rest], axis=0), across, **exact)
    ).reshape(reply.shape)
    stage(3, "gx", lambda p: reply.at[p], lambda p: back_x.at[p])
    stage(4, "gy", lambda p: back_x.at[:, p], lambda p: back_y.at[p])
    by_z = back_y.reshape(16, 8, 128)
    stage(5, "gz", lambda p: by_z.at[:, p], lambda p: answer.at[p])
    turned = answer[...].reshape(128, 128).T
    table[...] = jnp.dot(turned[0:8], slots[0], **exact) + jnp.dot(turned[8:16], slots[1], **exact)


def tiles_kernel(
    codes, cells, arms, frag, out, cand, mask, counts, where_v, where_s, place_v, place_s, own_v, wide_v, lens_v, lens_s, items,
    carry, lists, shifts, wide_a, wide_b, push_x, push_y, push_z, loads, sems,
):
    pushes = (push_x, push_y, push_z)
    lines = codes.shape[0]
    tiles = lines * 128
    pad = cells.shape[0] // 8
    ny, nz = 6, 18
    owned = 256
    depth = lists.shape[0] // (8 * owned)
    sub = lax.broadcasted_iota(jnp.int32, (8, 128), 0)
    lane = lax.broadcasted_iota(jnp.int32, (8, 128), 1)

    code = codes[...]
    own_of = (code * 38837) >> 20
    way = code - 27 * own_of
    step_x = ((way * 57) >> 9) - 1
    left = way - 9 * (step_x + 1)
    step_y = ((left * 11) >> 5) - 1
    step_z = left - 3 * (step_y + 1) - 1
    cell_of = ((own_of >> 6) + 1 + step_x) * (ny * nz) + (((own_of >> 4) & 3) + 1 + step_y) * nz
    cell_of = cell_of + (own_of & 15) + 1 + step_z
    for k, value in enumerate((cell_of, cell_of * 8, way, way * 8)):
        where_v[k * lines : (k + 1) * lines, :] = value
    own_v[...] = own_of
    first_copy = pltpu.make_async_copy(where_v, where_s, sems.at[0])
    first_copy.start()

    def reach_bits(g):
        base = pl.multiple_of(g * 64, 64)
        pos = [cells[pl.ds(base + k, 8, stride=8), :] for k in range(3)]
        reach = cells[pl.ds(base + 6, 8, stride=8), :] + REACH
        reach = reach * reach
        near = [p * p for p in pos]
        far = [(1.0 - p) * (1.0 - p) for p in pos]
        bits = jnp.full((8, 128), 1 << 13, jnp.int32)
        for o in range(27):
            steps = (o // 9 - 1, o // 3 % 3 - 1, o % 3 - 1)
            terms = [near[k] if s > 0 else far[k] for k, s in enumerate(steps) if s]
            if not terms:
                continue
            bits = bits | jnp.where(sum(terms[1:], terms[0]) <= reach, 1 << o, 0)
        cand[pl.ds(pl.multiple_of(g * 8, 8), 8), :] = bits

    @pl.loop(0, pad // 24)
    def _(g):
        for u in range(3):
            reach_bits(3 * g + u)

    @pl.loop(0, 27)
    def _(o):
        step_x = ((o * 57) >> 9) - 1
        left = o - 9 * (step_x + 1)
        step_y = ((left * 11) >> 5) - 1
        step_z = left - 3 * (step_y + 1) - 1
        value = jnp.where(sub == 0, step_x, jnp.where(sub == 1, step_y, jnp.where(sub == 2, step_z, 0)))
        shifts[pl.ds(pl.multiple_of(o * 8, 8), 8), :] = value.astype(jnp.float32)

    @pl.loop(0, owned // 16)
    def _(b):
        rows = pl.ds(pl.multiple_of(b * 128, 128), 128)
        for push in pushes:
            push[rows, :] = jnp.zeros((128, 128), jnp.float32)

    first_copy.wait()

    @pl.loop(0, lines)
    def _(b):
        for u in range(128):
            row = cand[pl.ds(where_s[b, u], 1), :]
            mask[pl.ds(b * 128 + u, 1), :] = (row >> where_s[2 * lines + b, u]) & 1

    row = lax.broadcasted_iota(jnp.int32, (128, 128), 0)
    col = lax.broadcasted_iota(jnp.int32, (128, 128), 1)
    before = (row < col).astype(jnp.bfloat16)
    ones = jnp.ones((8, 128), jnp.bfloat16)

    @pl.loop(0, lines)
    def _(b):
        rows = pl.ds(pl.multiple_of(b * 128, 128), 128)
        active = mask[rows, :]
        flags = active.astype(jnp.float32).astype(jnp.bfloat16)
        rank = jnp.dot(flags, before, preferred_element_type=jnp.float32).astype(jnp.int32)
        number = lax.dot_general(ones, flags, (((1,), (1,)), ((), ())), preferred_element_type=jnp.float32)
        counts[pl.ds(b, 1), :] = number[0:1]
        value = jnp.where(active > 0, ((col - rank) << 7) | col, 0)
        for bit in range(7):
            moved = pltpu.roll(value, 128 - (1 << bit), axis=1)
            flag = 1 << (7 + bit)
            value = jnp.where((moved & flag) != 0, moved, jnp.where((value & flag) != 0, 0, value))
        mask[rows, :] = value & 127

    both = jnp.concatenate([before, jnp.ones((128, 128), jnp.bfloat16)], axis=1)
    cell_id = lax.broadcasted_iota(jnp.int32, (owned, 128), 0)
    carry[...] = jnp.zeros((owned, 128), jnp.float32)

    @pl.loop(0, lines)
    def _(b):
        mine = own_v[pl.ds(b, 1), :]
        hot = cell_id == mine
        amount = jnp.where(hot, counts[pl.ds(b, 1), :], 0.0)
        summed = jnp.dot(amount.astype(jnp.bfloat16), both, preferred_element_type=jnp.float32)
        so_far = carry[...]
        at = jnp.sum(jnp.where(hot, summed[:, 0:128] + so_far, 0.0), axis=0, keepdims=True)
        carry[...] = so_far + summed[:, 128:256]
        spot = mine * (depth * 128) + at.astype(jnp.int32)
        place_v[pl.ds(b, 1), :] = (spot >> 7) << 3
        place_v[pl.ds(lines + b, 1), :] = spot & 127

    length = carry[...].astype(jnp.int32)
    cell_lane = lax.broadcasted_iota(jnp.int32, (owned, 128), 1)
    words = (
        cell_id * (depth * 8) + ((length >> 7) << 3),
        length & 127,
        jnp.minimum((length + 63) >> 6, QUICK),
        (cell_id << 16) + cell_id * (2 * depth),
        length,
        jnp.broadcast_to(jnp.max(length, axis=0, keepdims=True), (owned, 128)),
    )
    packed = words[0]
    for k, word in enumerate(words[1:]):
        packed = jnp.where((cell_lane & 15) == k + 1, word, packed)
    wide_v[...] = packed
    eight = lax.broadcasted_iota(jnp.int32, (owned // 8, 128), 1) >> 4
    folded = wide_v[pl.ds(0, owned // 8, stride=8), :]
    for u in range(1, 8):
        folded = jnp.where(eight == u, wide_v[pl.ds(u, owned // 8, stride=8), :], folded)
    lens_v[...] = folded
    copies = [
        pltpu.make_async_copy(place_v, place_s, sems.at[1]),
        pltpu.make_async_copy(lens_v, lens_s, sems.at[2]),
    ]
    for copy in copies:
        copy.start()
    for copy in copies:
        copy.wait()

    def append(sorted_rows, to, turn):
        to = pl.multiple_of(to, 8)
        turned = pltpu.roll(sorted_rows, turn, axis=1)
        pltpu.store(lists.at[pl.ds(to, 8), :], turned, mask=lane >= turn)
        lists[pl.ds(to + 8, 8), :] = turned

    @pl.loop(0, lines)
    def _(b):
        for u in range(128):
            values = cells[pl.ds(pl.multiple_of(where_s[lines + b, u], 8), 8), :]
            index = jnp.broadcast_to(mask[pl.ds(b * 128 + u, 1), :], (8, 128))
            shift = shifts[pl.ds(pl.multiple_of(where_s[3 * lines + b, u], 8), 8), :]
            append(lane_take(values, index) + shift, place_s[b, u], place_s[lines + b, u])

    dummy = jnp.where(sub < 3, 1000.0, 0.1)

    def close(b, total):
        for u in range(8):
            append(dummy, lens_s[b, 16 * u], lens_s[b, 16 * u + 1])
            first = lens_s[b, 16 * u + 3]
            for k in range(QUICK):
                items[total + k] = first + k
            total = total + lens_s[b, 16 * u + 2]
        return total

    number = lax.fori_loop(0, owned // 8, close, 0)

    def longer(c, total):
        line, at = c >> 3, (c & 7) * 16

        def add(k, total):
            items[total] = lens_s[line, at + 3] + k
            return total + 1

        return lax.fori_loop(QUICK, (lens_s[line, at + 4] + 63) >> 6, add, total)

    number = lax.fori_loop(0, jnp.where(lens_s[0, 5] > 64 * QUICK, owned, 0), longer, number)
    for k in range(3 * GROUP):
        items[number + k] = owned << 16

    which_row = lax.broadcasted_iota(jnp.int32, (24, 1024), 0)
    which_col = lax.broadcasted_iota(jnp.int32, (24, 1024), 1)
    pick = ((which_row & 7) == (which_col >> 7)).astype(jnp.float32).astype(jnp.bfloat16)

    def spread(words, wide):
        splits = []
        for word in words:
            spot = word & 0xFFFF
            values = lists[pl.ds(pl.multiple_of((spot >> 1) * 8, 8), 8), :]
            values = pltpu.roll(values, (spot & 1) * 64, axis=1)
            high = values.astype(jnp.bfloat16).astype(jnp.float32)
            rest = values - high
            mid = rest.astype(jnp.bfloat16).astype(jnp.float32)
            split = jnp.concatenate([high, mid, rest - mid], axis=0)
            splits.append(split.T[0:64])
        split = jnp.concatenate(splits, axis=0).astype(jnp.bfloat16)
        spreads = jnp.dot(split, pick, preferred_element_type=jnp.float32)
        for u in range(8 * len(words)):
            for k in range(8):
                wide[8 * u + k] = spreads[8 * u : 8 * u + 8, 128 * k : 128 * k + 128]

    def press(word, wide, first):
        c = word >> 16
        base = ((c >> 6) + 1) * (ny * nz) + (((c >> 4) & 3) + 1) * nz + (c & 15) + 1
        own = [jnp.broadcast_to(cells[pl.ds(base * 8 + k, 1), :], (8, 128)) for k in range(8)]
        total = [None] * 3
        for u in range(8):
            other = [wide[8 * (first + u) + k] for k in range(8)]
            apart = [other[k] - own[k] for k in range(3)]
            square = apart[0] * apart[0] + apart[1] * apart[1] + apart[2] * apart[2] + epsilon_sq
            inverse = lax.rsqrt(square)
            reach = own[6] + other[6]
            depth_in = jnp.where(own[7] != other[7], jnp.maximum(reach - square * inverse, 0.0), 0.0)
            closing = (
                (other[3] - own[3]) * apart[0] + (other[4] - own[4]) * apart[1] + (other[5] - own[5]) * apart[2]
            )
            along = closing * inverse - 50.0 * depth_in
            area = own[6] * other[6] * depth_in
            factor = area * lax.rsqrt(jnp.maximum(area * reach, 1e-20)) * along * inverse
            for k in range(3):
                term = factor * apart[k]
                total[k] = term if u == 0 else total[k] + term
        rows = pl.ds(pl.multiple_of(c * 8, 8), 8)
        for k in range(3):
            pushes[k][rows, :] += total[k]

    def group(n):
        return [items[n * GROUP + k] for k in range(GROUP)]

    spread(group(0), wide_a)

    @pl.loop(0, (number + (2 * GROUP - 1)) // (2 * GROUP))
    def _(p):
        def half(n, now, later):
            spread(group(n + 1), later)
            for k, word in enumerate(group(n)):
                press(word, now, 8 * k)

        half(2 * p, wide_a, wide_b)
        half(2 * p + 1, wide_b, wide_a)

    ids = lax.broadcasted_iota(jnp.int32, (128, 128), 0)

    def gather(g, total):
        rows = pl.ds(pl.multiple_of(g * 8, 8), 8)
        force = []
        for push in pushes:
            parts = [push[pl.ds(g * 64 + s, 8, stride=8), :] for s in range(8)]
            while len(parts) > 1:
                parts = [parts[i] + parts[i + 1] for i in range(0, len(parts), 2)]
            force.append(2.0 * parts[0])
        turn = cross_rows([arms[k, rows, :] for k in range(3)], force)
        zero = jnp.zeros((8, 128), jnp.float32)
        for k, value in enumerate(force + turn + [zero, zero]):
            loads[pl.ds(k, 8, stride=8), :] = value
        wide = jnp.concatenate([loads[pl.ds(8 * c, 8), :] for c in range(8)], axis=1)
        high = wide.astype(jnp.bfloat16).astype(jnp.float32)
        rest = wide - high
        mid = rest.astype(jnp.bfloat16).astype(jnp.float32)
        split = jnp.concatenate([high, mid, rest - mid], axis=0).astype(jnp.bfloat16)
        which = jnp.concatenate(
            [(ids == frag[pl.ds(g * 8 + c, 1), :]).astype(jnp.float32) for c in range(8)], axis=1
        ).astype(jnp.bfloat16)
        return total + lax.dot_general(split, which, (((1,), (1,)), ((), ())), preferred_element_type=jnp.float32)

    total = lax.fori_loop(0, owned // 8, gather, jnp.zeros((24, 128), jnp.float32))
    out[...] = total[0:8] + total[8:16] + total[16:24]


def move_kernel(state, arms, frag, table, clump_next, out, clump_out):
    clump_out[...] = clump_next[...]
    rows_of = [jnp.broadcast_to(table[k : k + 1, :], (8, 128)) for k in range(6)]
    for g in range(frag.shape[0] // 8):
        rows = pl.ds(8 * g, 8)
        index = frag[rows, :]
        motion = [lane_take(r, index) for r in rows_of]
        velocity, spin = motion[0:3], motion[3:6]
        lever = [arms[k, rows, :] for k in range(3)]
        half = [0.5 * time_step * w for w in spin]
        turned = cross_rows(half, lever)
        twice = cross_rows(half, turned)
        scale = 2.0 / (1.0 + half[0] * half[0] + half[1] * half[1] + half[2] * half[2])
        moved = [lever[k] + scale * (turned[k] + twice[k]) for k in range(3)]
        swing = cross_rows(spin, moved)
        for k in range(3):
            out[k, rows, :] = state[k, rows, :] + time_step * velocity[k] + (moved[k] - lever[k])
            out[3 + k, rows, :] = velocity[k] + swing[k]


def halo(state, frag, owner, clump, cells):
    return pl.pallas_call(
        halo_kernel,
        in_specs=[VMEM] * 4,
        out_specs=(HBM, VMEM),
        out_shape=(
            jax.ShapeDtypeStruct(tuple(c + 2 for c in cells) + (8, 128), jnp.float32),
            jax.ShapeDtypeStruct((2, 128), jnp.int32),
        ),
        scratch_shapes=[
            pltpu.VMEM((8 * frag.shape[0], 128), jnp.float32),
            pltpu.SemaphoreType.DMA((26,)),
            pltpu.SemaphoreType.DMA((26,)),
            pltpu.SemaphoreType.DMA,
        ],
        compiler_params=pltpu.CompilerParams(collective_id=0, has_side_effects=True),
        name="halo",
    )(state, frag, owner, clump)


def exchange(info, sums, motion, mass, moment):
    block = lambda *shape: pltpu.VMEM(shape + (128,), jnp.float32)
    return pl.pallas_call(
        exchange_kernel,
        in_specs=[VMEM] * 5,
        out_specs=(VMEM, VMEM),
        out_shape=(
            jax.ShapeDtypeStruct((8, 128), jnp.float32),
            jax.ShapeDtypeStruct(motion.shape, jnp.float32),
        ),
        scratch_shapes=[
            block(8, 16),
            block(16, 8),
            block(4, 4, 8),
            block(4, 4, 8),
            block(4, 4, 8),
            block(4, 4, 8),
            block(4, 4, 8),
            block(8, 16),
            pltpu.SemaphoreType.DMA((6, 7)),
            pltpu.SemaphoreType.DMA((6, 7)),
            pltpu.SemaphoreType.DMA((6,)),
        ],
        compiler_params=pltpu.CompilerParams(collective_id=1, has_side_effects=True),
        name="exchange",
    )(info, sums, motion, mass, moment)


def forces(codes, cells, arms, frag):
    lines = codes.shape[0] // 128
    owned, depth = frag.shape[0], 29
    return pl.pallas_call(
        tiles_kernel,
        in_specs=[VMEM, VMEM, VMEM, VMEM],
        out_specs=VMEM,
        out_shape=jax.ShapeDtypeStruct((8, 128), jnp.float32),
        scratch_shapes=[
            pltpu.VMEM((cells.shape[0] // 8, 128), jnp.int32),
            pltpu.VMEM((lines * 128, 128), jnp.int32),
            pltpu.VMEM((lines, 128), jnp.float32),
            pltpu.VMEM((4 * lines, 128), jnp.int32),
            pltpu.SMEM((4 * lines, 128), jnp.int32),
            pltpu.VMEM((2 * lines, 128), jnp.int32),
            pltpu.SMEM((2 * lines, 128), jnp.int32),
            pltpu.VMEM((lines, 128), jnp.int32),
            pltpu.VMEM((owned, 128), jnp.int32),
            pltpu.VMEM((owned // 8, 128), jnp.int32),
            pltpu.SMEM((owned // 8, 128), jnp.int32),
            pltpu.SMEM((owned * 54 + 32,), jnp.int32),
            pltpu.VMEM((owned, 128), jnp.float32),
            pltpu.VMEM((owned * depth * 8, 128), jnp.float32),
            pltpu.VMEM((27 * 8, 128), jnp.float32),
            pltpu.VMEM((64 * GROUP, 8, 128), jnp.float32),
            pltpu.VMEM((64 * GROUP, 8, 128), jnp.float32),
            pltpu.VMEM((owned * 8 + 8, 128), jnp.float32),
            pltpu.VMEM((owned * 8 + 8, 128), jnp.float32),
            pltpu.VMEM((owned * 8 + 8, 128), jnp.float32),
            pltpu.VMEM((64, 128), jnp.float32),
            pltpu.SemaphoreType.DMA((3,)),
        ],
        compiler_params=pltpu.CompilerParams(vmem_limit_bytes=60 * 1024 * 1024),
        name="forces",
    )(codes.reshape(lines, 128), cells, arms, frag)


def move(state, arms, frag, table, clump_next):
    n = frag.shape[0]
    part = n // 4
    return pl.pallas_call(
        move_kernel,
        grid=(4,),
        in_specs=[
            pl.BlockSpec((3, part, 128), lambda i: (0, i, 0)),
            pl.BlockSpec((3, part, 128), lambda i: (0, i, 0)),
            pl.BlockSpec((part, 128), lambda i: (i, 0)),
            pl.BlockSpec((8, 128), lambda i: (0, 0)),
            pl.BlockSpec(clump_next.shape, lambda i: (0, 0)),
        ],
        out_specs=(
            pl.BlockSpec((6, part, 128), lambda i: (0, i, 0)),
            pl.BlockSpec(clump_next.shape, lambda i: (0, 0)),
        ),
        out_shape=(
            jax.ShapeDtypeStruct((6, n, 128), jnp.float32),
            jax.ShapeDtypeStruct(clump_next.shape, jnp.float32),
        ),
        name="move",
    )(state, arms, frag, table, clump_next)


def local(state, arms, sphere_frag, frag_owner, frag_clump, tiles, clump_motion, inv_mass, inv_moment):
    cells = state.shape[1:4]
    slots = state.shape[4]
    count = cells[0] * cells[1] * cells[2]
    held = frag_clump.shape[0]
    frag = sphere_frag.reshape(count, slots)
    padded, info = halo(state.reshape(7, count, slots), frag, frag_owner.reshape(1, held), frag_clump[None], cells)
    sums = forces(tiles[0], padded.reshape(-1, slots), arms.reshape(3, count, slots), frag)
    table, clump_next = exchange(info, sums, clump_motion, inv_mass[None], inv_moment[None])
    sphere_next, clump_next = move(
        state.reshape(7, count, slots), arms.reshape(3, count, slots), frag, table, clump_next
    )
    return sphere_next.reshape((6,) + cells + (slots,)), clump_next


def solution(mesh):
    return jax.shard_map(
        local,
        mesh=mesh,
        in_specs=(
            P(None, "gx", "gy", "gz", None),
            P(None, "gx", "gy", "gz", None),
            P("gx", "gy", "gz", None),
            P(("gx", "gy", "gz"), None),
            P(("gx", "gy", "gz")),
            P(("gx", "gy", "gz"), None),
            P(None, ("gx", "gy", "gz")),
            P(("gx", "gy", "gz")),
            P(("gx", "gy", "gz")),
        ),
        out_specs=(P(None, "gx", "gy", "gz", None), P(None, ("gx", "gy", "gz"))),
        check_vma=False,
    )
```

```python
import functools

import jax
import jax.numpy as jnp
from jax import lax
from jax.experimental import pallas as pl
from jax.experimental.pallas import tpu as pltpu
from jax.sharding import PartitionSpec as P

CAP = 2
OWN = 48
QUICK = 8
GROUP = 16
BURST = 4
REACH = 0.14001
time_step = 0.01
gravity = 9.81
epsilon_sq = 1e-08
VMEM = pl.BlockSpec(memory_space=pltpu.VMEM)


def lane_take(rows, index):
    return jnp.take_along_axis(rows, index, axis=1, mode="promise_in_bounds")


def cross_rows(first, second):
    return [
        first[1] * second[2] - first[2] * second[1],
        first[2] * second[0] - first[0] * second[2],
        first[0] * second[1] - first[1] * second[0],
    ]


MESH = pl.DeviceIdType.MESH
HBM = pl.BlockSpec(memory_space=pl.ANY)


def place_of(shift):
    return tuple(
        lax.rem(lax.axis_index(axis) + step + lax.axis_size(axis), lax.axis_size(axis))
        for axis, step in zip(("gx", "gy", "gz"), shift)
    )


def meet(others):
    barrier = pltpu.get_barrier_semaphore()
    for other in others:
        pl.semaphore_signal(barrier, inc=1, device_id=other, device_id_type=MESH)
    return lambda: pl.semaphore_wait(barrier, len(others))


def halo_kernel(state, frag, owner, clump, out, info, own, send, recv, near):
    sizes = out.shape[0] - 2, out.shape[1] - 2, out.shape[2] - 2
    shifts = [(o // 9 - 1, o // 3 % 3 - 1, o % 3 - 1) for o in range(27) if o != 13]
    shifts.sort(key=lambda s: sum(map(abs, s)))
    arrive = meet([place_of(s) for s in shifts])
    held = owner.shape[1]
    info[...] = jnp.full(info.shape, -1, jnp.int32)
    info[0:1, 0:held] = owner[...]
    info[1:2, 0:held] = clump[...]
    keys = info[0:1, :] * OWN + info[1:2, :]
    keys = jnp.broadcast_to(keys.astype(jnp.float32), (8, 128))
    for g in range(frag.shape[0] // 8):
        rows = pl.ds(8 * g, 8)
        for k in range(7):
            own[pl.ds(64 * g + k, 8, stride=8), :] = state[k, rows, :]
        own[pl.ds(64 * g + 7, 8, stride=8), :] = lane_take(keys, frag[rows, :])
    arrive()
    cells = own.reshape(sizes + (8, 128))
    copies = []
    for n, shift in enumerate(shifts):
        source = [pl.ds(0, size) if s == 0 else pl.ds(size - 1 if s > 0 else 0, 1) for s, size in zip(shift, sizes)]
        target = [pl.ds(1, size) if s == 0 else pl.ds(0 if s > 0 else size + 1, 1) for s, size in zip(shift, sizes)]
        copies.append(
            pltpu.make_async_remote_copy(
                src_ref=cells.at[tuple(source)],
                dst_ref=out.at[tuple(target)],
                send_sem=send.at[n],
                recv_sem=recv.at[n],
                device_id=place_of(shift),
                device_id_type=MESH,
            )
        )
        copies[-1].start()
    inner = pltpu.make_async_copy(cells, out.at[tuple(pl.ds(1, size) for size in sizes)], near)
    inner.start()
    for copy in copies:
        copy.wait()
    inner.wait()


def exchange_kernel(
    info, sums, motion, mass, moment, table, clump_next,
    outbox, got_z, got_y, inbox, reply, back_x, back_y, answer, send, recv, near,
):
    axes = ("gz", "gy", "gx")
    me = {axis: lax.axis_index(axis) for axis in axes}
    size = {axis: lax.axis_size(axis) for axis in axes}
    peers = {
        axis: [lax.rem(me[axis] + d, size[axis]) for d in range(1, size[axis])] for axis in axes
    }

    def device(axis, index):
        return tuple(index if a == axis else me[a] for a in ("gx", "gy", "gz"))

    arrive = meet([device(axis, p) for axis in axes for p in peers[axis]])

    def stage(number, axis, source, target):
        copies = [pltpu.make_async_copy(source(me[axis]), target(me[axis]), near.at[number])]
        copies[0].start()
        for n, peer in enumerate(peers[axis]):
            copies.append(
                pltpu.make_async_remote_copy(
                    src_ref=source(peer),
                    dst_ref=target(me[axis]),
                    send_sem=send.at[number, n],
                    recv_sem=recv.at[number, n],
                    device_id=device(axis, peer),
                    device_id_type=MESH,
                )
            )
            copies[-1].start()
        for copy in copies:
            copy.wait()

    exact = dict(precision=lax.Precision.HIGHEST, preferred_element_type=jnp.float32)
    owner = info[0:1, :]
    place = (owner & 7) * 16 + ((owner >> 3) & 3) * 4 + (owner >> 5)
    place = jnp.where(owner >= 0, place, -1)
    row = lax.broadcasted_iota(jnp.int32, (128, 128), 0)
    col = lax.broadcasted_iota(jnp.int32, (128, 128), 1)
    hit = (row == place).astype(jnp.float32)
    earlier = jnp.dot(
        hit.astype(jnp.bfloat16), (row < col).astype(jnp.float32).astype(jnp.bfloat16),
        preferred_element_type=jnp.float32,
    )
    slots = [jnp.where(earlier == float(e), hit, 0.0) for e in range(CAP)]
    across = (((1,), (1,)), ((), ()))
    filler = jnp.zeros((112, 128), jnp.float32)
    empty = jnp.zeros((8, 128), jnp.float32)
    sub = lax.broadcasted_iota(jnp.int32, (8, 128), 0)
    label = (info[1:2, :] + 1).astype(jnp.float32)
    payload = jnp.where(sub == 6, label, jnp.where(sub == 7, 0.0, sums[...]))
    outbox[...] = (
        lax.dot_general(slots[0], jnp.concatenate([payload, empty, filler], axis=0), across, **exact)
        + lax.dot_general(slots[1], jnp.concatenate([empty, payload, filler], axis=0), across, **exact)
    ).reshape(outbox.shape)
    arrive()
    stage(0, "gz", lambda p: outbox.at[p], lambda p: got_z.at[:, p])
    by_y = got_z.reshape(4, 4, 8, 128)
    stage(1, "gy", lambda p: by_y.at[p], lambda p: got_y.at[:, p])
    stage(2, "gx", lambda p: got_y.at[p], lambda p: inbox.at[p])

    flat = inbox[...].reshape(128, 128)
    turned = flat.T
    names = lax.broadcasted_iota(jnp.int32, (128, motion.shape[1]), 1).astype(jnp.float32) + 1.0
    which = [(jnp.broadcast_to(flat[:, 8 * e + 6 : 8 * e + 7], names.shape) == names).astype(jnp.float32) for e in range(CAP)]
    total = jnp.dot(turned[0:8], which[0], **exact) + jnp.dot(turned[8:16], which[1], **exact)
    lower = lax.broadcasted_iota(jnp.int32, (3, motion.shape[1]), 0)
    pull = jnp.where(lower == 2, gravity, 0.0)
    velocity = motion[0:3, :] + time_step * (total[0:3] * mass[...] - pull)
    spin = motion[3:6, :] + time_step * total[3:6] * moment[...]
    clump_next[0:3, :] = velocity
    clump_next[3:6, :] = spin
    moved = jnp.concatenate([velocity, spin, jnp.zeros((2, motion.shape[1]), jnp.float32)], axis=0)
    blank = jnp.zeros((8, motion.shape[1]), jnp.float32)
    rest = jnp.zeros((112, motion.shape[1]), jnp.float32)
    reply[...] = (
        lax.dot_general(which[0], jnp.concatenate([moved, blank, rest], axis=0), across, **exact)
        + lax.dot_general(which[1], jnp.concatenate([blank, moved, rest], axis=0), across, **exact)
    ).reshape(reply.shape)
    stage(3, "gx", lambda p: reply.at[p], lambda p: back_x.at[p])
    stage(4, "gy", lambda p: back_x.at[:, p], lambda p: back_y.at[p])
    by_z = back_y.reshape(16, 8, 128)
    stage(5, "gz", lambda p: by_z.at[:, p], lambda p: answer.at[p])
    turned = answer[...].reshape(128, 128).T
    table[...] = jnp.dot(turned[0:8], slots[0], **exact) + jnp.dot(turned[8:16], slots[1], **exact)


def tiles_kernel(
    codes, cells, arms, frag, out, cand, mask, counts, where_v, where_s, place_v, place_s, own_v, wide_v, lens_v, lens_s, items,
    carry, lists, shifts, wide_a, wide_b, push_x, push_y, push_z, loads, sems,
):
    pushes = (push_x, push_y, push_z)
    lines = codes.shape[0]
    tiles = lines * 128
    pad = cells.shape[0] // 8
    ny, nz = 6, 18
    owned = 256
    depth = lists.shape[0] // (8 * owned)
    sub = lax.broadcasted_iota(jnp.int32, (8, 128), 0)
    lane = lax.broadcasted_iota(jnp.int32, (8, 128), 1)

    code = codes[...]
    own_of = (code * 38837) >> 20
    way = code - 27 * own_of
    step_x = ((way * 57) >> 9) - 1
    left = way - 9 * (step_x + 1)
    step_y = ((left * 11) >> 5) - 1
    step_z = left - 3 * (step_y + 1) - 1
    cell_of = ((own_of >> 6) + 1 + step_x) * (ny * nz) + (((own_of >> 4) & 3) + 1 + step_y) * nz
    cell_of = cell_of + (own_of & 15) + 1 + step_z
    for k, value in enumerate((cell_of, cell_of * 8, way, way * 8)):
        where_v[k * lines : (k + 1) * lines, :] = value
    own_v[...] = own_of
    first_copy = pltpu.make_async_copy(where_v, where_s, sems.at[0])
    first_copy.start()

    def reach_bits(g):
        base = pl.multiple_of(g * 64, 64)
        pos = [cells[pl.ds(base + k, 8, stride=8), :] for k in range(3)]
        reach = cells[pl.ds(base + 6, 8, stride=8), :] + REACH
        reach = reach * reach
        near = [p * p for p in pos]
        far = [(1.0 - p) * (1.0 - p) for p in pos]
        bits = jnp.full((8, 128), 1 << 13, jnp.int32)
        for o in range(27):
            steps = (o // 9 - 1, o // 3 % 3 - 1, o % 3 - 1)
            terms = [near[k] if s > 0 else far[k] for k, s in enumerate(steps) if s]
            if not terms:
                continue
            bits = bits | jnp.where(sum(terms[1:], terms[0]) <= reach, 1 << o, 0)
        cand[pl.ds(pl.multiple_of(g * 8, 8), 8), :] = bits

    @pl.loop(0, pad // 24)
    def _(g):
        for u in range(3):
            reach_bits(3 * g + u)

    @pl.loop(0, 27)
    def _(o):
        step_x = ((o * 57) >> 9) - 1
        left = o - 9 * (step_x + 1)
        step_y = ((left * 11) >> 5) - 1
        step_z = left - 3 * (step_y + 1) - 1
        value = jnp.where(sub == 0, step_x, jnp.where(sub == 1, step_y, jnp.where(sub == 2, step_z, 0)))
        shifts[pl.ds(pl.multiple_of(o * 8, 8), 8), :] = value.astype(jnp.float32)

    @pl.loop(0, owned // 16)
    def _(b):
        first = ((b >> 2) + 1) * (ny * nz) + ((b & 3) + 1) * nz + 1
        rows = pl.ds(pl.multiple_of(first * 8, 8), 128)
        for push in pushes:
            push[rows, :] = jnp.zeros((128, 128), jnp.float32)

    first_copy.wait()

    @pl.loop(0, lines)
    def _(b):
        for u in range(128):
            row = cand[pl.ds(where_s[b, u], 1), :]
            mask[pl.ds(b * 128 + u, 1), :] = (row >> where_s[2 * lines + b, u]) & 1

    row = lax.broadcasted_iota(jnp.int32, (128, 128), 0)
    col = lax.broadcasted_iota(jnp.int32, (128, 128), 1)
    before = (row < col).astype(jnp.bfloat16)
    ones = jnp.ones((8, 128), jnp.bfloat16)

    @pl.loop(0, lines // BURST)
    def _(b):
        rows = pl.ds(pl.multiple_of(b * (128 * BURST), 128 * BURST), 128 * BURST)
        col = lax.broadcasted_iota(jnp.int32, (128 * BURST, 128), 1)
        active = mask[rows, :]
        flags = active.astype(jnp.float32).astype(jnp.bfloat16)
        rank = jnp.dot(flags, before, preferred_element_type=jnp.float32).astype(jnp.int32)
        number = lax.dot_general(ones, flags, (((1,), (1,)), ((), ())), preferred_element_type=jnp.float32)
        for q in range(BURST):
            counts[pl.ds(b * BURST + q, 1), :] = number[0:1, 128 * q : 128 * q + 128]
        value = jnp.where(active > 0, ((col - rank) << 7) | col, 0)
        for bit in range(7):
            moved = pltpu.roll(value, 128 - (1 << bit), axis=1)
            flag = 1 << (7 + bit)
            value = jnp.where((moved & flag) != 0, moved, jnp.where((value & flag) != 0, 0, value))
        mask[rows, :] = value & 127

    both = jnp.concatenate([before, jnp.ones((128, 128), jnp.bfloat16)], axis=1)
    cell_id = lax.broadcasted_iota(jnp.int32, (owned, 128), 0)
    carry[...] = jnp.zeros((owned, 128), jnp.float32)

    @pl.loop(0, lines)
    def _(b):
        mine = own_v[pl.ds(b, 1), :]
        hot = cell_id == mine
        amount = jnp.where(hot, counts[pl.ds(b, 1), :], 0.0)
        summed = jnp.dot(amount.astype(jnp.bfloat16), both, preferred_element_type=jnp.float32)
        so_far = carry[...]
        at = jnp.sum(jnp.where(hot, summed[:, 0:128] + so_far, 0.0), axis=0, keepdims=True)
        carry[...] = so_far + summed[:, 128:256]
        spot = mine * (depth * 128) + at.astype(jnp.int32)
        place_v[pl.ds(b, 1), :] = (spot >> 7) << 3
        place_v[pl.ds(lines + b, 1), :] = spot & 127

    length = carry[...].astype(jnp.int32)
    cell_lane = lax.broadcasted_iota(jnp.int32, (owned, 128), 1)
    padded_id = ((cell_id >> 6) + 1) * (ny * nz) + (((cell_id >> 4) & 3) + 1) * nz + (cell_id & 15) + 1
    words = (
        cell_id * (depth * 8) + ((length >> 7) << 3),
        length & 127,
        jnp.minimum((length + 63) >> 6, QUICK),
        (padded_id << 16) + cell_id * (2 * depth),
        length,
        jnp.broadcast_to(jnp.max(length, axis=0, keepdims=True), (owned, 128)),
    )
    packed = words[0]
    for k, word in enumerate(words[1:]):
        packed = jnp.where((cell_lane & 15) == k + 1, word, packed)
    wide_v[...] = packed
    eight = lax.broadcasted_iota(jnp.int32, (owned // 8, 128), 1) >> 4
    folded = wide_v[pl.ds(0, owned // 8, stride=8), :]
    for u in range(1, 8):
        folded = jnp.where(eight == u, wide_v[pl.ds(u, owned // 8, stride=8), :], folded)
    lens_v[...] = folded
    copies = [
        pltpu.make_async_copy(place_v, place_s, sems.at[1]),
        pltpu.make_async_copy(lens_v, lens_s, sems.at[2]),
    ]
    for copy in copies:
        copy.start()
    for copy in copies:
        copy.wait()

    def append(sorted_rows, to, turn):
        to = pl.multiple_of(to, 8)
        turned = pltpu.roll(sorted_rows, turn, axis=1)
        pltpu.store(lists.at[pl.ds(to, 8), :], turned, mask=lane >= turn)
        lists[pl.ds(to + 8, 8), :] = turned

    @pl.loop(0, lines)
    def _(b):
        for u in range(128):
            values = cells[pl.ds(pl.multiple_of(where_s[lines + b, u], 8), 8), :]
            index = jnp.broadcast_to(mask[pl.ds(b * 128 + u, 1), :], (8, 128))
            shift = shifts[pl.ds(pl.multiple_of(where_s[3 * lines + b, u], 8), 8), :]
            append(lane_take(values, index) + shift, place_s[b, u], place_s[lines + b, u])

    dummy = jnp.where(sub < 3, 1000.0, 0.1)

    def close(b, total):
        for u in range(8):
            append(dummy, lens_s[b, 16 * u], lens_s[b, 16 * u + 1])
            first = lens_s[b, 16 * u + 3]
            for k in range(QUICK):
                items[total + k] = first + k
            total = total + lens_s[b, 16 * u + 2]
        return total

    number = lax.fori_loop(0, owned // 8, close, 0)

    def longer(c, total):
        line, at = c >> 3, (c & 7) * 16

        def add(k, total):
            items[total] = lens_s[line, at + 3] + k
            return total + 1

        return lax.fori_loop(QUICK, (lens_s[line, at + 4] + 63) >> 6, add, total)

    number = lax.fori_loop(0, jnp.where(lens_s[0, 5] > 64 * QUICK, owned, 0), longer, number)
    for k in range(3 * GROUP):
        items[number + k] = 0

    which_row = lax.broadcasted_iota(jnp.int32, (24, 1024), 0)
    which_col = lax.broadcasted_iota(jnp.int32, (24, 1024), 1)
    pick = ((which_row & 7) == (which_col >> 7)).astype(jnp.float32).astype(jnp.bfloat16)

    def spread(words, wide):
        splits = []
        for word in words:
            spot = word & 0xFFFF
            values = lists[pl.ds(pl.multiple_of((spot >> 1) * 8, 8), 8), :]
            values = pltpu.roll(values, (spot & 1) * 64, axis=1)
            high = values.astype(jnp.bfloat16).astype(jnp.float32)
            rest = values - high
            mid = rest.astype(jnp.bfloat16).astype(jnp.float32)
            split = jnp.concatenate([high, mid, rest - mid], axis=0)
            splits.append(split.T[0:64])
        split = jnp.concatenate(splits, axis=0).astype(jnp.bfloat16)
        spreads = jnp.dot(split, pick, preferred_element_type=jnp.float32)
        for u in range(8 * len(words)):
            for k in range(8):
                wide[8 * u + k] = spreads[8 * u : 8 * u + 8, 128 * k : 128 * k + 128]

    def press(word, wide, first):
        base = pl.multiple_of((word >> 16) * 8, 8)
        own = [jnp.broadcast_to(cells[pl.ds(base + k, 1), :], (8, 128)) for k in range(8)]
        total = [None] * 3
        for u in range(8):
            other = [wide[8 * (first + u) + k] for k in range(8)]
            apart = [other[k] - own[k] for k in range(3)]
            square = apart[0] * apart[0] + apart[1] * apart[1] + apart[2] * apart[2] + epsilon_sq
            inverse = lax.rsqrt(square)
            reach = own[6] + other[6]
            depth_in = jnp.where(own[7] != other[7], jnp.maximum(reach - square * inverse, 0.0), 0.0)
            closing = (
                (other[3] - own[3]) * apart[0] + (other[4] - own[4]) * apart[1] + (other[5] - own[5]) * apart[2]
            )
            along = closing * inverse - 50.0 * depth_in
            area = own[6] * other[6] * depth_in
            factor = area * lax.rsqrt(jnp.maximum(area * reach, 1e-20)) * along * inverse
            for k in range(3):
                term = factor * apart[k]
                total[k] = term if u == 0 else total[k] + term
        rows = pl.ds(base, 8)
        for k in range(3):
            pushes[k][rows, :] += total[k]

    def group(n):
        return [items[n * GROUP + k] for k in range(GROUP)]

    spread(group(0), wide_a)

    @pl.loop(0, (number + (2 * GROUP - 1)) // (2 * GROUP))
    def _(p):
        def half(n, now, later):
            spread(group(n + 1), later)
            for k, word in enumerate(group(n)):
                press(word, now, 8 * k)

        half(2 * p, wide_a, wide_b)
        half(2 * p + 1, wide_b, wide_a)

    ids = lax.broadcasted_iota(jnp.int32, (128, 128), 0)

    def operands(g, loads):
        rows = pl.ds(pl.multiple_of(g * 8, 8), 8)
        force = []
        first = (((g >> 3) + 1) * (ny * nz) + (((g >> 1) & 3) + 1) * nz + (g & 1) * 8 + 1) * 8
        for push in pushes:
            parts = [push[pl.ds(first + s, 8, stride=8), :] for s in range(8)]
            while len(parts) > 1:
                parts = [parts[i] + parts[i + 1] for i in range(0, len(parts), 2)]
            force.append(2.0 * parts[0])
        turn = cross_rows([arms[k, rows, :] for k in range(3)], force)
        zero = jnp.zeros((8, 128), jnp.float32)
        for k, value in enumerate(force + turn + [zero, zero]):
            loads[pl.ds(k, 8, stride=8), :] = value
        wide = jnp.concatenate([loads[pl.ds(8 * c, 8), :] for c in range(8)], axis=1)
        high = wide.astype(jnp.bfloat16).astype(jnp.float32)
        rest = wide - high
        mid = rest.astype(jnp.bfloat16).astype(jnp.float32)
        split = jnp.concatenate([high, mid, rest - mid], axis=0).astype(jnp.bfloat16)
        which = jnp.concatenate(
            [(ids == frag[pl.ds(g * 8 + c, 1), :]).astype(jnp.float32) for c in range(8)], axis=1
        ).astype(jnp.bfloat16)
        return split, which

    def gather(b, total):
        pairs = [operands(b * BURST + q, loads.at[pl.ds(64 * q, 64), :]) for q in range(BURST)]
        split, which = (jnp.concatenate(parts, axis=1) for parts in zip(*pairs))
        return total + lax.dot_general(split, which, (((1,), (1,)), ((), ())), preferred_element_type=jnp.float32)

    total = lax.fori_loop(0, owned // (8 * BURST), gather, jnp.zeros((24, 128), jnp.float32))
    out[...] = total[0:8] + total[8:16] + total[16:24]


def move_kernel(state, arms, frag, table, clump_next, out, clump_out):
    clump_out[...] = clump_next[...]
    rows_of = [jnp.broadcast_to(table[k : k + 1, :], (8, 128)) for k in range(6)]
    for g in range(frag.shape[0] // 8):
        rows = pl.ds(8 * g, 8)
        index = frag[rows, :]
        motion = [lane_take(r, index) for r in rows_of]
        velocity, spin = motion[0:3], motion[3:6]
        lever = [arms[k, rows, :] for k in range(3)]
        half = [0.5 * time_step * w for w in spin]
        turned = cross_rows(half, lever)
        twice = cross_rows(half, turned)
        scale = 2.0 / (1.0 + half[0] * half[0] + half[1] * half[1] + half[2] * half[2])
        moved = [lever[k] + scale * (turned[k] + twice[k]) for k in range(3)]
        swing = cross_rows(spin, moved)
        for k in range(3):
            out[k, rows, :] = state[k, rows, :] + time_step * velocity[k] + (moved[k] - lever[k])
            out[3 + k, rows, :] = velocity[k] + swing[k]


def halo(state, frag, owner, clump, cells):
    return pl.pallas_call(
        halo_kernel,
        in_specs=[VMEM] * 4,
        out_specs=(HBM, VMEM),
        out_shape=(
            jax.ShapeDtypeStruct(tuple(c + 2 for c in cells) + (8, 128), jnp.float32),
            jax.ShapeDtypeStruct((2, 128), jnp.int32),
        ),
        scratch_shapes=[
            pltpu.VMEM((8 * frag.shape[0], 128), jnp.float32),
            pltpu.SemaphoreType.DMA((26,)),
            pltpu.SemaphoreType.DMA((26,)),
            pltpu.SemaphoreType.DMA,
        ],
        compiler_params=pltpu.CompilerParams(collective_id=0, has_side_effects=True),
        name="halo",
    )(state, frag, owner, clump)


def exchange(info, sums, motion, mass, moment):
    block = lambda *shape: pltpu.VMEM(shape + (128,), jnp.float32)
    return pl.pallas_call(
        exchange_kernel,
        in_specs=[VMEM] * 5,
        out_specs=(VMEM, VMEM),
        out_shape=(
            jax.ShapeDtypeStruct((8, 128), jnp.float32),
            jax.ShapeDtypeStruct(motion.shape, jnp.float32),
        ),
        scratch_shapes=[
            block(8, 16),
            block(16, 8),
            block(4, 4, 8),
            block(4, 4, 8),
            block(4, 4, 8),
            block(4, 4, 8),
            block(4, 4, 8),
            block(8, 16),
            pltpu.SemaphoreType.DMA((6, 7)),
            pltpu.SemaphoreType.DMA((6, 7)),
            pltpu.SemaphoreType.DMA((6,)),
        ],
        compiler_params=pltpu.CompilerParams(collective_id=1, has_side_effects=True),
        name="exchange",
    )(info, sums, motion, mass, moment)


def forces(codes, cells, arms, frag):
    lines = codes.shape[0] // 128
    owned, depth = frag.shape[0], 29
    return pl.pallas_call(
        tiles_kernel,
        in_specs=[VMEM, VMEM, VMEM, VMEM],
        out_specs=VMEM,
        out_shape=jax.ShapeDtypeStruct((8, 128), jnp.float32),
        scratch_shapes=[
            pltpu.VMEM((cells.shape[0] // 8, 128), jnp.int32),
            pltpu.VMEM((lines * 128, 128), jnp.int32),
            pltpu.VMEM((lines, 128), jnp.float32),
            pltpu.VMEM((4 * lines, 128), jnp.int32),
            pltpu.SMEM((4 * lines, 128), jnp.int32),
            pltpu.VMEM((2 * lines, 128), jnp.int32),
            pltpu.SMEM((2 * lines, 128), jnp.int32),
            pltpu.VMEM((lines, 128), jnp.int32),
            pltpu.VMEM((owned, 128), jnp.int32),
            pltpu.VMEM((owned // 8, 128), jnp.int32),
            pltpu.SMEM((owned // 8, 128), jnp.int32),
            pltpu.SMEM((owned * 54 + 64,), jnp.int32),
            pltpu.VMEM((owned, 128), jnp.float32),
            pltpu.VMEM((owned * depth * 8, 128), jnp.float32),
            pltpu.VMEM((27 * 8, 128), jnp.float32),
            pltpu.VMEM((64 * GROUP, 8, 128), jnp.float32),
            pltpu.VMEM((64 * GROUP, 8, 128), jnp.float32),
            pltpu.VMEM(cells.shape, jnp.float32),
            pltpu.VMEM(cells.shape, jnp.float32),
            pltpu.VMEM(cells.shape, jnp.float32),
            pltpu.VMEM((64 * BURST, 128), jnp.float32),
            pltpu.SemaphoreType.DMA((3,)),
        ],
        compiler_params=pltpu.CompilerParams(
            vmem_limit_bytes=60 * 1024 * 1024,
        ),
        name="forces",
    )(codes.reshape(lines, 128), cells, arms, frag)


def move(state, arms, frag, table, clump_next):
    n = frag.shape[0]
    part = n // 4
    return pl.pallas_call(
        move_kernel,
        grid=(4,),
        in_specs=[
            pl.BlockSpec((3, part, 128), lambda i: (0, i, 0)),
            pl.BlockSpec((3, part, 128), lambda i: (0, i, 0)),
            pl.BlockSpec((part, 128), lambda i: (i, 0)),
            pl.BlockSpec((8, 128), lambda i: (0, 0)),
            pl.BlockSpec(clump_next.shape, lambda i: (0, 0)),
        ],
        out_specs=(
            pl.BlockSpec((6, part, 128), lambda i: (0, i, 0)),
            pl.BlockSpec(clump_next.shape, lambda i: (0, 0)),
        ),
        out_shape=(
            jax.ShapeDtypeStruct((6, n, 128), jnp.float32),
            jax.ShapeDtypeStruct(clump_next.shape, jnp.float32),
        ),
        name="move",
    )(state, arms, frag, table, clump_next)


def local(state, arms, sphere_frag, frag_owner, frag_clump, tiles, clump_motion, inv_mass, inv_moment):
    cells = state.shape[1:4]
    slots = state.shape[4]
    count = cells[0] * cells[1] * cells[2]
    held = frag_clump.shape[0]
    frag = sphere_frag.reshape(count, slots)
    padded, info = halo(state.reshape(7, count, slots), frag, frag_owner.reshape(1, held), frag_clump[None], cells)
    sums = forces(tiles[0], padded.reshape(-1, slots), arms.reshape(3, count, slots), frag)
    table, clump_next = exchange(info, sums, clump_motion, inv_mass[None], inv_moment[None])
    sphere_next, clump_next = move(
        state.reshape(7, count, slots), arms.reshape(3, count, slots), frag, table, clump_next
    )
    return sphere_next.reshape((6,) + cells + (slots,)), clump_next


def solution(mesh):
    return jax.shard_map(
        local,
        mesh=mesh,
        in_specs=(
            P(None, "gx", "gy", "gz", None),
            P(None, "gx", "gy", "gz", None),
            P("gx", "gy", "gz", None),
            P(("gx", "gy", "gz"), None),
            P(("gx", "gy", "gz")),
            P(("gx", "gy", "gz"), None),
            P(None, ("gx", "gy", "gz")),
            P(("gx", "gy", "gz")),
            P(("gx", "gy", "gz")),
        ),
        out_specs=(P(None, "gx", "gy", "gz", None), P(None, ("gx", "gy", "gz"))),
        check_vma=False,
    )
```

```python
import functools

import jax
import jax.numpy as jnp
from jax import lax
from jax.experimental import pallas as pl
from jax.experimental.pallas import tpu as pltpu
from jax.sharding import PartitionSpec as P

CAP = 2
OWN = 48
QUICK = 8
GROUP = 16
BURST = 8
REACH = 0.14001
time_step = 0.01
gravity = 9.81
epsilon_sq = 1e-08
VMEM = pl.BlockSpec(memory_space=pltpu.VMEM)


def lane_take(rows, index):
    return jnp.take_along_axis(rows, index, axis=1, mode="promise_in_bounds")


def cross_rows(first, second):
    return [
        first[1] * second[2] - first[2] * second[1],
        first[2] * second[0] - first[0] * second[2],
        first[0] * second[1] - first[1] * second[0],
    ]


MESH = pl.DeviceIdType.MESH
HBM = pl.BlockSpec(memory_space=pl.ANY)


def place_of(shift):
    return tuple(
        lax.rem(lax.axis_index(axis) + step + lax.axis_size(axis), lax.axis_size(axis))
        for axis, step in zip(("gx", "gy", "gz"), shift)
    )


def meet(others):
    barrier = pltpu.get_barrier_semaphore()
    for other in others:
        pl.semaphore_signal(barrier, inc=1, device_id=other, device_id_type=MESH)
    return lambda: pl.semaphore_wait(barrier, len(others))


def halo_kernel(state, frag, owner, clump, out, info, own, send, recv, near):
    sizes = out.shape[0] - 2, out.shape[1] - 2, out.shape[2] - 2
    shifts = [(o // 9 - 1, o // 3 % 3 - 1, o % 3 - 1) for o in range(27) if o != 13]
    shifts.sort(key=lambda s: sum(map(abs, s)))
    arrive = meet([place_of(s) for s in shifts])
    held = owner.shape[1]
    info[...] = jnp.full(info.shape, -1, jnp.int32)
    info[0:1, 0:held] = owner[...]
    info[1:2, 0:held] = clump[...]
    keys = info[0:1, :] * OWN + info[1:2, :]
    keys = jnp.broadcast_to(keys.astype(jnp.float32), (8, 128))
    for g in range(frag.shape[0] // 8):
        rows = pl.ds(8 * g, 8)
        for k in range(7):
            own[pl.ds(64 * g + k, 8, stride=8), :] = state[k, rows, :]
        own[pl.ds(64 * g + 7, 8, stride=8), :] = lane_take(keys, frag[rows, :])
    arrive()
    cells = own.reshape(sizes + (8, 128))
    copies = []
    for n, shift in enumerate(shifts):
        source = [pl.ds(0, size) if s == 0 else pl.ds(size - 1 if s > 0 else 0, 1) for s, size in zip(shift, sizes)]
        target = [pl.ds(1, size) if s == 0 else pl.ds(0 if s > 0 else size + 1, 1) for s, size in zip(shift, sizes)]
        copies.append(
            pltpu.make_async_remote_copy(
                src_ref=cells.at[tuple(source)],
                dst_ref=out.at[tuple(target)],
                send_sem=send.at[n],
                recv_sem=recv.at[n],
                device_id=place_of(shift),
                device_id_type=MESH,
            )
        )
        copies[-1].start()
    inner = pltpu.make_async_copy(cells, out.at[tuple(pl.ds(1, size) for size in sizes)], near)
    inner.start()
    for copy in copies:
        copy.wait()
    inner.wait()


def exchange_kernel(
    info, sums, motion, mass, moment, table, clump_next,
    outbox, got_z, got_y, inbox, reply, back_x, back_y, answer, send, recv, near,
):
    axes = ("gz", "gy", "gx")
    me = {axis: lax.axis_index(axis) for axis in axes}
    size = {axis: lax.axis_size(axis) for axis in axes}
    peers = {
        axis: [lax.rem(me[axis] + d, size[axis]) for d in range(1, size[axis])] for axis in axes
    }

    def device(axis, index):
        return tuple(index if a == axis else me[a] for a in ("gx", "gy", "gz"))

    arrive = meet([device(axis, p) for axis in axes for p in peers[axis]])

    def stage(number, axis, source, target):
        copies = [pltpu.make_async_copy(source(me[axis]), target(me[axis]), near.at[number])]
        copies[0].start()
        for n, peer in enumerate(peers[axis]):
            copies.append(
                pltpu.make_async_remote_copy(
                    src_ref=source(peer),
                    dst_ref=target(me[axis]),
                    send_sem=send.at[number, n],
                    recv_sem=recv.at[number, n],
                    device_id=device(axis, peer),
                    device_id_type=MESH,
                )
            )
            copies[-1].start()
        for copy in copies:
            copy.wait()

    exact = dict(precision=lax.Precision.HIGHEST, preferred_element_type=jnp.float32)
    owner = info[0:1, :]
    place = (owner & 7) * 16 + ((owner >> 3) & 3) * 4 + (owner >> 5)
    place = jnp.where(owner >= 0, place, -1)
    row = lax.broadcasted_iota(jnp.int32, (128, 128), 0)
    col = lax.broadcasted_iota(jnp.int32, (128, 128), 1)
    hit = (row == place).astype(jnp.float32)
    earlier = jnp.dot(
        hit.astype(jnp.bfloat16), (row < col).astype(jnp.float32).astype(jnp.bfloat16),
        preferred_element_type=jnp.float32,
    )
    slots = [jnp.where(earlier == float(e), hit, 0.0) for e in range(CAP)]
    across = (((1,), (1,)), ((), ()))
    filler = jnp.zeros((112, 128), jnp.float32)
    empty = jnp.zeros((8, 128), jnp.float32)
    sub = lax.broadcasted_iota(jnp.int32, (8, 128), 0)
    label = (info[1:2, :] + 1).astype(jnp.float32)
    payload = jnp.where(sub == 6, label, jnp.where(sub == 7, 0.0, sums[...]))
    outbox[...] = (
        lax.dot_general(slots[0], jnp.concatenate([payload, empty, filler], axis=0), across, **exact)
        + lax.dot_general(slots[1], jnp.concatenate([empty, payload, filler], axis=0), across, **exact)
    ).reshape(outbox.shape)
    arrive()
    stage(0, "gz", lambda p: outbox.at[p], lambda p: got_z.at[:, p])
    by_y = got_z.reshape(4, 4, 8, 128)
    stage(1, "gy", lambda p: by_y.at[p], lambda p: got_y.at[:, p])
    stage(2, "gx", lambda p: got_y.at[p], lambda p: inbox.at[p])

    flat = inbox[...].reshape(128, 128)
    turned = flat.T
    names = lax.broadcasted_iota(jnp.int32, (128, motion.shape[1]), 1).astype(jnp.float32) + 1.0
    which = [(jnp.broadcast_to(flat[:, 8 * e + 6 : 8 * e + 7], names.shape) == names).astype(jnp.float32) for e in range(CAP)]
    total = jnp.dot(turned[0:8], which[0], **exact) + jnp.dot(turned[8:16], which[1], **exact)
    lower = lax.broadcasted_iota(jnp.int32, (3, motion.shape[1]), 0)
    pull = jnp.where(lower == 2, gravity, 0.0)
    velocity = motion[0:3, :] + time_step * (total[0:3] * mass[...] - pull)
    spin = motion[3:6, :] + time_step * total[3:6] * moment[...]
    clump_next[0:3, :] = velocity
    clump_next[3:6, :] = spin
    moved = jnp.concatenate([velocity, spin, jnp.zeros((2, motion.shape[1]), jnp.float32)], axis=0)
    blank = jnp.zeros((8, motion.shape[1]), jnp.float32)
    rest = jnp.zeros((112, motion.shape[1]), jnp.float32)
    reply[...] = (
        lax.dot_general(which[0], jnp.concatenate([moved, blank, rest], axis=0), across, **exact)
        + lax.dot_general(which[1], jnp.concatenate([blank, moved, rest], axis=0), across, **exact)
    ).reshape(reply.shape)
    stage(3, "gx", lambda p: reply.at[p], lambda p: back_x.at[p])
    stage(4, "gy", lambda p: back_x.at[:, p], lambda p: back_y.at[p])
    by_z = back_y.reshape(16, 8, 128)
    stage(5, "gz", lambda p: by_z.at[:, p], lambda p: answer.at[p])
    turned = answer[...].reshape(128, 128).T
    table[...] = jnp.dot(turned[0:8], slots[0], **exact) + jnp.dot(turned[8:16], slots[1], **exact)


def tiles_kernel(
    codes, cells, arms, frag, out, cand, mask, counts, where_v, where_s, place_v, place_s, own_v, wide_v, lens_v, lens_s, items,
    carry, lists, shifts, wide_a, wide_b, push_x, push_y, push_z, loads, sems,
):
    pushes = (push_x, push_y, push_z)
    lines = codes.shape[0]
    tiles = lines * 128
    pad = cells.shape[0] // 8
    ny, nz = 6, 18
    owned = 256
    depth = lists.shape[0] // (8 * owned)
    sub = lax.broadcasted_iota(jnp.int32, (8, 128), 0)
    lane = lax.broadcasted_iota(jnp.int32, (8, 128), 1)

    code = codes[...]
    own_of = (code * 38837) >> 20
    way = code - 27 * own_of
    step_x = ((way * 57) >> 9) - 1
    left = way - 9 * (step_x + 1)
    step_y = ((left * 11) >> 5) - 1
    step_z = left - 3 * (step_y + 1) - 1
    cell_of = ((own_of >> 6) + 1 + step_x) * (ny * nz) + (((own_of >> 4) & 3) + 1 + step_y) * nz
    cell_of = cell_of + (own_of & 15) + 1 + step_z
    for k, value in enumerate((cell_of, cell_of * 8, way, way * 8)):
        where_v[k * lines : (k + 1) * lines, :] = value
    own_v[...] = own_of
    first_copy = pltpu.make_async_copy(where_v, where_s, sems.at[0])
    first_copy.start()

    def reach_bits(g):
        base = pl.multiple_of(g * 64, 64)
        pos = [cells[pl.ds(base + k, 8, stride=8), :] for k in range(3)]
        reach = cells[pl.ds(base + 6, 8, stride=8), :] + REACH
        reach = reach * reach
        near = [p * p for p in pos]
        far = [(1.0 - p) * (1.0 - p) for p in pos]
        bits = jnp.full((8, 128), 1 << 13, jnp.int32)
        for o in range(27):
            steps = (o // 9 - 1, o // 3 % 3 - 1, o % 3 - 1)
            terms = [near[k] if s > 0 else far[k] for k, s in enumerate(steps) if s]
            if not terms:
                continue
            bits = bits | jnp.where(sum(terms[1:], terms[0]) <= reach, 1 << o, 0)
        cand[pl.ds(pl.multiple_of(g * 8, 8), 8), :] = bits

    @pl.loop(0, pad // 24)
    def _(g):
        for u in range(3):
            reach_bits(3 * g + u)

    @pl.loop(0, 27)
    def _(o):
        step_x = ((o * 57) >> 9) - 1
        left = o - 9 * (step_x + 1)
        step_y = ((left * 11) >> 5) - 1
        step_z = left - 3 * (step_y + 1) - 1
        value = jnp.where(sub == 0, step_x, jnp.where(sub == 1, step_y, jnp.where(sub == 2, step_z, 0)))
        shifts[pl.ds(pl.multiple_of(o * 8, 8), 8), :] = value.astype(jnp.float32)

    @pl.loop(0, owned // 16)
    def _(b):
        first = ((b >> 2) + 1) * (ny * nz) + ((b & 3) + 1) * nz + 1
        rows = pl.ds(pl.multiple_of(first * 8, 8), 128)
        for push in pushes:
            push[rows, :] = jnp.zeros((128, 128), jnp.float32)

    first_copy.wait()

    @pl.loop(0, lines)
    def _(b):
        for u in range(128):
            row = cand[pl.ds(where_s[b, u], 1), :]
            mask[pl.ds(b * 128 + u, 1), :] = (row >> where_s[2 * lines + b, u]) & 1

    row = lax.broadcasted_iota(jnp.int32, (128, 128), 0)
    col = lax.broadcasted_iota(jnp.int32, (128, 128), 1)
    before = (row < col).astype(jnp.bfloat16)
    ones = jnp.ones((8, 128), jnp.bfloat16)

    @pl.loop(0, lines // BURST)
    def _(b):
        rows = pl.ds(pl.multiple_of(b * (128 * BURST), 128 * BURST), 128 * BURST)
        col = lax.broadcasted_iota(jnp.int32, (128 * BURST, 128), 1)
        active = mask[rows, :]
        flags = active.astype(jnp.float32).astype(jnp.bfloat16)
        rank = jnp.dot(flags, before, preferred_element_type=jnp.float32).astype(jnp.int32)
        number = lax.dot_general(ones, flags, (((1,), (1,)), ((), ())), preferred_element_type=jnp.float32)
        for q in range(BURST):
            counts[pl.ds(b * BURST + q, 1), :] = number[0:1, 128 * q : 128 * q + 128]
        value = jnp.where(active > 0, ((col - rank) << 7) | col, 0)
        for bit in range(7):
            moved = pltpu.roll(value, 128 - (1 << bit), axis=1)
            flag = 1 << (7 + bit)
            value = jnp.where((moved & flag) != 0, moved, jnp.where((value & flag) != 0, 0, value))
        mask[rows, :] = value & 127

    both = jnp.concatenate([before, jnp.ones((128, 128), jnp.bfloat16)], axis=1)
    cell_id = lax.broadcasted_iota(jnp.int32, (owned, 128), 0)
    carry[...] = jnp.zeros((owned, 128), jnp.float32)

    @pl.loop(0, lines // 4)
    def _(n):
        mine = [own_v[pl.ds(4 * n + q, 1), :] for q in range(4)]
        hot = [cell_id == m for m in mine]
        amount = [jnp.where(hot[q], counts[pl.ds(4 * n + q, 1), :], 0.0) for q in range(4)]
        amount = jnp.concatenate(amount, axis=0).astype(jnp.bfloat16)
        summed = jnp.dot(amount, both, preferred_element_type=jnp.float32)
        for q in range(4):
            part = summed[owned * q : owned * (q + 1)]
            so_far = carry[...]
            at = jnp.sum(jnp.where(hot[q], part[:, 0:128] + so_far, 0.0), axis=0, keepdims=True)
            carry[...] = so_far + part[:, 128:256]
            spot = mine[q] * (depth * 128) + at.astype(jnp.int32)
            place_v[pl.ds(4 * n + q, 1), :] = (spot >> 7) << 3
            place_v[pl.ds(lines + 4 * n + q, 1), :] = spot & 127

    length = carry[...].astype(jnp.int32)
    cell_lane = lax.broadcasted_iota(jnp.int32, (owned, 128), 1)
    padded_id = ((cell_id >> 6) + 1) * (ny * nz) + (((cell_id >> 4) & 3) + 1) * nz + (cell_id & 15) + 1
    words = (
        cell_id * (depth * 8) + ((length >> 7) << 3),
        length & 127,
        jnp.minimum((length + 63) >> 6, QUICK),
        (padded_id << 16) + cell_id * (2 * depth),
        length,
        jnp.broadcast_to(jnp.max(length, axis=0, keepdims=True), (owned, 128)),
    )
    packed = words[0]
    for k, word in enumerate(words[1:]):
        packed = jnp.where((cell_lane & 15) == k + 1, word, packed)
    wide_v[...] = packed
    eight = lax.broadcasted_iota(jnp.int32, (owned // 8, 128), 1) >> 4
    folded = wide_v[pl.ds(0, owned // 8, stride=8), :]
    for u in range(1, 8):
        folded = jnp.where(eight == u, wide_v[pl.ds(u, owned // 8, stride=8), :], folded)
    lens_v[...] = folded
    copies = [
        pltpu.make_async_copy(place_v, place_s, sems.at[1]),
        pltpu.make_async_copy(lens_v, lens_s, sems.at[2]),
    ]
    for copy in copies:
        copy.start()
    for copy in copies:
        copy.wait()

    def append(sorted_rows, to, turn):
        to = pl.multiple_of(to, 8)
        turned = pltpu.roll(sorted_rows, turn, axis=1)
        pltpu.store(lists.at[pl.ds(to, 8), :], turned, mask=lane >= turn)
        lists[pl.ds(to + 8, 8), :] = turned

    @pl.loop(0, lines)
    def _(b):
        for u in range(128):
            values = cells[pl.ds(pl.multiple_of(where_s[lines + b, u], 8), 8), :]
            index = jnp.broadcast_to(mask[pl.ds(b * 128 + u, 1), :], (8, 128))
            shift = shifts[pl.ds(pl.multiple_of(where_s[3 * lines + b, u], 8), 8), :]
            append(lane_take(values, index) + shift, place_s[b, u], place_s[lines + b, u])

    dummy = jnp.where(sub < 3, 1000.0, 0.1)

    def close(b, total):
        for u in range(8):
            append(dummy, lens_s[b, 16 * u], lens_s[b, 16 * u + 1])
            first = lens_s[b, 16 * u + 3]
            for k in range(QUICK):
                items[total + k] = first + k
            total = total + lens_s[b, 16 * u + 2]
        return total

    number = lax.fori_loop(0, owned // 8, close, 0)

    def longer(c, total):
        line, at = c >> 3, (c & 7) * 16

        def add(k, total):
            items[total] = lens_s[line, at + 3] + k
            return total + 1

        return lax.fori_loop(QUICK, (lens_s[line, at + 4] + 63) >> 6, add, total)

    number = lax.fori_loop(0, jnp.where(lens_s[0, 5] > 64 * QUICK, owned, 0), longer, number)
    for k in range(3 * GROUP):
        items[number + k] = 0

    which_row = lax.broadcasted_iota(jnp.int32, (24, 1024), 0)
    which_col = lax.broadcasted_iota(jnp.int32, (24, 1024), 1)
    pick = ((which_row & 7) == (which_col >> 7)).astype(jnp.float32).astype(jnp.bfloat16)

    def spread(words, wide):
        splits = []
        for word in words:
            spot = word & 0xFFFF
            values = lists[pl.ds(pl.multiple_of((spot >> 1) * 8, 8), 8), :]
            values = pltpu.roll(values, (spot & 1) * 64, axis=1)
            high = values.astype(jnp.bfloat16).astype(jnp.float32)
            rest = values - high
            mid = rest.astype(jnp.bfloat16).astype(jnp.float32)
            split = jnp.concatenate([high, mid, rest - mid], axis=0)
            splits.append(split.T[0:64])
        split = jnp.concatenate(splits, axis=0).astype(jnp.bfloat16)
        spreads = jnp.dot(split, pick, preferred_element_type=jnp.float32)
        for u in range(8 * len(words)):
            for k in range(8):
                wide[8 * u + k] = spreads[8 * u : 8 * u + 8, 128 * k : 128 * k + 128]

    def press(word, wide, first):
        base = pl.multiple_of((word >> 16) * 8, 8)
        own = [jnp.broadcast_to(cells[pl.ds(base + k, 1), :], (8, 128)) for k in range(8)]
        total = [None] * 3
        for u in range(8):
            other = [wide[8 * (first + u) + k] for k in range(8)]
            apart = [other[k] - own[k] for k in range(3)]
            square = apart[0] * apart[0] + apart[1] * apart[1] + apart[2] * apart[2] + epsilon_sq
            inverse = lax.rsqrt(square)
            reach = own[6] + other[6]
            depth_in = jnp.where(own[7] != other[7], jnp.maximum(reach - square * inverse, 0.0), 0.0)
            closing = (
                (other[3] - own[3]) * apart[0] + (other[4] - own[4]) * apart[1] + (other[5] - own[5]) * apart[2]
            )
            along = closing * inverse - 50.0 * depth_in
            area = own[6] * other[6] * depth_in
            factor = area * lax.rsqrt(jnp.maximum(area * reach, 1e-20)) * along * inverse
            for k in range(3):
                term = factor * apart[k]
                total[k] = term if u == 0 else total[k] + term
        rows = pl.ds(base, 8)
        for k in range(3):
            pushes[k][rows, :] += total[k]

    def group(n):
        return [items[n * GROUP + k] for k in range(GROUP)]

    spread(group(0), wide_a)

    @pl.loop(0, (number + (2 * GROUP - 1)) // (2 * GROUP))
    def _(p):
        def half(n, now, later):
            spread(group(n + 1), later)
            for k, word in enumerate(group(n)):
                press(word, now, 8 * k)

        half(2 * p, wide_a, wide_b)
        half(2 * p + 1, wide_b, wide_a)

    ids = lax.broadcasted_iota(jnp.int32, (128, 128), 0)

    def operands(g, loads):
        rows = pl.ds(pl.multiple_of(g * 8, 8), 8)
        force = []
        first = (((g >> 3) + 1) * (ny * nz) + (((g >> 1) & 3) + 1) * nz + (g & 1) * 8 + 1) * 8
        for push in pushes:
            parts = [push[pl.ds(first + s, 8, stride=8), :] for s in range(8)]
            while len(parts) > 1:
                parts = [parts[i] + parts[i + 1] for i in range(0, len(parts), 2)]
            force.append(2.0 * parts[0])
        turn = cross_rows([arms[k, rows, :] for k in range(3)], force)
        zero = jnp.zeros((8, 128), jnp.float32)
        for k, value in enumerate(force + turn + [zero, zero]):
            loads[pl.ds(k, 8, stride=8), :] = value
        wide = jnp.concatenate([loads[pl.ds(8 * c, 8), :] for c in range(8)], axis=1)
        high = wide.astype(jnp.bfloat16).astype(jnp.float32)
        rest = wide - high
        mid = rest.astype(jnp.bfloat16).astype(jnp.float32)
        split = jnp.concatenate([high, mid, rest - mid], axis=0).astype(jnp.bfloat16)
        which = jnp.concatenate(
            [(ids == frag[pl.ds(g * 8 + c, 1), :]).astype(jnp.float32) for c in range(8)], axis=1
        ).astype(jnp.bfloat16)
        return split, which

    def gather(b, total):
        pairs = [operands(b * BURST + q, loads.at[pl.ds(64 * q, 64), :]) for q in range(BURST)]
        split, which = (jnp.concatenate(parts, axis=1) for parts in zip(*pairs))
        return total + lax.dot_general(split, which, (((1,), (1,)), ((), ())), preferred_element_type=jnp.float32)

    total = lax.fori_loop(0, owned // (8 * BURST), gather, jnp.zeros((24, 128), jnp.float32))
    out[...] = total[0:8] + total[8:16] + total[16:24]


def move_kernel(state, arms, frag, table, clump_next, out, clump_out):
    clump_out[...] = clump_next[...]
    rows_of = [jnp.broadcast_to(table[k : k + 1, :], (8, 128)) for k in range(6)]
    for g in range(frag.shape[0] // 8):
        rows = pl.ds(8 * g, 8)
        index = frag[rows, :]
        motion = [lane_take(r, index) for r in rows_of]
        velocity, spin = motion[0:3], motion[3:6]
        lever = [arms[k, rows, :] for k in range(3)]
        half = [0.5 * time_step * w for w in spin]
        turned = cross_rows(half, lever)
        twice = cross_rows(half, turned)
        scale = 2.0 / (1.0 + half[0] * half[0] + half[1] * half[1] + half[2] * half[2])
        moved = [lever[k] + scale * (turned[k] + twice[k]) for k in range(3)]
        swing = cross_rows(spin, moved)
        for k in range(3):
            out[k, rows, :] = state[k, rows, :] + time_step * velocity[k] + (moved[k] - lever[k])
            out[3 + k, rows, :] = velocity[k] + swing[k]


def halo(state, frag, owner, clump, cells):
    return pl.pallas_call(
        halo_kernel,
        in_specs=[VMEM] * 4,
        out_specs=(HBM, VMEM),
        out_shape=(
            jax.ShapeDtypeStruct(tuple(c + 2 for c in cells) + (8, 128), jnp.float32),
            jax.ShapeDtypeStruct((2, 128), jnp.int32),
        ),
        scratch_shapes=[
            pltpu.VMEM((8 * frag.shape[0], 128), jnp.float32),
            pltpu.SemaphoreType.DMA((26,)),
            pltpu.SemaphoreType.DMA((26,)),
            pltpu.SemaphoreType.DMA,
        ],
        compiler_params=pltpu.CompilerParams(collective_id=0, has_side_effects=True),
        name="halo",
    )(state, frag, owner, clump)


def exchange(info, sums, motion, mass, moment):
    block = lambda *shape: pltpu.VMEM(shape + (128,), jnp.float32)
    return pl.pallas_call(
        exchange_kernel,
        in_specs=[VMEM] * 5,
        out_specs=(VMEM, VMEM),
        out_shape=(
            jax.ShapeDtypeStruct((8, 128), jnp.float32),
            jax.ShapeDtypeStruct(motion.shape, jnp.float32),
        ),
        scratch_shapes=[
            block(8, 16),
            block(16, 8),
            block(4, 4, 8),
            block(4, 4, 8),
            block(4, 4, 8),
            block(4, 4, 8),
            block(4, 4, 8),
            block(8, 16),
            pltpu.SemaphoreType.DMA((6, 7)),
            pltpu.SemaphoreType.DMA((6, 7)),
            pltpu.SemaphoreType.DMA((6,)),
        ],
        compiler_params=pltpu.CompilerParams(collective_id=1, has_side_effects=True),
        name="exchange",
    )(info, sums, motion, mass, moment)


def forces(codes, cells, arms, frag):
    lines = codes.shape[0] // 128
    owned, depth = frag.shape[0], 29
    return pl.pallas_call(
        tiles_kernel,
        in_specs=[VMEM, VMEM, VMEM, VMEM],
        out_specs=VMEM,
        out_shape=jax.ShapeDtypeStruct((8, 128), jnp.float32),
        scratch_shapes=[
            pltpu.VMEM((cells.shape[0] // 8, 128), jnp.int32),
            pltpu.VMEM((lines * 128, 128), jnp.int32),
            pltpu.VMEM((lines, 128), jnp.float32),
            pltpu.VMEM((4 * lines, 128), jnp.int32),
            pltpu.SMEM((4 * lines, 128), jnp.int32),
            pltpu.VMEM((2 * lines, 128), jnp.int32),
            pltpu.SMEM((2 * lines, 128), jnp.int32),
            pltpu.VMEM((lines, 128), jnp.int32),
            pltpu.VMEM((owned, 128), jnp.int32),
            pltpu.VMEM((owned // 8, 128), jnp.int32),
            pltpu.SMEM((owned // 8, 128), jnp.int32),
            pltpu.SMEM((owned * 54 + 96,), jnp.int32),
            pltpu.VMEM((owned, 128), jnp.float32),
            pltpu.VMEM((owned * depth * 8, 128), jnp.float32),
            pltpu.VMEM((27 * 8, 128), jnp.float32),
            pltpu.VMEM((64 * GROUP, 8, 128), jnp.float32),
            pltpu.VMEM((64 * GROUP, 8, 128), jnp.float32),
            pltpu.VMEM(cells.shape, jnp.float32),
            pltpu.VMEM(cells.shape, jnp.float32),
            pltpu.VMEM(cells.shape, jnp.float32),
            pltpu.VMEM((64 * BURST, 128), jnp.float32),
            pltpu.SemaphoreType.DMA((3,)),
        ],
        compiler_params=pltpu.CompilerParams(
            vmem_limit_bytes=60 * 1024 * 1024,
        ),
        name="forces",
    )(codes.reshape(lines, 128), cells, arms, frag)


def move(state, arms, frag, table, clump_next):
    n = frag.shape[0]
    part = n // 4
    return pl.pallas_call(
        move_kernel,
        grid=(4,),
        in_specs=[
            pl.BlockSpec((3, part, 128), lambda i: (0, i, 0)),
            pl.BlockSpec((3, part, 128), lambda i: (0, i, 0)),
            pl.BlockSpec((part, 128), lambda i: (i, 0)),
            pl.BlockSpec((8, 128), lambda i: (0, 0)),
            pl.BlockSpec(clump_next.shape, lambda i: (0, 0)),
        ],
        out_specs=(
            pl.BlockSpec((6, part, 128), lambda i: (0, i, 0)),
            pl.BlockSpec(clump_next.shape, lambda i: (0, 0)),
        ),
        out_shape=(
            jax.ShapeDtypeStruct((6, n, 128), jnp.float32),
            jax.ShapeDtypeStruct(clump_next.shape, jnp.float32),
        ),
        name="move",
    )(state, arms, frag, table, clump_next)


def local(state, arms, sphere_frag, frag_owner, frag_clump, tiles, clump_motion, inv_mass, inv_moment):
    cells = state.shape[1:4]
    slots = state.shape[4]
    count = cells[0] * cells[1] * cells[2]
    held = frag_clump.shape[0]
    frag = sphere_frag.reshape(count, slots)
    padded, info = halo(state.reshape(7, count, slots), frag, frag_owner.reshape(1, held), frag_clump[None], cells)
    sums = forces(tiles[0], padded.reshape(-1, slots), arms.reshape(3, count, slots), frag)
    table, clump_next = exchange(info, sums, clump_motion, inv_mass[None], inv_moment[None])
    sphere_next, clump_next = move(
        state.reshape(7, count, slots), arms.reshape(3, count, slots), frag, table, clump_next
    )
    return sphere_next.reshape((6,) + cells + (slots,)), clump_next


def solution(mesh):
    return jax.shard_map(
        local,
        mesh=mesh,
        in_specs=(
            P(None, "gx", "gy", "gz", None),
            P(None, "gx", "gy", "gz", None),
            P("gx", "gy", "gz", None),
            P(("gx", "gy", "gz"), None),
            P(("gx", "gy", "gz")),
            P(("gx", "gy", "gz"), None),
            P(None, ("gx", "gy", "gz")),
            P(("gx", "gy", "gz")),
            P(("gx", "gy", "gz")),
        ),
        out_specs=(P(None, "gx", "gy", "gz", None), P(None, ("gx", "gy", "gz"))),
        check_vma=False,
    )
```

```python
import functools

import jax
import jax.numpy as jnp
from jax import lax
from jax.experimental import pallas as pl
from jax.experimental.pallas import tpu as pltpu
from jax.sharding import PartitionSpec as P

CAP = 2
OWN = 48
QUICK = 8
GROUP = 16
BURST = 8
REACH = 0.14001
time_step = 0.01
gravity = 9.81
epsilon_sq = 1e-08
VMEM = pl.BlockSpec(memory_space=pltpu.VMEM)


def lane_take(rows, index):
    return jnp.take_along_axis(rows, index, axis=1, mode="promise_in_bounds")


def cross_rows(first, second):
    return [
        first[1] * second[2] - first[2] * second[1],
        first[2] * second[0] - first[0] * second[2],
        first[0] * second[1] - first[1] * second[0],
    ]


MESH = pl.DeviceIdType.MESH
HBM = pl.BlockSpec(memory_space=pl.ANY)


def place_of(shift):
    return tuple(
        lax.rem(lax.axis_index(axis) + step + lax.axis_size(axis), lax.axis_size(axis))
        for axis, step in zip(("gx", "gy", "gz"), shift)
    )


def meet(others):
    barrier = pltpu.get_barrier_semaphore()
    for other in others:
        pl.semaphore_signal(barrier, inc=1, device_id=other, device_id_type=MESH)
    return lambda: pl.semaphore_wait(barrier, len(others))


def halo_kernel(state, frag, owner, clump, out, info, own, send, recv, near):
    sizes = out.shape[0] - 2, out.shape[1] - 2, out.shape[2] - 2
    shifts = [(o // 9 - 1, o // 3 % 3 - 1, o % 3 - 1) for o in range(27) if o != 13]
    shifts.sort(key=lambda s: sum(map(abs, s)))
    arrive = meet([place_of(s) for s in shifts])
    held = owner.shape[1]
    info[...] = jnp.full(info.shape, -1, jnp.int32)
    info[0:1, 0:held] = owner[...]
    info[1:2, 0:held] = clump[...]
    keys = info[0:1, :] * OWN + info[1:2, :]
    keys = jnp.broadcast_to(keys.astype(jnp.float32), (8, 128))
    for g in range(frag.shape[0] // 8):
        rows = pl.ds(8 * g, 8)
        for k in range(7):
            own[pl.ds(64 * g + k, 8, stride=8), :] = state[k, rows, :]
        own[pl.ds(64 * g + 7, 8, stride=8), :] = lane_take(keys, frag[rows, :])
    arrive()
    cells = own.reshape(sizes + (8, 128))
    copies = []
    for n, shift in enumerate(shifts):
        source = [pl.ds(0, size) if s == 0 else pl.ds(size - 1 if s > 0 else 0, 1) for s, size in zip(shift, sizes)]
        target = [pl.ds(1, size) if s == 0 else pl.ds(0 if s > 0 else size + 1, 1) for s, size in zip(shift, sizes)]
        copies.append(
            pltpu.make_async_remote_copy(
                src_ref=cells.at[tuple(source)],
                dst_ref=out.at[tuple(target)],
                send_sem=send.at[n],
                recv_sem=recv.at[n],
                device_id=place_of(shift),
                device_id_type=MESH,
            )
        )
        copies[-1].start()
    inner = pltpu.make_async_copy(cells, out.at[tuple(pl.ds(1, size) for size in sizes)], near)
    inner.start()
    for copy in copies:
        copy.wait()
    inner.wait()


def exchange_kernel(
    info, sums, motion, mass, moment, table, clump_next,
    outbox, got_z, inbox, reply, back, answer, send, recv, near,
):
    me = [lax.axis_index(axis) for axis in ("gx", "gy", "gz")]
    size = [lax.axis_size(axis) for axis in ("gx", "gy", "gz")]
    line = [(0, 0, d) for d in range(1, size[2])]
    plane = [(dx, dy, 0) for dx in range(size[0]) for dy in range(size[1]) if dx or dy]

    def beyond(step):
        return tuple(lax.rem(m + d, n) for m, d, n in zip(me, step, size))

    arrive = meet([beyond(step) for step in line + plane])

    def stage(number, steps, source, target):
        copies = [pltpu.make_async_copy(source(*me), target(*me), near.at[number])]
        copies[0].start()
        for n, step in enumerate(steps):
            other = beyond(step)
            copies.append(
                pltpu.make_async_remote_copy(
                    src_ref=source(*other),
                    dst_ref=target(*me),
                    send_sem=send.at[number, n],
                    recv_sem=recv.at[number, n],
                    device_id=other,
                    device_id_type=MESH,
                )
            )
            copies[-1].start()
        for copy in copies:
            copy.wait()

    exact = dict(precision=lax.Precision.HIGHEST, preferred_element_type=jnp.float32)
    owner = info[0:1, :]
    place = (owner & 7) * 16 + ((owner >> 3) & 3) * 4 + (owner >> 5)
    place = jnp.where(owner >= 0, place, -1)
    row = lax.broadcasted_iota(jnp.int32, (128, 128), 0)
    col = lax.broadcasted_iota(jnp.int32, (128, 128), 1)
    hit = (row == place).astype(jnp.float32)
    earlier = jnp.dot(
        hit.astype(jnp.bfloat16), (row < col).astype(jnp.float32).astype(jnp.bfloat16),
        preferred_element_type=jnp.float32,
    )
    slots = [jnp.where(earlier == float(e), hit, 0.0) for e in range(CAP)]
    across = (((1,), (1,)), ((), ()))
    filler = jnp.zeros((112, 128), jnp.float32)
    empty = jnp.zeros((8, 128), jnp.float32)
    sub = lax.broadcasted_iota(jnp.int32, (8, 128), 0)
    label = (info[1:2, :] + 1).astype(jnp.float32)
    payload = jnp.where(sub == 6, label, jnp.where(sub == 7, 0.0, sums[...]))
    outbox[...] = (
        lax.dot_general(slots[0], jnp.concatenate([payload, empty, filler], axis=0), across, **exact)
        + lax.dot_general(slots[1], jnp.concatenate([empty, payload, filler], axis=0), across, **exact)
    ).reshape(outbox.shape)
    arrive()
    stage(0, line, lambda x, y, z: outbox.at[z], lambda x, y, z: got_z.at[:, z])
    stage(1, plane, lambda x, y, z: got_z.at[y * 4 + x], lambda x, y, z: inbox.at[x, y])

    flat = inbox[...].reshape(128, 128)
    turned = flat.T
    names = lax.broadcasted_iota(jnp.int32, (128, motion.shape[1]), 1).astype(jnp.float32) + 1.0
    which = [(jnp.broadcast_to(flat[:, 8 * e + 6 : 8 * e + 7], names.shape) == names).astype(jnp.float32) for e in range(CAP)]
    total = jnp.dot(turned[0:8], which[0], **exact) + jnp.dot(turned[8:16], which[1], **exact)
    lower = lax.broadcasted_iota(jnp.int32, (3, motion.shape[1]), 0)
    pull = jnp.where(lower == 2, gravity, 0.0)
    velocity = motion[0:3, :] + time_step * (total[0:3] * mass[...] - pull)
    spin = motion[3:6, :] + time_step * total[3:6] * moment[...]
    clump_next[0:3, :] = velocity
    clump_next[3:6, :] = spin
    moved = jnp.concatenate([velocity, spin, jnp.zeros((2, motion.shape[1]), jnp.float32)], axis=0)
    blank = jnp.zeros((8, motion.shape[1]), jnp.float32)
    rest = jnp.zeros((112, motion.shape[1]), jnp.float32)
    reply[...] = (
        lax.dot_general(which[0], jnp.concatenate([moved, blank, rest], axis=0), across, **exact)
        + lax.dot_general(which[1], jnp.concatenate([blank, moved, rest], axis=0), across, **exact)
    ).reshape(reply.shape)
    stage(2, plane, lambda x, y, z: reply.at[x, y], lambda x, y, z: back.at[y * 4 + x])
    stage(3, line, lambda x, y, z: back.at[:, z], lambda x, y, z: answer.at[z])
    turned = answer[...].reshape(128, 128).T
    table[...] = jnp.dot(turned[0:8], slots[0], **exact) + jnp.dot(turned[8:16], slots[1], **exact)


def tiles_kernel(
    codes, cells, arms, frag, out, cand, mask, counts, where_v, where_s, place_v, place_s, own_v, wide_v, lens_v, lens_s, items,
    carry, lists, shifts, wide_a, wide_b, push_x, push_y, push_z, loads, sems,
):
    pushes = (push_x, push_y, push_z)
    lines = codes.shape[0]
    tiles = lines * 128
    pad = cells.shape[0] // 8
    ny, nz = 6, 18
    owned = 256
    depth = lists.shape[0] // (8 * owned)
    sub = lax.broadcasted_iota(jnp.int32, (8, 128), 0)
    lane = lax.broadcasted_iota(jnp.int32, (8, 128), 1)

    code = codes[...]
    own_of = (code * 38837) >> 20
    way = code - 27 * own_of
    step_x = ((way * 57) >> 9) - 1
    left = way - 9 * (step_x + 1)
    step_y = ((left * 11) >> 5) - 1
    step_z = left - 3 * (step_y + 1) - 1
    cell_of = ((own_of >> 6) + 1 + step_x) * (ny * nz) + (((own_of >> 4) & 3) + 1 + step_y) * nz
    cell_of = cell_of + (own_of & 15) + 1 + step_z
    for k, value in enumerate((cell_of, cell_of * 8, way, way * 8)):
        where_v[k * lines : (k + 1) * lines, :] = value
    own_v[...] = own_of
    first_copy = pltpu.make_async_copy(where_v, where_s, sems.at[0])
    first_copy.start()

    def reach_bits(g):
        base = pl.multiple_of(g * 64, 64)
        pos = [cells[pl.ds(base + k, 8, stride=8), :] for k in range(3)]
        reach = cells[pl.ds(base + 6, 8, stride=8), :] + REACH
        reach = reach * reach
        near = [p * p for p in pos]
        far = [(1.0 - p) * (1.0 - p) for p in pos]
        bits = jnp.full((8, 128), 1 << 13, jnp.int32)
        for o in range(27):
            steps = (o // 9 - 1, o // 3 % 3 - 1, o % 3 - 1)
            terms = [near[k] if s > 0 else far[k] for k, s in enumerate(steps) if s]
            if not terms:
                continue
            bits = bits | jnp.where(sum(terms[1:], terms[0]) <= reach, 1 << o, 0)
        cand[pl.ds(pl.multiple_of(g * 8, 8), 8), :] = bits

    @pl.loop(0, pad // 24)
    def _(g):
        for u in range(3):
            reach_bits(3 * g + u)

    @pl.loop(0, 27)
    def _(o):
        step_x = ((o * 57) >> 9) - 1
        left = o - 9 * (step_x + 1)
        step_y = ((left * 11) >> 5) - 1
        step_z = left - 3 * (step_y + 1) - 1
        value = jnp.where(sub == 0, step_x, jnp.where(sub == 1, step_y, jnp.where(sub == 2, step_z, 0)))
        shifts[pl.ds(pl.multiple_of(o * 8, 8), 8), :] = value.astype(jnp.float32)

    @pl.loop(0, owned // 16)
    def _(b):
        first = ((b >> 2) + 1) * (ny * nz) + ((b & 3) + 1) * nz + 1
        rows = pl.ds(pl.multiple_of(first * 8, 8), 128)
        for push in pushes:
            push[rows, :] = jnp.zeros((128, 128), jnp.float32)

    first_copy.wait()

    @pl.loop(0, lines)
    def _(b):
        for u in range(128):
            row = cand[pl.ds(where_s[b, u], 1), :]
            mask[pl.ds(b * 128 + u, 1), :] = (row >> where_s[2 * lines + b, u]) & 1

    row = lax.broadcasted_iota(jnp.int32, (128, 128), 0)
    col = lax.broadcasted_iota(jnp.int32, (128, 128), 1)
    before = (row < col).astype(jnp.bfloat16)
    ones = jnp.ones((8, 128), jnp.bfloat16)

    @pl.loop(0, lines // BURST)
    def _(b):
        rows = pl.ds(pl.multiple_of(b * (128 * BURST), 128 * BURST), 128 * BURST)
        col = lax.broadcasted_iota(jnp.int32, (128 * BURST, 128), 1)
        active = mask[rows, :]
        flags = active.astype(jnp.float32).astype(jnp.bfloat16)
        rank = jnp.dot(flags, before, preferred_element_type=jnp.float32).astype(jnp.int32)
        number = lax.dot_general(ones, flags, (((1,), (1,)), ((), ())), preferred_element_type=jnp.float32)
        for q in range(BURST):
            counts[pl.ds(b * BURST + q, 1), :] = number[0:1, 128 * q : 128 * q + 128]
        value = jnp.where(active > 0, ((col - rank) << 7) | col, 0)
        for bit in range(7):
            moved = pltpu.roll(value, 128 - (1 << bit), axis=1)
            flag = 1 << (7 + bit)
            value = jnp.where((moved & flag) != 0, moved, jnp.where((value & flag) != 0, 0, value))
        mask[rows, :] = value & 127

    both = jnp.concatenate([before, jnp.ones((128, 128), jnp.bfloat16)], axis=1)
    cell_id = lax.broadcasted_iota(jnp.int32, (owned, 128), 0)
    carry[...] = jnp.zeros((owned, 128), jnp.float32)

    @pl.loop(0, lines // 4)
    def _(n):
        mine = [own_v[pl.ds(4 * n + q, 1), :] for q in range(4)]
        hot = [cell_id == m for m in mine]
        amount = [jnp.where(hot[q], counts[pl.ds(4 * n + q, 1), :], 0.0) for q in range(4)]
        amount = jnp.concatenate(amount, axis=0).astype(jnp.bfloat16)
        summed = jnp.dot(amount, both, preferred_element_type=jnp.float32)
        for q in range(4):
            part = summed[owned * q : owned * (q + 1)]
            so_far = carry[...]
            at = jnp.sum(jnp.where(hot[q], part[:, 0:128] + so_far, 0.0), axis=0, keepdims=True)
            carry[...] = so_far + part[:, 128:256]
            spot = mine[q] * (depth * 128) + at.astype(jnp.int32)
            place_v[pl.ds(4 * n + q, 1), :] = (spot >> 7) << 3
            place_v[pl.ds(lines + 4 * n + q, 1), :] = spot & 127

    length = carry[...].astype(jnp.int32)
    cell_lane = lax.broadcasted_iota(jnp.int32, (owned, 128), 1)
    padded_id = ((cell_id >> 6) + 1) * (ny * nz) + (((cell_id >> 4) & 3) + 1) * nz + (cell_id & 15) + 1
    words = (
        cell_id * (depth * 8) + ((length >> 7) << 3),
        length & 127,
        jnp.minimum((length + 63) >> 6, QUICK),
        (padded_id << 16) + cell_id * (2 * depth),
        length,
        jnp.broadcast_to(jnp.max(length, axis=0, keepdims=True), (owned, 128)),
    )
    packed = words[0]
    for k, word in enumerate(words[1:]):
        packed = jnp.where((cell_lane & 15) == k + 1, word, packed)
    wide_v[...] = packed
    eight = lax.broadcasted_iota(jnp.int32, (owned // 8, 128), 1) >> 4
    folded = wide_v[pl.ds(0, owned // 8, stride=8), :]
    for u in range(1, 8):
        folded = jnp.where(eight == u, wide_v[pl.ds(u, owned // 8, stride=8), :], folded)
    lens_v[...] = folded
    copies = [
        pltpu.make_async_copy(place_v, place_s, sems.at[1]),
        pltpu.make_async_copy(lens_v, lens_s, sems.at[2]),
    ]
    for copy in copies:
        copy.start()
    for copy in copies:
        copy.wait()

    def append(sorted_rows, to, turn):
        to = pl.multiple_of(to, 8)
        turned = pltpu.roll(sorted_rows, turn, axis=1)
        pltpu.store(lists.at[pl.ds(to, 8), :], turned, mask=lane >= turn)
        lists[pl.ds(to + 8, 8), :] = turned

    @pl.loop(0, lines)
    def _(b):
        for u in range(128):
            values = cells[pl.ds(pl.multiple_of(where_s[lines + b, u], 8), 8), :]
            index = jnp.broadcast_to(mask[pl.ds(b * 128 + u, 1), :], (8, 128))
            shift = shifts[pl.ds(pl.multiple_of(where_s[3 * lines + b, u], 8), 8), :]
            append(lane_take(values, index) + shift, place_s[b, u], place_s[lines + b, u])

    dummy = jnp.where(sub < 3, 1000.0, 0.1)

    def close(b, total):
        for u in range(8):
            append(dummy, lens_s[b, 16 * u], lens_s[b, 16 * u + 1])
            first = lens_s[b, 16 * u + 3]
            for k in range(QUICK):
                items[total + k] = first + k
            total = total + lens_s[b, 16 * u + 2]
        return total

    number = lax.fori_loop(0, owned // 8, close, 0)

    def longer(c, total):
        line, at = c >> 3, (c & 7) * 16

        def add(k, total):
            items[total] = lens_s[line, at + 3] + k
            return total + 1

        return lax.fori_loop(QUICK, (lens_s[line, at + 4] + 63) >> 6, add, total)

    number = lax.fori_loop(0, jnp.where(lens_s[0, 5] > 64 * QUICK, owned, 0), longer, number)
    for k in range(3 * GROUP):
        items[number + k] = 0

    which_row = lax.broadcasted_iota(jnp.int32, (24, 1024), 0)
    which_col = lax.broadcasted_iota(jnp.int32, (24, 1024), 1)
    pick = ((which_row & 7) == (which_col >> 7)).astype(jnp.float32).astype(jnp.bfloat16)

    def spread(words, wide):
        splits = []
        for word in words:
            spot = word & 0xFFFF
            values = lists[pl.ds(pl.multiple_of((spot >> 1) * 8, 8), 8), :]
            values = pltpu.roll(values, (spot & 1) * 64, axis=1)
            high = values.astype(jnp.bfloat16).astype(jnp.float32)
            rest = values - high
            mid = rest.astype(jnp.bfloat16).astype(jnp.float32)
            split = jnp.concatenate([high, mid, rest - mid], axis=0)
            splits.append(split.T[0:64])
        split = jnp.concatenate(splits, axis=0).astype(jnp.bfloat16)
        spreads = jnp.dot(split, pick, preferred_element_type=jnp.float32)
        for u in range(8 * len(words)):
            for k in range(8):
                wide[8 * u + k] = spreads[8 * u : 8 * u + 8, 128 * k : 128 * k + 128]

    def press(word, wide, first):
        base = pl.multiple_of((word >> 16) * 8, 8)
        own = [jnp.broadcast_to(cells[pl.ds(base + k, 1), :], (8, 128)) for k in range(8)]
        total = [None] * 3
        for u in range(8):
            other = [wide[8 * (first + u) + k] for k in range(8)]
            apart = [other[k] - own[k] for k in range(3)]
            square = apart[0] * apart[0] + apart[1] * apart[1] + apart[2] * apart[2] + epsilon_sq
            inverse = lax.rsqrt(square)
            reach = own[6] + other[6]
            depth_in = jnp.where(own[7] != other[7], jnp.maximum(reach - square * inverse, 0.0), 0.0)
            closing = (
                (other[3] - own[3]) * apart[0] + (other[4] - own[4]) * apart[1] + (other[5] - own[5]) * apart[2]
            )
            along = closing * inverse - 50.0 * depth_in
            area = own[6] * other[6] * depth_in
            factor = area * lax.rsqrt(jnp.maximum(area * reach, 1e-20)) * along * inverse
            for k in range(3):
                term = factor * apart[k]
                total[k] = term if u == 0 else total[k] + term
        rows = pl.ds(base, 8)
        for k in range(3):
            pushes[k][rows, :] += total[k]

    def group(n):
        return [items[n * GROUP + k] for k in range(GROUP)]

    spread(group(0), wide_a)

    @pl.loop(0, (number + (2 * GROUP - 1)) // (2 * GROUP))
    def _(p):
        def half(n, now, later):
            spread(group(n + 1), later)
            for k, word in enumerate(group(n)):
                press(word, now, 8 * k)

        half(2 * p, wide_a, wide_b)
        half(2 * p + 1, wide_b, wide_a)

    ids = lax.broadcasted_iota(jnp.int32, (128, 128), 0)

    def operands(g, loads):
        rows = pl.ds(pl.multiple_of(g * 8, 8), 8)
        force = []
        first = (((g >> 3) + 1) * (ny * nz) + (((g >> 1) & 3) + 1) * nz + (g & 1) * 8 + 1) * 8
        for push in pushes:
            parts = [push[pl.ds(first + s, 8, stride=8), :] for s in range(8)]
            while len(parts) > 1:
                parts = [parts[i] + parts[i + 1] for i in range(0, len(parts), 2)]
            force.append(2.0 * parts[0])
        turn = cross_rows([arms[k, rows, :] for k in range(3)], force)
        zero = jnp.zeros((8, 128), jnp.float32)
        for k, value in enumerate(force + turn + [zero, zero]):
            loads[pl.ds(k, 8, stride=8), :] = value
        wide = jnp.concatenate([loads[pl.ds(8 * c, 8), :] for c in range(8)], axis=1)
        high = wide.astype(jnp.bfloat16).astype(jnp.float32)
        rest = wide - high
        mid = rest.astype(jnp.bfloat16).astype(jnp.float32)
        split = jnp.concatenate([high, mid, rest - mid], axis=0).astype(jnp.bfloat16)
        which = jnp.concatenate(
            [(ids == frag[pl.ds(g * 8 + c, 1), :]).astype(jnp.float32) for c in range(8)], axis=1
        ).astype(jnp.bfloat16)
        return split, which

    def gather(b, total):
        pairs = [operands(b * BURST + q, loads.at[pl.ds(64 * q, 64), :]) for q in range(BURST)]
        split, which = (jnp.concatenate(parts, axis=1) for parts in zip(*pairs))
        return total + lax.dot_general(split, which, (((1,), (1,)), ((), ())), preferred_element_type=jnp.float32)

    total = lax.fori_loop(0, owned // (8 * BURST), gather, jnp.zeros((24, 128), jnp.float32))
    out[...] = total[0:8] + total[8:16] + total[16:24]


def move_kernel(state, arms, frag, table, clump_next, out, clump_out):
    clump_out[...] = clump_next[...]
    rows_of = [jnp.broadcast_to(table[k : k + 1, :], (8, 128)) for k in range(6)]
    for g in range(frag.shape[0] // 8):
        rows = pl.ds(8 * g, 8)
        index = frag[rows, :]
        motion = [lane_take(r, index) for r in rows_of]
        velocity, spin = motion[0:3], motion[3:6]
        lever = [arms[k, rows, :] for k in range(3)]
        half = [0.5 * time_step * w for w in spin]
        turned = cross_rows(half, lever)
        twice = cross_rows(half, turned)
        scale = 2.0 / (1.0 + half[0] * half[0] + half[1] * half[1] + half[2] * half[2])
        moved = [lever[k] + scale * (turned[k] + twice[k]) for k in range(3)]
        swing = cross_rows(spin, moved)
        for k in range(3):
            out[k, rows, :] = state[k, rows, :] + time_step * velocity[k] + (moved[k] - lever[k])
            out[3 + k, rows, :] = velocity[k] + swing[k]


def halo(state, frag, owner, clump, cells):
    return pl.pallas_call(
        halo_kernel,
        in_specs=[VMEM] * 4,
        out_specs=(HBM, VMEM),
        out_shape=(
            jax.ShapeDtypeStruct(tuple(c + 2 for c in cells) + (8, 128), jnp.float32),
            jax.ShapeDtypeStruct((2, 128), jnp.int32),
        ),
        scratch_shapes=[
            pltpu.VMEM((8 * frag.shape[0], 128), jnp.float32),
            pltpu.SemaphoreType.DMA((26,)),
            pltpu.SemaphoreType.DMA((26,)),
            pltpu.SemaphoreType.DMA,
        ],
        compiler_params=pltpu.CompilerParams(collective_id=0, has_side_effects=True),
        name="halo",
    )(state, frag, owner, clump)


def exchange(info, sums, motion, mass, moment):
    block = lambda *shape: pltpu.VMEM(shape + (128,), jnp.float32)
    return pl.pallas_call(
        exchange_kernel,
        in_specs=[VMEM] * 5,
        out_specs=(VMEM, VMEM),
        out_shape=(
            jax.ShapeDtypeStruct((8, 128), jnp.float32),
            jax.ShapeDtypeStruct(motion.shape, jnp.float32),
        ),
        scratch_shapes=[
            block(8, 16),
            block(16, 8),
            block(4, 4, 8),
            block(4, 4, 8),
            block(16, 8),
            block(8, 16),
            pltpu.SemaphoreType.DMA((4, 15)),
            pltpu.SemaphoreType.DMA((4, 15)),
            pltpu.SemaphoreType.DMA((4,)),
        ],
        compiler_params=pltpu.CompilerParams(collective_id=1, has_side_effects=True),
        name="exchange",
    )(info, sums, motion, mass, moment)


def forces(codes, cells, arms, frag):
    lines = codes.shape[0] // 128
    owned, depth = frag.shape[0], 29
    return pl.pallas_call(
        tiles_kernel,
        in_specs=[VMEM, VMEM, VMEM, VMEM],
        out_specs=VMEM,
        out_shape=jax.ShapeDtypeStruct((8, 128), jnp.float32),
        scratch_shapes=[
            pltpu.VMEM((cells.shape[0] // 8, 128), jnp.int32),
            pltpu.VMEM((lines * 128, 128), jnp.int32),
            pltpu.VMEM((lines, 128), jnp.float32),
            pltpu.VMEM((4 * lines, 128), jnp.int32),
            pltpu.SMEM((4 * lines, 128), jnp.int32),
            pltpu.VMEM((2 * lines, 128), jnp.int32),
            pltpu.SMEM((2 * lines, 128), jnp.int32),
            pltpu.VMEM((lines, 128), jnp.int32),
            pltpu.VMEM((owned, 128), jnp.int32),
            pltpu.VMEM((owned // 8, 128), jnp.int32),
            pltpu.SMEM((owned // 8, 128), jnp.int32),
            pltpu.SMEM((owned * 54 + 96,), jnp.int32),
            pltpu.VMEM((owned, 128), jnp.float32),
            pltpu.VMEM((owned * depth * 8, 128), jnp.float32),
            pltpu.VMEM((27 * 8, 128), jnp.float32),
            pltpu.VMEM((64 * GROUP, 8, 128), jnp.float32),
            pltpu.VMEM((64 * GROUP, 8, 128), jnp.float32),
            pltpu.VMEM(cells.shape, jnp.float32),
            pltpu.VMEM(cells.shape, jnp.float32),
            pltpu.VMEM(cells.shape, jnp.float32),
            pltpu.VMEM((64 * BURST, 128), jnp.float32),
            pltpu.SemaphoreType.DMA((3,)),
        ],
        compiler_params=pltpu.CompilerParams(
            vmem_limit_bytes=60 * 1024 * 1024,
        ),
        name="forces",
    )(codes.reshape(lines, 128), cells, arms, frag)


def move(state, arms, frag, table, clump_next):
    n = frag.shape[0]
    part = n // 4
    return pl.pallas_call(
        move_kernel,
        grid=(4,),
        in_specs=[
            pl.BlockSpec((3, part, 128), lambda i: (0, i, 0)),
            pl.BlockSpec((3, part, 128), lambda i: (0, i, 0)),
            pl.BlockSpec((part, 128), lambda i: (i, 0)),
            pl.BlockSpec((8, 128), lambda i: (0, 0)),
            pl.BlockSpec(clump_next.shape, lambda i: (0, 0)),
        ],
        out_specs=(
            pl.BlockSpec((6, part, 128), lambda i: (0, i, 0)),
            pl.BlockSpec(clump_next.shape, lambda i: (0, 0)),
        ),
        out_shape=(
            jax.ShapeDtypeStruct((6, n, 128), jnp.float32),
            jax.ShapeDtypeStruct(clump_next.shape, jnp.float32),
        ),
        name="move",
    )(state, arms, frag, table, clump_next)


def local(state, arms, sphere_frag, frag_owner, frag_clump, tiles, clump_motion, inv_mass, inv_moment):
    cells = state.shape[1:4]
    slots = state.shape[4]
    count = cells[0] * cells[1] * cells[2]
    held = frag_clump.shape[0]
    frag = sphere_frag.reshape(count, slots)
    padded, info = halo(state.reshape(7, count, slots), frag, frag_owner.reshape(1, held), frag_clump[None], cells)
    sums = forces(tiles[0], padded.reshape(-1, slots), arms.reshape(3, count, slots), frag)
    table, clump_next = exchange(info, sums, clump_motion, inv_mass[None], inv_moment[None])
    sphere_next, clump_next = move(
        state.reshape(7, count, slots), arms.reshape(3, count, slots), frag, table, clump_next
    )
    return sphere_next.reshape((6,) + cells + (slots,)), clump_next


def solution(mesh):
    return jax.shard_map(
        local,
        mesh=mesh,
        in_specs=(
            P(None, "gx", "gy", "gz", None),
            P(None, "gx", "gy", "gz", None),
            P("gx", "gy", "gz", None),
            P(("gx", "gy", "gz"), None),
            P(("gx", "gy", "gz")),
            P(("gx", "gy", "gz"), None),
            P(None, ("gx", "gy", "gz")),
            P(("gx", "gy", "gz")),
            P(("gx", "gy", "gz")),
        ),
        out_specs=(P(None, "gx", "gy", "gz", None), P(None, ("gx", "gy", "gz"))),
        check_vma=False,
    )
```

```python
import functools

import jax
import jax.numpy as jnp
from jax import lax
from jax.experimental import pallas as pl
from jax.experimental.pallas import tpu as pltpu
from jax.sharding import PartitionSpec as P

CAP = 2
OWN = 48
QUICK = 8
GROUP = 16
BURST = 8
REACH = 0.14001
time_step = 0.01
gravity = 9.81
epsilon_sq = 1e-08
VMEM = pl.BlockSpec(memory_space=pltpu.VMEM)


def lane_take(rows, index):
    return jnp.take_along_axis(rows, index, axis=1, mode="promise_in_bounds")


def cross_rows(first, second):
    return [
        first[1] * second[2] - first[2] * second[1],
        first[2] * second[0] - first[0] * second[2],
        first[0] * second[1] - first[1] * second[0],
    ]


MESH = pl.DeviceIdType.MESH
HBM = pl.BlockSpec(memory_space=pl.ANY)


def place_of(shift):
    return tuple(
        lax.rem(lax.axis_index(axis) + step + lax.axis_size(axis), lax.axis_size(axis))
        for axis, step in zip(("gx", "gy", "gz"), shift)
    )


def meet(others):
    barrier = pltpu.get_barrier_semaphore()
    for other in others:
        pl.semaphore_signal(barrier, inc=1, device_id=other, device_id_type=MESH)
    return lambda: pl.semaphore_wait(barrier, len(others))


def halo_kernel(state, frag, owner, clump, out, info, own, send, recv, near):
    sizes = out.shape[0] - 2, out.shape[1] - 2, out.shape[2] - 2
    shifts = [(o // 9 - 1, o // 3 % 3 - 1, o % 3 - 1) for o in range(27) if o != 13]
    shifts.sort(key=lambda s: -sum(map(abs, s)))
    arrive = meet([place_of(s) for s in shifts])
    held = owner.shape[1]
    info[...] = jnp.full(info.shape, -1, jnp.int32)
    info[0:1, 0:held] = owner[...]
    info[1:2, 0:held] = clump[...]
    keys = info[0:1, :] * OWN + info[1:2, :]
    keys = jnp.broadcast_to(keys.astype(jnp.float32), (8, 128))
    for g in range(frag.shape[0] // 8):
        rows = pl.ds(8 * g, 8)
        for k in range(7):
            own[pl.ds(64 * g + k, 8, stride=8), :] = state[k, rows, :]
        own[pl.ds(64 * g + 7, 8, stride=8), :] = lane_take(keys, frag[rows, :])
    arrive()
    cells = own.reshape(sizes + (8, 128))
    copies = []
    for n, shift in enumerate(shifts):
        source = [pl.ds(0, size) if s == 0 else pl.ds(size - 1 if s > 0 else 0, 1) for s, size in zip(shift, sizes)]
        target = [pl.ds(1, size) if s == 0 else pl.ds(0 if s > 0 else size + 1, 1) for s, size in zip(shift, sizes)]
        copies.append(
            pltpu.make_async_remote_copy(
                src_ref=cells.at[tuple(source)],
                dst_ref=out.at[tuple(target)],
                send_sem=send.at[n],
                recv_sem=recv.at[n],
                device_id=place_of(shift),
                device_id_type=MESH,
            )
        )
        copies[-1].start()
    inner = pltpu.make_async_copy(cells, out.at[tuple(pl.ds(1, size) for size in sizes)], near)
    inner.start()
    for copy in copies:
        copy.wait()
    inner.wait()


def exchange_kernel(
    info, sums, motion, mass, moment, table, clump_next,
    outbox, got_z, inbox, reply, back, answer, send, recv, near,
):
    me = [lax.axis_index(axis) for axis in ("gx", "gy", "gz")]
    size = [lax.axis_size(axis) for axis in ("gx", "gy", "gz")]
    line = [(0, 0, d) for d in range(1, size[2])]
    plane = [(dx, dy, 0) for dx in range(size[0]) for dy in range(size[1]) if dx or dy]

    def beyond(step):
        return tuple(lax.rem(m + d, n) for m, d, n in zip(me, step, size))

    arrive = meet([beyond(step) for step in line + plane])

    def stage(number, steps, source, target):
        copies = [pltpu.make_async_copy(source(*me), target(*me), near.at[number])]
        copies[0].start()
        for n, step in enumerate(steps):
            other = beyond(step)
            copies.append(
                pltpu.make_async_remote_copy(
                    src_ref=source(*other),
                    dst_ref=target(*me),
                    send_sem=send.at[number, n],
                    recv_sem=recv.at[number, n],
                    device_id=other,
                    device_id_type=MESH,
                )
            )
            copies[-1].start()
        for copy in copies:
            copy.wait()

    exact = dict(precision=lax.Precision.HIGHEST, preferred_element_type=jnp.float32)
    owner = info[0:1, :]
    place = (owner & 7) * 16 + ((owner >> 3) & 3) * 4 + (owner >> 5)
    place = jnp.where(owner >= 0, place, -1)
    row = lax.broadcasted_iota(jnp.int32, (128, 128), 0)
    col = lax.broadcasted_iota(jnp.int32, (128, 128), 1)
    hit = (row == place).astype(jnp.float32)
    earlier = jnp.dot(
        hit.astype(jnp.bfloat16), (row < col).astype(jnp.float32).astype(jnp.bfloat16),
        preferred_element_type=jnp.float32,
    )
    slots = [jnp.where(earlier == float(e), hit, 0.0) for e in range(CAP)]
    across = (((1,), (1,)), ((), ()))
    filler = jnp.zeros((112, 128), jnp.float32)
    empty = jnp.zeros((8, 128), jnp.float32)
    sub = lax.broadcasted_iota(jnp.int32, (8, 128), 0)
    label = (info[1:2, :] + 1).astype(jnp.float32)
    payload = jnp.where(sub == 6, label, jnp.where(sub == 7, 0.0, sums[...]))
    outbox[...] = (
        lax.dot_general(slots[0], jnp.concatenate([payload, empty, filler], axis=0), across, **exact)
        + lax.dot_general(slots[1], jnp.concatenate([empty, payload, filler], axis=0), across, **exact)
    ).reshape(outbox.shape)
    arrive()
    stage(0, line, lambda x, y, z: outbox.at[z], lambda x, y, z: got_z.at[:, z])
    stage(1, plane, lambda x, y, z: got_z.at[y * 4 + x], lambda x, y, z: inbox.at[x, y])

    flat = inbox[...].reshape(128, 128)
    turned = flat.T
    names = lax.broadcasted_iota(jnp.int32, (128, motion.shape[1]), 1).astype(jnp.float32) + 1.0
    which = [(jnp.broadcast_to(flat[:, 8 * e + 6 : 8 * e + 7], names.shape) == names).astype(jnp.float32) for e in range(CAP)]
    total = jnp.dot(turned[0:8], which[0], **exact) + jnp.dot(turned[8:16], which[1], **exact)
    lower = lax.broadcasted_iota(jnp.int32, (3, motion.shape[1]), 0)
    pull = jnp.where(lower == 2, gravity, 0.0)
    velocity = motion[0:3, :] + time_step * (total[0:3] * mass[...] - pull)
    spin = motion[3:6, :] + time_step * total[3:6] * moment[...]
    clump_next[0:3, :] = velocity
    clump_next[3:6, :] = spin
    moved = jnp.concatenate([velocity, spin, jnp.zeros((2, motion.shape[1]), jnp.float32)], axis=0)
    blank = jnp.zeros((8, motion.shape[1]), jnp.float32)
    rest = jnp.zeros((112, motion.shape[1]), jnp.float32)
    reply[...] = (
        lax.dot_general(which[0], jnp.concatenate([moved, blank, rest], axis=0), across, **exact)
        + lax.dot_general(which[1], jnp.concatenate([blank, moved, rest], axis=0), across, **exact)
    ).reshape(reply.shape)
    stage(2, plane, lambda x, y, z: reply.at[x, y], lambda x, y, z: back.at[y * 4 + x])
    stage(3, line, lambda x, y, z: back.at[:, z], lambda x, y, z: answer.at[z])
    turned = answer[...].reshape(128, 128).T
    table[...] = jnp.dot(turned[0:8], slots[0], **exact) + jnp.dot(turned[8:16], slots[1], **exact)


def tiles_kernel(
    codes, cells, arms, frag, out, cand, mask, counts, where_v, where_s, place_v, place_s, own_v, wide_v, lens_v, lens_s, items,
    carry, lists, shifts, wide_a, wide_b, push_x, push_y, push_z, loads, sems,
):
    pushes = (push_x, push_y, push_z)
    lines = codes.shape[0]
    tiles = lines * 128
    pad = cells.shape[0] // 8
    ny, nz = 6, 18
    owned = 256
    depth = lists.shape[0] // (8 * owned)
    sub = lax.broadcasted_iota(jnp.int32, (8, 128), 0)
    lane = lax.broadcasted_iota(jnp.int32, (8, 128), 1)

    code = codes[...]
    own_of = (code * 38837) >> 20
    way = code - 27 * own_of
    step_x = ((way * 57) >> 9) - 1
    left = way - 9 * (step_x + 1)
    step_y = ((left * 11) >> 5) - 1
    step_z = left - 3 * (step_y + 1) - 1
    cell_of = ((own_of >> 6) + 1 + step_x) * (ny * nz) + (((own_of >> 4) & 3) + 1 + step_y) * nz
    cell_of = cell_of + (own_of & 15) + 1 + step_z
    for k, value in enumerate((cell_of, cell_of * 8, way, way * 8)):
        where_v[k * lines : (k + 1) * lines, :] = value
    own_v[...] = own_of
    first_copy = pltpu.make_async_copy(where_v, where_s, sems.at[0])
    first_copy.start()

    def reach_bits(g):
        base = pl.multiple_of(g * 64, 64)
        pos = [cells[pl.ds(base + k, 8, stride=8), :] for k in range(3)]
        reach = cells[pl.ds(base + 6, 8, stride=8), :] + REACH
        reach = reach * reach
        near = [p * p for p in pos]
        far = [(1.0 - p) * (1.0 - p) for p in pos]
        bits = jnp.full((8, 128), 1 << 13, jnp.int32)
        for o in range(27):
            steps = (o // 9 - 1, o // 3 % 3 - 1, o % 3 - 1)
            terms = [near[k] if s > 0 else far[k] for k, s in enumerate(steps) if s]
            if not terms:
                continue
            bits = bits | jnp.where(sum(terms[1:], terms[0]) <= reach, 1 << o, 0)
        cand[pl.ds(pl.multiple_of(g * 8, 8), 8), :] = bits

    @pl.loop(0, pad // 24)
    def _(g):
        for u in range(3):
            reach_bits(3 * g + u)

    @pl.loop(0, 27)
    def _(o):
        step_x = ((o * 57) >> 9) - 1
        left = o - 9 * (step_x + 1)
        step_y = ((left * 11) >> 5) - 1
        step_z = left - 3 * (step_y + 1) - 1
        value = jnp.where(sub == 0, step_x, jnp.where(sub == 1, step_y, jnp.where(sub == 2, step_z, 0)))
        shifts[pl.ds(pl.multiple_of(o * 8, 8), 8), :] = value.astype(jnp.float32)

    @pl.loop(0, owned // 16)
    def _(b):
        first = ((b >> 2) + 1) * (ny * nz) + ((b & 3) + 1) * nz + 1
        rows = pl.ds(pl.multiple_of(first * 8, 8), 128)
        for push in pushes:
            push[rows, :] = jnp.zeros((128, 128), jnp.float32)

    first_copy.wait()

    @pl.loop(0, lines)
    def _(b):
        for u in range(128):
            row = cand[pl.ds(where_s[b, u], 1), :]
            mask[pl.ds(b * 128 + u, 1), :] = (row >> where_s[2 * lines + b, u]) & 1

    row = lax.broadcasted_iota(jnp.int32, (128, 128), 0)
    col = lax.broadcasted_iota(jnp.int32, (128, 128), 1)
    before = (row < col).astype(jnp.bfloat16)
    ones = jnp.ones((8, 128), jnp.bfloat16)

    @pl.loop(0, lines // BURST)
    def _(b):
        rows = pl.ds(pl.multiple_of(b * (128 * BURST), 128 * BURST), 128 * BURST)
        col = lax.broadcasted_iota(jnp.int32, (128 * BURST, 128), 1)
        active = mask[rows, :]
        flags = active.astype(jnp.float32).astype(jnp.bfloat16)
        rank = jnp.dot(flags, before, preferred_element_type=jnp.float32).astype(jnp.int32)
        number = lax.dot_general(ones, flags, (((1,), (1,)), ((), ())), preferred_element_type=jnp.float32)
        for q in range(BURST):
            counts[pl.ds(b * BURST + q, 1), :] = number[0:1, 128 * q : 128 * q + 128]
        value = jnp.where(active > 0, ((col - rank) << 7) | col, 0)
        for bit in range(7):
            moved = pltpu.roll(value, 128 - (1 << bit), axis=1)
            flag = 1 << (7 + bit)
            value = jnp.where((moved & flag) != 0, moved, jnp.where((value & flag) != 0, 0, value))
        mask[rows, :] = value & 127

    both = jnp.concatenate([before, jnp.ones((128, 128), jnp.bfloat16)], axis=1)
    cell_id = lax.broadcasted_iota(jnp.int32, (owned, 128), 0)
    carry[...] = jnp.zeros((owned, 128), jnp.float32)

    @pl.loop(0, lines // 4)
    def _(n):
        mine = [own_v[pl.ds(4 * n + q, 1), :] for q in range(4)]
        hot = [cell_id == m for m in mine]
        amount = [jnp.where(hot[q], counts[pl.ds(4 * n + q, 1), :], 0.0) for q in range(4)]
        amount = jnp.concatenate(amount, axis=0).astype(jnp.bfloat16)
        summed = jnp.dot(amount, both, preferred_element_type=jnp.float32)
        for q in range(4):
            part = summed[owned * q : owned * (q + 1)]
            so_far = carry[...]
            at = jnp.sum(jnp.where(hot[q], part[:, 0:128] + so_far, 0.0), axis=0, keepdims=True)
            carry[...] = so_far + part[:, 128:256]
            spot = mine[q] * (depth * 128) + at.astype(jnp.int32)
            place_v[pl.ds(4 * n + q, 1), :] = (spot >> 7) << 3
            place_v[pl.ds(lines + 4 * n + q, 1), :] = spot & 127

    length = carry[...].astype(jnp.int32)
    cell_lane = lax.broadcasted_iota(jnp.int32, (owned, 128), 1)
    padded_id = ((cell_id >> 6) + 1) * (ny * nz) + (((cell_id >> 4) & 3) + 1) * nz + (cell_id & 15) + 1
    words = (
        cell_id * (depth * 8) + ((length >> 7) << 3),
        length & 127,
        jnp.minimum((length + 63) >> 6, QUICK),
        (padded_id << 16) + cell_id * (2 * depth),
        length,
        jnp.broadcast_to(jnp.max(length, axis=0, keepdims=True), (owned, 128)),
    )
    packed = words[0]
    for k, word in enumerate(words[1:]):
        packed = jnp.where((cell_lane & 15) == k + 1, word, packed)
    wide_v[...] = packed
    eight = lax.broadcasted_iota(jnp.int32, (owned // 8, 128), 1) >> 4
    folded = wide_v[pl.ds(0, owned // 8, stride=8), :]
    for u in range(1, 8):
        folded = jnp.where(eight == u, wide_v[pl.ds(u, owned // 8, stride=8), :], folded)
    lens_v[...] = folded
    copies = [
        pltpu.make_async_copy(place_v, place_s, sems.at[1]),
        pltpu.make_async_copy(lens_v, lens_s, sems.at[2]),
    ]
    for copy in copies:
        copy.start()
    for copy in copies:
        copy.wait()

    def append(sorted_rows, to, turn):
        to = pl.multiple_of(to, 8)
        turned = pltpu.roll(sorted_rows, turn, axis=1)
        pltpu.store(lists.at[pl.ds(to, 8), :], turned, mask=lane >= turn)
        lists[pl.ds(to + 8, 8), :] = turned

    @pl.loop(0, lines)
    def _(b):
        for u in range(128):
            values = cells[pl.ds(pl.multiple_of(where_s[lines + b, u], 8), 8), :]
            index = jnp.broadcast_to(mask[pl.ds(b * 128 + u, 1), :], (8, 128))
            shift = shifts[pl.ds(pl.multiple_of(where_s[3 * lines + b, u], 8), 8), :]
            append(lane_take(values, index) + shift, place_s[b, u], place_s[lines + b, u])

    dummy = jnp.where(sub < 3, 1000.0, 0.1)

    def close(b, total):
        for u in range(8):
            append(dummy, lens_s[b, 16 * u], lens_s[b, 16 * u + 1])
            first = lens_s[b, 16 * u + 3]
            for k in range(QUICK):
                items[total + k] = first + k
            total = total + lens_s[b, 16 * u + 2]
        return total

    number = lax.fori_loop(0, owned // 8, close, 0)

    def longer(c, total):
        line, at = c >> 3, (c & 7) * 16

        def add(k, total):
            items[total] = lens_s[line, at + 3] + k
            return total + 1

        return lax.fori_loop(QUICK, (lens_s[line, at + 4] + 63) >> 6, add, total)

    number = lax.fori_loop(0, jnp.where(lens_s[0, 5] > 64 * QUICK, owned, 0), longer, number)
    for k in range(3 * GROUP):
        items[number + k] = 0

    which_row = lax.broadcasted_iota(jnp.int32, (24, 1024), 0)
    which_col = lax.broadcasted_iota(jnp.int32, (24, 1024), 1)
    pick = ((which_row & 7) == (which_col >> 7)).astype(jnp.float32).astype(jnp.bfloat16)

    def spread(words, wide):
        splits = []
        for word in words:
            spot = word & 0xFFFF
            values = lists[pl.ds(pl.multiple_of((spot >> 1) * 8, 8), 8), :]
            values = pltpu.roll(values, (spot & 1) * 64, axis=1)
            high = values.astype(jnp.bfloat16).astype(jnp.float32)
            rest = values - high
            mid = rest.astype(jnp.bfloat16).astype(jnp.float32)
            split = jnp.concatenate([high, mid, rest - mid], axis=0)
            splits.append(split.T[0:64])
        split = jnp.concatenate(splits, axis=0).astype(jnp.bfloat16)
        spreads = jnp.dot(split, pick, preferred_element_type=jnp.float32)
        for u in range(8 * len(words)):
            for k in range(8):
                wide[8 * u + k] = spreads[8 * u : 8 * u + 8, 128 * k : 128 * k + 128]

    def press(word, wide, first):
        base = pl.multiple_of((word >> 16) * 8, 8)
        own = [jnp.broadcast_to(cells[pl.ds(base + k, 1), :], (8, 128)) for k in range(8)]
        total = [None] * 3
        for u in range(8):
            other = [wide[8 * (first + u) + k] for k in range(8)]
            apart = [other[k] - own[k] for k in range(3)]
            square = apart[0] * apart[0] + apart[1] * apart[1] + apart[2] * apart[2] + epsilon_sq
            inverse = lax.rsqrt(square)
            reach = own[6] + other[6]
            depth_in = jnp.where(own[7] != other[7], jnp.maximum(reach - square * inverse, 0.0), 0.0)
            closing = (
                (other[3] - own[3]) * apart[0] + (other[4] - own[4]) * apart[1] + (other[5] - own[5]) * apart[2]
            )
            along = closing * inverse - 50.0 * depth_in
            area = own[6] * other[6] * depth_in
            factor = area * lax.rsqrt(jnp.maximum(area * reach, 1e-20)) * along * inverse
            for k in range(3):
                term = factor * apart[k]
                total[k] = term if u == 0 else total[k] + term
        rows = pl.ds(base, 8)
        for k in range(3):
            pushes[k][rows, :] += total[k]

    def group(n):
        return [items[n * GROUP + k] for k in range(GROUP)]

    spread(group(0), wide_a)

    @pl.loop(0, (number + (2 * GROUP - 1)) // (2 * GROUP))
    def _(p):
        def half(n, now, later):
            spread(group(n + 1), later)
            for k, word in enumerate(group(n)):
                press(word, now, 8 * k)

        half(2 * p, wide_a, wide_b)
        half(2 * p + 1, wide_b, wide_a)

    ids = lax.broadcasted_iota(jnp.int32, (128, 128), 0)

    def operands(g, loads):
        rows = pl.ds(pl.multiple_of(g * 8, 8), 8)
        force = []
        first = (((g >> 3) + 1) * (ny * nz) + (((g >> 1) & 3) + 1) * nz + (g & 1) * 8 + 1) * 8
        for push in pushes:
            parts = [push[pl.ds(first + s, 8, stride=8), :] for s in range(8)]
            while len(parts) > 1:
                parts = [parts[i] + parts[i + 1] for i in range(0, len(parts), 2)]
            force.append(2.0 * parts[0])
        turn = cross_rows([arms[k, rows, :] for k in range(3)], force)
        zero = jnp.zeros((8, 128), jnp.float32)
        for k, value in enumerate(force + turn + [zero, zero]):
            loads[pl.ds(k, 8, stride=8), :] = value
        wide = jnp.concatenate([loads[pl.ds(8 * c, 8), :] for c in range(8)], axis=1)
        high = wide.astype(jnp.bfloat16).astype(jnp.float32)
        rest = wide - high
        mid = rest.astype(jnp.bfloat16).astype(jnp.float32)
        split = jnp.concatenate([high, mid, rest - mid], axis=0).astype(jnp.bfloat16)
        which = jnp.concatenate(
            [(ids == frag[pl.ds(g * 8 + c, 1), :]).astype(jnp.float32) for c in range(8)], axis=1
        ).astype(jnp.bfloat16)
        return split, which

    def gather(b, total):
        pairs = [operands(b * BURST + q, loads.at[pl.ds(64 * q, 64), :]) for q in range(BURST)]
        split, which = (jnp.concatenate(parts, axis=1) for parts in zip(*pairs))
        return total + lax.dot_general(split, which, (((1,), (1,)), ((), ())), preferred_element_type=jnp.float32)

    total = lax.fori_loop(0, owned // (8 * BURST), gather, jnp.zeros((24, 128), jnp.float32))
    out[...] = total[0:8] + total[8:16] + total[16:24]


def move_kernel(state, arms, frag, table, clump_next, out, clump_out):
    clump_out[...] = clump_next[...]
    rows_of = [jnp.broadcast_to(table[k : k + 1, :], (8, 128)) for k in range(6)]
    for g in range(frag.shape[0] // 8):
        rows = pl.ds(8 * g, 8)
        index = frag[rows, :]
        motion = [lane_take(r, index) for r in rows_of]
        velocity, spin = motion[0:3], motion[3:6]
        lever = [arms[k, rows, :] for k in range(3)]
        half = [0.5 * time_step * w for w in spin]
        turned = cross_rows(half, lever)
        twice = cross_rows(half, turned)
        scale = 2.0 / (1.0 + half[0] * half[0] + half[1] * half[1] + half[2] * half[2])
        moved = [lever[k] + scale * (turned[k] + twice[k]) for k in range(3)]
        swing = cross_rows(spin, moved)
        for k in range(3):
            out[k, rows, :] = state[k, rows, :] + time_step * velocity[k] + (moved[k] - lever[k])
            out[3 + k, rows, :] = velocity[k] + swing[k]


def halo(state, frag, owner, clump, cells):
    return pl.pallas_call(
        halo_kernel,
        in_specs=[VMEM] * 4,
        out_specs=(HBM, VMEM),
        out_shape=(
            jax.ShapeDtypeStruct(tuple(c + 2 for c in cells) + (8, 128), jnp.float32),
            jax.ShapeDtypeStruct((2, 128), jnp.int32),
        ),
        scratch_shapes=[
            pltpu.VMEM((8 * frag.shape[0], 128), jnp.float32),
            pltpu.SemaphoreType.DMA((26,)),
            pltpu.SemaphoreType.DMA((26,)),
            pltpu.SemaphoreType.DMA,
        ],
        compiler_params=pltpu.CompilerParams(collective_id=0, has_side_effects=True),
        name="halo",
    )(state, frag, owner, clump)


def exchange(info, sums, motion, mass, moment):
    block = lambda *shape: pltpu.VMEM(shape + (128,), jnp.float32)
    return pl.pallas_call(
        exchange_kernel,
        in_specs=[VMEM] * 5,
        out_specs=(VMEM, VMEM),
        out_shape=(
            jax.ShapeDtypeStruct((8, 128), jnp.float32),
            jax.ShapeDtypeStruct(motion.shape, jnp.float32),
        ),
        scratch_shapes=[
            block(8, 16),
            block(16, 8),
            block(4, 4, 8),
            block(4, 4, 8),
            block(16, 8),
            block(8, 16),
            pltpu.SemaphoreType.DMA((4, 15)),
            pltpu.SemaphoreType.DMA((4, 15)),
            pltpu.SemaphoreType.DMA((4,)),
        ],
        compiler_params=pltpu.CompilerParams(collective_id=1, has_side_effects=True),
        name="exchange",
    )(info, sums, motion, mass, moment)


def forces(codes, cells, arms, frag):
    lines = codes.shape[0] // 128
    owned, depth = frag.shape[0], 29
    return pl.pallas_call(
        tiles_kernel,
        in_specs=[VMEM, VMEM, VMEM, VMEM],
        out_specs=VMEM,
        out_shape=jax.ShapeDtypeStruct((8, 128), jnp.float32),
        scratch_shapes=[
            pltpu.VMEM((cells.shape[0] // 8, 128), jnp.int32),
            pltpu.VMEM((lines * 128, 128), jnp.int32),
            pltpu.VMEM((lines, 128), jnp.float32),
            pltpu.VMEM((4 * lines, 128), jnp.int32),
            pltpu.SMEM((4 * lines, 128), jnp.int32),
            pltpu.VMEM((2 * lines, 128), jnp.int32),
            pltpu.SMEM((2 * lines, 128), jnp.int32),
            pltpu.VMEM((lines, 128), jnp.int32),
            pltpu.VMEM((owned, 128), jnp.int32),
            pltpu.VMEM((owned // 8, 128), jnp.int32),
            pltpu.SMEM((owned // 8, 128), jnp.int32),
            pltpu.SMEM((owned * 54 + 96,), jnp.int32),
            pltpu.VMEM((owned, 128), jnp.float32),
            pltpu.VMEM((owned * depth * 8, 128), jnp.float32),
            pltpu.VMEM((27 * 8, 128), jnp.float32),
            pltpu.VMEM((64 * GROUP, 8, 128), jnp.float32),
            pltpu.VMEM((64 * GROUP, 8, 128), jnp.float32),
            pltpu.VMEM(cells.shape, jnp.float32),
            pltpu.VMEM(cells.shape, jnp.float32),
            pltpu.VMEM(cells.shape, jnp.float32),
            pltpu.VMEM((64 * BURST, 128), jnp.float32),
            pltpu.SemaphoreType.DMA((3,)),
        ],
        compiler_params=pltpu.CompilerParams(
            vmem_limit_bytes=60 * 1024 * 1024,
        ),
        name="forces",
    )(codes.reshape(lines, 128), cells, arms, frag)


def move(state, arms, frag, table, clump_next):
    n = frag.shape[0]
    part = n // 4
    return pl.pallas_call(
        move_kernel,
        grid=(4,),
        in_specs=[
            pl.BlockSpec((3, part, 128), lambda i: (0, i, 0)),
            pl.BlockSpec((3, part, 128), lambda i: (0, i, 0)),
            pl.BlockSpec((part, 128), lambda i: (i, 0)),
            pl.BlockSpec((8, 128), lambda i: (0, 0)),
            pl.BlockSpec(clump_next.shape, lambda i: (0, 0)),
        ],
        out_specs=(
            pl.BlockSpec((6, part, 128), lambda i: (0, i, 0)),
            pl.BlockSpec(clump_next.shape, lambda i: (0, 0)),
        ),
        out_shape=(
            jax.ShapeDtypeStruct((6, n, 128), jnp.float32),
            jax.ShapeDtypeStruct(clump_next.shape, jnp.float32),
        ),
        name="move",
    )(state, arms, frag, table, clump_next)


def local(state, arms, sphere_frag, frag_owner, frag_clump, tiles, clump_motion, inv_mass, inv_moment):
    cells = state.shape[1:4]
    slots = state.shape[4]
    count = cells[0] * cells[1] * cells[2]
    held = frag_clump.shape[0]
    frag = sphere_frag.reshape(count, slots)
    padded, info = halo(state.reshape(7, count, slots), frag, frag_owner.reshape(1, held), frag_clump[None], cells)
    sums = forces(tiles[0], padded.reshape(-1, slots), arms.reshape(3, count, slots), frag)
    table, clump_next = exchange(info, sums, clump_motion, inv_mass[None], inv_moment[None])
    sphere_next, clump_next = move(
        state.reshape(7, count, slots), arms.reshape(3, count, slots), frag, table, clump_next
    )
    return sphere_next.reshape((6,) + cells + (slots,)), clump_next


def solution(mesh):
    return jax.shard_map(
        local,
        mesh=mesh,
        in_specs=(
            P(None, "gx", "gy", "gz", None),
            P(None, "gx", "gy", "gz", None),
            P("gx", "gy", "gz", None),
            P(("gx", "gy", "gz"), None),
            P(("gx", "gy", "gz")),
            P(("gx", "gy", "gz"), None),
            P(None, ("gx", "gy", "gz")),
            P(("gx", "gy", "gz")),
            P(("gx", "gy", "gz")),
        ),
        out_specs=(P(None, "gx", "gy", "gz", None), P(None, ("gx", "gy", "gz"))),
        check_vma=False,
    )
```
